32 devices in a mesh: vocab: 8 (over z, x), width: 4 (over y, core).
Axes of the slice: x: 2, y: 2, z: 4, core: 2. Of those that a mesh axis runs over, the one named last changes fastest.
Arguments:
- hidden: bfloat16 [384, 2048], P('vocab', 'width'), may hold values from -2000 to 2000, as said below
- norm_gain: bfloat16 [2048], replicated, may hold values from 0.25 to 1.75
- head_weight: bfloat16 [2048, 163840], P('width', 'vocab'), may hold values from -8 to 8, as said below
- lengths: int32 [16], replicated, may hold values from 1 to 96, 384 in all
- deal: int32 [384], P('width'), may hold values from 0 to 383, each once
- targets: int32 [384], P('width'), may hold values from 0 to 163839
Outputs:
- token_logprob: float32 [384], P('vocab')
- request_stats: float32 [4, 16], replicated
The draws below stay inside these ranges and needn't reach their ends.
Inputs may be any that keep to these rules, and one draw needn't show every extreme that they name: The 16 lengths sum to 384. `deal`: each position occurs once. `hidden`: real values. `head_weight`: real values.
All inputs are finite; a program needn't handle non-finite values.
Results may differ from the reference program's by a relative error of at most 0.00055.
Values may be sent and summed in bfloat16 or wider, within the bound.
A program may use at most 128 MiB of HBM per device.

```python
import math
import jax
import jax.numpy as jnp
import numpy as np
from jax import lax

D = 2048
VOCAB = 163840
REQS = 16
TOKENS = 384


def draw_head_weight(key, part):
    scale = 3.0 / math.sqrt(D)
    base = jnp.clip(jax.random.normal(jax.random.fold_in(key, 1), (D, VOCAB), jnp.float32), -6.0, 6.0) * scale
    return base.astype(jnp.bfloat16)


def draw_hidden(key, part):
    spread = jax.random.uniform(jax.random.fold_in(key, 3), (D,), jnp.float32)
    position = jnp.arange(D, dtype=jnp.float32) / D
    col_scale = jnp.exp(math.log(10.0) * (0.5 * position + 0.5 * spread))
    rising = jax.random.uniform(jax.random.fold_in(key, 4), (TOKENS, 1), jnp.float32)
    row_scale = jnp.exp(math.log(10.0) * rising)
    noise = jnp.clip(jax.random.normal(jax.random.fold_in(key, 5), (TOKENS, D), jnp.float32), -5.0, 5.0)
    base = noise * col_scale[None, :] * row_scale
    return base.astype(jnp.bfloat16)


def set_ends(result, rng, low, high):
    shape = result.shape
    spot = [jax.random.randint(jax.random.fold_in(rng, axis), (), 0, shape[axis]) for axis in range(len(shape))]
    result = result.at[tuple(spot)].set(low)
    longest = shape.index(max(shape))
    spot[longest] = (spot[longest] + 1) % shape[longest]
    return result.at[tuple(spot)].set(high)


def ranked_wide(rng, extent, count, skew):
    loads = [min(1 << octave, count + 1 - (1 << octave)) * (1 << 20) // math.isqrt((1 << octave) ** skew) + 1 for octave in range((count + 1).bit_length()) if 1 << octave <= count]
    scale = 1 + sum(loads) // (1 << 30)
    listing = np.cumsum(np.array([max(1, weight // scale) for weight in loads]))
    lot = jax.random.randint(jax.random.fold_in(rng, 1), extent, 0, int(listing[len(loads) - 1]))
    start = jnp.left_shift(1, jnp.searchsorted(jnp.asarray(listing, jnp.int32), lot, side="right").astype(jnp.int32))
    rank = start - 1 + jax.random.randint(jax.random.fold_in(rng, 4), extent, 0, 1 << 30) % jnp.minimum(start, count + 1 - start)
    return jax.random.permutation(jax.random.fold_in(rng, 2), count)[rank].astype(jnp.int32)


def split_up(number_of, total, reach, slope):
    loads = [(1 << 20) // math.isqrt(standing ** slope) + 1 for standing in range(2, number_of + 1)]
    surplus, given = total - reach - (number_of - 1), [1] * (number_of - 1)
    while surplus > 0:
        free = [i for i in range(number_of - 1) if given[i] < reach]
        pool, left = sum([loads[i] for i in free]), surplus
        for i in free:
            addition = min(reach - given[i], max(1, left * loads[i] // pool), surplus)
            given[i] = given[i] + addition
            surplus = surplus - addition
    return np.array([reach] + given)


def uneven(rng, count, total, most, slope):
    if count == 2:
        one = jax.random.randint(rng, (), max(1, total - most), min(most, total - 1) + 1)
        return jnp.stack([one, total - one])
    sizes = jnp.asarray(split_up(count, total, most, slope), jnp.int32)
    twos = (count - 1) // 2
    donor, receiver = sizes[1:1 + 2 * twos:2], sizes[2:2 + 2 * twos:2]
    margin = jnp.minimum(donor - 1, most - receiver)
    moved = jax.random.randint(jax.random.fold_in(rng, 1), (twos,), 0, 1 << 20) % (margin + 1)
    sizes = sizes.at[1:1 + 2 * twos:2].set(donor - moved).at[2:2 + 2 * twos:2].set(receiver + moved)
    return sizes[jax.random.permutation(jax.random.fold_in(rng, 2), count)]


def setup_inputs(seed: int = 0) -> dict:
    streams_of = jax.random.split(jax.random.key(seed), 7)
    return {
        "hidden": draw_hidden(jax.random.fold_in(streams_of[6], 71), 0),
        "norm_gain": jnp.clip(1.0 + 0.15 * jax.random.normal(streams_of[1], (D,), jnp.float32), 0.25, 1.75).astype(jnp.bfloat16),
        "head_weight": draw_head_weight(jax.random.fold_in(streams_of[6], 71), 0),
        "lengths": uneven(streams_of[3], REQS, TOKENS, TOKENS // 4, 2).astype(jnp.int32),
        "deal": jax.random.permutation(streams_of[4], TOKENS).astype(jnp.int32),
        "targets": set_ends(ranked_wide(streams_of[5], (TOKENS,), VOCAB, 2), jax.random.fold_in(streams_of[5], 3), 0, VOCAB - 1).astype(jnp.int32),
    }


epsilon = 1e-06

def reference(hidden, norm_gain, head_weight, lengths, deal, targets):
    tokens = hidden.shape[0]
    widened = hidden.astype(jnp.float32)
    mean_sq = lax.optimization_barrier(jnp.mean(widened * widened, axis=1))
    normed = (widened * lax.rsqrt(mean_sq + epsilon)[:, None] * norm_gain[None, :]).astype(jnp.bfloat16)
    block = math.gcd(tokens, 512)
    columns = lax.iota(jnp.int32, head_weight.shape[1])

    def block_stats(first):
        rows = lax.dynamic_slice_in_dim(normed, first, block, 0)
        wanted = lax.dynamic_slice_in_dim(targets, first, block, 0)
        logits = jnp.dot(rows, head_weight, preferred_element_type=jnp.float32)
        largest = lax.optimization_barrier(jnp.max(logits, axis=1))
        powers = jnp.exp(logits - largest[:, None])
        picked = lax.optimization_barrier(jnp.sum(jnp.where(columns[None, :] == wanted[:, None], logits, 0.0), axis=1))
        return (largest, lax.optimization_barrier(jnp.sum(powers, axis=1)), lax.optimization_barrier(jnp.sum(powers * logits, axis=1)), picked)
    firsts = (lax.iota(jnp.int32, tokens // block) * block).astype(jnp.int32)
    results = lax.map(block_stats, firsts)
    largest, total, weighted, picked = [pieces.reshape(tokens) for pieces in results]
    log_total = jnp.log(total)
    logprob_dealt = picked - largest - log_total
    entropy = largest + log_total - weighted / total
    rms = jnp.sqrt(mean_sq + epsilon)
    token_logprob = jnp.zeros((tokens,), jnp.float32).at[deal].set(logprob_dealt)
    ends = jnp.cumsum(lengths).astype(jnp.int32)
    starts = (ends - lengths).astype(jnp.int32)
    positions = lax.iota(jnp.int32, tokens)
    member = (positions[None, :] >= starts[:, None]) & (positions[None, :] < ends[:, None])
    packed = jnp.zeros((3, tokens), jnp.float32).at[:, deal].set(jnp.stack([logprob_dealt, entropy, rms]))
    peaks = jnp.zeros((tokens,), jnp.float32).at[deal].set(largest)
    sums = lax.optimization_barrier(jnp.sum(jnp.where(member[None], packed[:, None, :], 0.0), axis=2))
    highest = lax.optimization_barrier(jnp.max(jnp.where(member, peaks[None, :], -1e+30), axis=1))
    counts = lengths.astype(jnp.float32)
    request_stats = jnp.concatenate([sums / counts[None, :], highest[None, :]], axis=0)
    return (token_logprob, request_stats)
```

```python
import functools

import jax
import jax.numpy as jnp
from jax import lax
from jax.experimental import pallas as pl
from jax.experimental.pallas import tpu as pltpu
from jax.sharding import PartitionSpec as P

D = 2048
epsilon = 1e-06
LOW = -1e30
TINY = 1e-30
STEPS = 32767.0
DEPTH = 3
LANES = 128
WIDTH = 4


def kernel(
    cfg,
    aim_ref,
    deal_ref,
    lens_ref,
    gain_ref,
    hid_ref,
    w_ref,
    tok_ref,
    stat_ref,
    gains,
    ints_all,
    ints_cols,
    mate_hid,
    split_rows,
    chip_scale,
    ratio,
    sq_all,
    msq_all,
    nrm,
    wbuf,
    sbuf,
    rbuf,
    xbuf,
    ybuf,
    zsend,
    zrecv,
    m_acc,
    t_acc,
    g_acc,
    p_acc,
    st1,
    st2,
    once_send,
    x_recv,
    i_recv,
    q_recv,
    h_recv,
    f_recv,
    r_recv,
    wl_sem,
    w_recv,
    y_recv,
    z_recv,
    ya_recv,
    a_recv,
    b_recv,
):
    V, rows, tokens, feats, slab, quarter, cn, n, mb, mb_late, reqs = cfg
    v = lax.axis_index("vocab")
    w = lax.axis_index("width")
    lo = lax.rem(w, 2)
    hi = w // 2
    mate = w + 1 - 2 * lo
    far = w + 2 - 4 * hi
    bw = tokens // WIDTH
    x_send, i_send, q_send, h_send, f_send, r_send = [once_send.at[k] for k in range(6)]
    w_send, y_send, z_send, ya_send, a_send, b_send = [once_send.at[k] for k in range(6, 12)]

    def rcopy(src, dst, ss, rs, where):
        return pltpu.make_async_remote_copy(
            src_ref=src,
            dst_ref=dst,
            send_sem=ss,
            recv_sem=rs,
            device_id=where,
            device_id_type=pl.DeviceIdType.MESH,
        )

    def vpeer(d):
        return lax.rem(v + d, V)

    def vsource(d):
        return lax.rem(v + V - d, V)

    def wpeer(d):
        return lax.rem(w + d, WIDTH)

    def wsource(d):
        return lax.rem(w + WIDTH - d, WIDTH)

    def wcols(k, is_keep, dev):
        dev_far = dev + 2 - 4 * (dev // 2)
        q = dev if is_keep else dev_far
        base = k - n if is_keep else k
        return pl.ds(pl.multiple_of(q * quarter + base * cn, LANES), cn)

    own_half = pl.ds(pl.multiple_of(lo * feats, LANES), feats)
    mate_half = pl.ds(pl.multiple_of((1 - lo) * feats, LANES), feats)

    def wlocal(k, is_keep):
        return pltpu.make_async_copy(
            w_ref.at[:, wcols(k, is_keep, w)], wbuf.at[k, own_half, :], wl_sem.at[k]
        )

    def wremote(k, is_keep):
        return rcopy(
            w_ref.at[:, wcols(k, is_keep, mate)],
            wbuf.at[k, own_half, :],
            w_send,
            w_recv.at[k],
            (v, mate),
        )

    def wwait(k, is_keep):
        wlocal(k, is_keep).wait()
        rcopy(
            w_ref.at[:, wcols(k, is_keep, mate)],
            wbuf.at[k, mate_half, :],
            w_send,
            w_recv.at[k],
            (v, mate),
        ).wait_recv()

    barrier = pltpu.get_barrier_semaphore()

    @pl.loop(1, WIDTH)
    def _(d):
        pl.semaphore_signal(
            barrier, inc=1, device_id=(v, wpeer(d)), device_id_type=pl.DeviceIdType.MESH
        )

    @pl.loop(1, V)
    def _(d):
        pl.semaphore_signal(
            barrier, inc=1, device_id=(vpeer(d), w), device_id_type=pl.DeviceIdType.MESH
        )

    @pl.loop(0, n)
    def _(k):
        wlocal(k, False).start()

    def squares(x):
        return jnp.sum(x * x, axis=1, keepdims=True)

    def to_row(column, wide):
        height = column.shape[0]
        there = lax.broadcasted_iota(jnp.int32, (height, wide), 1)
        here = lax.broadcasted_iota(jnp.int32, (height, wide), 0)
        return jnp.sum(jnp.where(there == here, column, 0.0), axis=0, keepdims=True)

    def to_column(row, height):
        wide = row.shape[1]
        there = lax.broadcasted_iota(jnp.int32, (height, wide), 1)
        here = lax.broadcasted_iota(jnp.int32, (height, wide), 0)
        return jnp.sum(jnp.where(there == here, row, 0.0), axis=1, keepdims=True)

    x = hid_ref[...].astype(jnp.float32)
    sq = squares(x)
    sq_all[w] = to_row(sq, LANES)
    gains[...] = gain_ref[...].astype(jnp.float32)
    ints_all[w] = jnp.zeros(ints_all.shape[1:], jnp.int32)
    ints_all[w, 0:1, 0:bw] = aim_ref[...]
    ints_all[w, 1:2, 0:bw] = deal_ref[...]
    pl.semaphore_wait(barrier, WIDTH - 1 + V - 1)

    def xcopy():
        return rcopy(hid_ref, mate_hid, x_send, x_recv, (v, mate))

    def icopy(d, dev):
        return rcopy(ints_all.at[w], ints_all.at[dev], i_send, i_recv.at[d], (v, wpeer(d)))

    across = far + 1 - 2 * lo

    def qstart(there):
        rcopy(sq_all.at[w], sq_all.at[w], q_send, q_recv.at[lo], (v, there)).start()

    def qwait(there):
        rcopy(
            sq_all.at[w], sq_all.at[there], q_send, q_recv.at[lax.rem(there, 2)], (v, there)
        ).wait_recv()

    xcopy().start()
    qstart(far)
    qstart(across)

    @pl.loop(0, n)
    def _(k):
        wremote(k, False).start()

    @pl.loop(1, WIDTH)
    def _(d):
        icopy(d, w).start()

    groups = feats // LANES
    xcopy().wait_recv()
    y = mate_hid[...].astype(jnp.float32)
    sq_mate = squares(y)
    sq_all[mate] = to_row(sq_mate, LANES)
    chip_sq = sq + sq_mate
    chip_scale[...] = jnp.broadcast_to(
        lax.rsqrt(chip_sq * (1.0 / (2 * feats)) + epsilon), (rows, LANES)
    )
    for half, dev, value in ((lo, w, x), (1 - lo, mate, y)):
        for g in range(groups):
            column = pl.ds(pl.multiple_of(half * feats + g * LANES, LANES), LANES)
            scaled = value[:, g * LANES : (g + 1) * LANES] * gains[pl.ds(dev * groups + g, 1), :]
            upper = scaled.astype(jnp.bfloat16)
            split_rows[0:rows, column] = upper
            split_rows[rows : 2 * rows, column] = (scaled - upper.astype(jnp.float32)).astype(
                jnp.bfloat16
            )

    def vspan(dev):
        return pl.ds(pl.multiple_of(dev * rows, 16), rows)

    def normalize():
        qwait(far)
        qwait(across)
        total_sq = sq_all[0] + sq_all[1] + sq_all[2] + sq_all[3]
        mean_row = total_sq * (1.0 / D)
        msq_all[v] = mean_row
        mean_sq = to_column(mean_row, rows)
        scale = lax.rsqrt(mean_sq + epsilon)
        far_sq = to_column(sq_all[far] + sq_all[across], rows)
        far_scale = lax.rsqrt(far_sq * (1.0 / (2 * feats)) + epsilon)
        ratio[0:rows, :] = jnp.broadcast_to(scale / far_scale, (rows, LANES))
        for half, dev, source in ((lo, w, hid_ref), (1 - lo, mate, mate_hid)):
            for g in range(groups):
                column = pl.ds(pl.multiple_of(half * feats + g * LANES, LANES), LANES)
                value = source[:, g * LANES : (g + 1) * LANES].astype(jnp.float32)
                nrm[0:rows, column] = (
                    value * scale * gains[pl.ds(dev * groups + g, 1), :]
                ).astype(jnp.bfloat16)

    def slot(d):
        return pl.ds(pl.multiple_of(d * rows, 16), rows)

    def hcopy(d):
        return rcopy(
            nrm.at[slot(0), own_half],
            nrm.at[slot(d), own_half],
            h_send,
            h_recv.at[d],
            (vpeer(d), w),
        )

    def fcopy(d, half):
        part = nrm.at[slot(d), half]
        return rcopy(part, part, f_send, f_recv.at[d], (v, mate))

    def rmscopy(d, dev):
        return rcopy(msq_all.at[v], msq_all.at[dev], r_send, r_recv.at[d], (vpeer(d), w))

    ratio[pl.ds(rows, tokens - rows), :] = jnp.ones((tokens - rows, LANES), jnp.float32)
    m_acc[...] = jnp.full((tokens, LANES), LOW, jnp.float32)
    t_acc[...] = jnp.zeros((tokens, LANES), jnp.float32)
    g_acc[...] = jnp.zeros((tokens, LANES), jnp.float32)
    p_acc[...] = jnp.zeros((tokens, LANES), jnp.float32)

    late = tokens - rows

    def ycopy(i):
        part = pl.ds(rows, late)
        return rcopy(
            sbuf.at[i, part, :], rbuf.at[i, part, :], y_send, y_recv.at[i], (v, far)
        )

    def yacopy(i):
        part = pl.ds(0, rows)
        return rcopy(
            sbuf.at[i, part, :], rbuf.at[i, part, :], ya_send, ya_recv.at[i], (v, far)
        )

    def zcopy(k):
        return rcopy(zsend.at[k], zrecv.at[k], z_send, z_recv.at[k], (v, far))

    def ystart(i):
        zcopy(n + i).start()
        ycopy(i).start()

    def yarrive(i):
        zcopy(i).wait_recv()
        yacopy(i).wait_recv()
        zcopy(n + i).wait_recv()
        ycopy(i).wait_recv()

    def quantize(i, span, rate):
        sbuf[i, span, :] = (
            jnp.round(ybuf[span, :] * rate).astype(jnp.int32).astype(jnp.int16)
        )

    def first_dot(i):
        wwait(i, False)
        both = jnp.dot(split_rows[...], wbuf[i], preferred_element_type=jnp.float32)
        z = (both[0:rows] + both[rows : 2 * rows]) * chip_scale[:, 0:1]
        peak = jnp.maximum(TINY, jnp.max(jnp.abs(z), axis=0, keepdims=True))
        zsend[i] = peak * (1.0 / STEPS)
        sbuf[i, 0:rows, :] = jnp.round(z * (STEPS / peak)).astype(jnp.int32).astype(jnp.int16)
        zcopy(i).start()
        yacopy(i).start()

    def send_dot(i):
        def multiply(r, peak):
            span = pl.ds(pl.multiple_of(rows + r * mb_late, 16), mb_late)
            z = jnp.dot(nrm[span, :], wbuf[i], preferred_element_type=jnp.float32)
            ybuf[span, :] = z
            return jnp.maximum(peak, jnp.max(jnp.abs(z), axis=0, keepdims=True))

        peak = lax.fori_loop(
            0, late // mb_late, multiply, jnp.full((1, cn), TINY, jnp.float32)
        )
        zsend[n + i] = peak * (1.0 / STEPS)
        rate = STEPS / peak

        @pl.loop(1, V)
        def _(r):
            quantize(i, slot(r), rate)

    def keep_dot(i):
        wwait(n + i, True)

        @pl.loop(0, tokens // mb)
        def _(r):
            span = pl.ds(pl.multiple_of(r * mb, 16), mb)
            xbuf[span, :] = jnp.dot(
                nrm[span, :], wbuf[n + i], preferred_element_type=jnp.float32
            )

    rb = rows
    first_column = v * slab + w * quarter

    def stats(i):
        @pl.loop(0, V)
        def _(r):
            held = slot(r)
            span = vspan(vsource(r))
            late_z = n * ((r + V - 1) // V) + i
            target = ints_cols[span, 0:1]
            factor = ratio[held, :]
            lane = lax.broadcasted_iota(jnp.int32, (rb, LANES), 1)
            aim = jnp.broadcast_to(target, (rb, LANES)) - lane - (first_column + i * cn)
            xs = [
                xbuf[held, g * LANES : (g + 1) * LANES]
                + rbuf[i, held, g * LANES : (g + 1) * LANES].astype(jnp.int32).astype(jnp.float32)
                * (zrecv[late_z, 0:1, g * LANES : (g + 1) * LANES] * factor)
                for g in range(cn // LANES)
            ]
            m_old = m_acc[span, :]
            m_new = functools.reduce(jnp.maximum, xs, m_old)
            decay = jnp.exp(m_old - m_new)
            t = t_acc[span, :] * decay
            g_ = g_acc[span, :] * decay
            p = p_acc[span, :]
            for g, z in enumerate(xs):
                e = jnp.exp(z - m_new)
                t = t + e
                g_ = g_ + e * z
                p = p + jnp.where(aim == g * LANES, z, 0.0)
            m_acc[span, :] = m_new
            t_acc[span, :] = t
            g_acc[span, :] = g_
            p_acc[span, :] = p

    def relay(d):
        hcopy(d).wait_recv()
        fcopy(d, own_half).start()

    head = min(2, n)

    @pl.loop(0, head)
    def _(i):
        first_dot(i)

    normalize()

    @pl.loop(1, V)
    def _(d):
        hcopy(d).start()

    @pl.loop(head, n)
    def _(i):
        first_dot(i)

    @pl.loop(1, V)
    def _(d):
        relay(d)

    @pl.loop(1, V)
    def _(d):
        fcopy(d, mate_half).wait_recv()

    @pl.loop(0, DEPTH)
    def _(i):
        send_dot(i)
        ystart(i)

    @pl.loop(0, n)
    def _(k):
        wremote(n + k, True).start()
        wlocal(n + k, True).start()

    @pl.loop(1, V)
    def _(d):
        rmscopy(d, v).start()

    @pl.loop(1, WIDTH)
    def _(d):
        icopy(d, wsource(d)).wait_recv()

    for q in range(WIDTH):
        columns = [
            jnp.broadcast_to(to_column(ints_all[q, k : k + 1, :].astype(jnp.float32), bw), (bw, LANES))
            for k in range(2)
        ]
        pick_lane = lax.broadcasted_iota(jnp.int32, (bw, LANES), 1)
        ints_cols[q * bw : (q + 1) * bw, :] = jnp.where(
            pick_lane == 0, columns[0], columns[1]
        ).astype(jnp.int32)

    @pl.loop(0, n - DEPTH)
    def _(i):
        keep_dot(i)
        send_dot(i + DEPTH)
        yarrive(i)
        ystart(i + DEPTH)
        stats(i)

    @pl.loop(n - DEPTH, n)
    def _(i):
        keep_dot(i)
        yarrive(i)
        stats(i)

    m = m_acc[...]
    top = jnp.max(m, axis=1, keepdims=True)
    share = jnp.exp(m - top)
    tot = jnp.sum(t_acc[...] * share, axis=1, keepdims=True)
    wei = jnp.sum(g_acc[...] * share, axis=1, keepdims=True)
    pic = jnp.sum(p_acc[...], axis=1, keepdims=True)
    lane = lax.broadcasted_iota(jnp.int32, (tokens, LANES), 1)
    table = jnp.where(
        lane == 0, top, jnp.where(lane == 1, tot, jnp.where(lane == 2, wei, pic))
    )
    st1[w] = jnp.transpose(table)[0:4, :]

    def acopy(d, dev):
        return rcopy(st1.at[w], st1.at[dev], a_send, a_recv.at[d], (v, wpeer(d)))

    def bcopy(d, dev):
        return rcopy(st2.at[v], st2.at[dev], b_send, b_recv.at[d], (vpeer(d), w))

    def joined(parts):
        top = functools.reduce(jnp.maximum, [s[0:1, :] for s in parts])
        tot = jnp.zeros_like(top)
        wei = jnp.zeros_like(top)
        pic = jnp.zeros_like(top)
        for s in parts:
            share = jnp.exp(s[0:1, :] - top)
            tot = tot + s[1:2, :] * share
            wei = wei + s[2:3, :] * share
            pic = pic + s[3:4, :]
        return top, tot, wei, pic

    @pl.loop(1, WIDTH)
    def _(d):
        acopy(d, w).start()

    @pl.loop(1, WIDTH)
    def _(d):
        acopy(d, wsource(d)).wait_recv()

    sub = lax.broadcasted_iota(jnp.int32, (4, tokens), 0)
    top, tot, wei, pic = joined([st1[q] for q in range(WIDTH)])
    st2[v] = jnp.where(sub == 0, top, jnp.where(sub == 1, tot, jnp.where(sub == 2, wei, pic)))

    @pl.loop(1, V)
    def _(d):
        bcopy(d, v).start()

    @pl.loop(1, V)
    def _(d):
        rmscopy(d, vsource(d)).wait_recv()

    @pl.loop(1, V)
    def _(d):
        bcopy(d, vsource(d)).wait_recv()

    top, tot, wei, pic = joined([st2[q] for q in range(V)])
    big = lax.broadcasted_iota(jnp.int32, (LANES, tokens), 0)
    table = jnp.transpose(
        jnp.where(big == 0, top, jnp.where(big == 1, tot, jnp.where(big == 2, wei, pic)))
    )
    largest = table[:, 0:1]
    log_total = jnp.log(table[:, 1:2])
    logprob = table[:, 3:4] - largest - log_total
    entropy = largest + log_total - table[:, 2:3] / table[:, 1:2]
    rms = jnp.concatenate(
        [to_column(jnp.sqrt(msq_all[q] + epsilon), rows) for q in range(V)], axis=0
    )
    deal = ints_cols[:, 1:2]

    spots = lax.broadcasted_iota(jnp.int32, (tokens, rows), 1) + v * rows
    tok_ref[...] = jnp.sum(
        jnp.where(deal == spots, logprob, 0.0), axis=0, keepdims=True
    )

    r_row = lax.broadcasted_iota(jnp.int32, (1, LANES), 1)
    ends = jnp.zeros((1, LANES), jnp.int32)
    counts = jnp.ones((1, LANES), jnp.int32)
    for r in range(reqs):
        ends = ends + jnp.where(r_row >= r, lens_ref[r], 0)
        counts = jnp.where(r_row == r, lens_ref[r], counts)
    starts = (ends - counts).astype(jnp.float32)
    ends = ends.astype(jnp.float32)
    counts = counts.astype(jnp.float32)
    place = deal.astype(jnp.float32)
    member = (place >= starts) & (place < ends)
    for row, figure in enumerate((logprob, entropy, rms)):
        summed = jnp.sum(jnp.where(member, figure, 0.0), axis=0, keepdims=True)
        stat_ref[row : row + 1, :] = (summed / counts)[:, 0:reqs]
    highest = jnp.max(jnp.where(member, largest, LOW), axis=0, keepdims=True)
    stat_ref[3:4, :] = highest[:, 0:reqs]

    def drained(ref, sem):
        rcopy(ref, ref, sem, x_recv, (v, mate)).wait_send()

    xcopy().wait_send()
    drained(sq_all.at[0:2], q_send)
    drained(ints_all.at[0 : WIDTH - 1], i_send)
    drained(st1.at[0 : WIDTH - 1], a_send)
    drained(st2.at[0 : V - 1], b_send)
    drained(msq_all.at[0 : V - 1], r_send)
    drained(nrm.at[pl.ds(rows, late), own_half], h_send)
    drained(nrm.at[pl.ds(rows, late), own_half], f_send)
    drained(wbuf.at[:, own_half, :], w_send)
    drained(sbuf.at[:, pl.ds(rows, late), :], y_send)
    drained(sbuf.at[:, 0:rows, :], ya_send)
    drained(zsend, z_send)


def body(hidden, norm_gain, head_weight, lengths, deal, targets):
    rows, feats = hidden.shape
    V = lax.axis_size("vocab")
    tokens = rows * V
    slab = head_weight.shape[1]
    quarter = slab // WIDTH
    cn = next(c for c in (512, 256, 128) if quarter % c == 0)
    n = quarter // cn
    mb = next(c for c in (384, 256, 192, 128, 64, 48, 16) if tokens % c == 0)
    reqs = lengths.shape[0]
    bw = tokens // WIDTH

    gain = norm_gain.reshape(-1, LANES)
    bwp = -(-bw // LANES) * LANES
    late = tokens - rows
    mb_late = next(c for c in (336, 192, 144, 96, 48, 16) if late % c == 0)

    cfg = (V, rows, tokens, feats, slab, quarter, cn, n, mb, mb_late, reqs)
    f32, bf16 = jnp.float32, jnp.bfloat16
    dma = pltpu.SemaphoreType.DMA
    vmem = pl.BlockSpec(memory_space=pltpu.VMEM)
    smem = pl.BlockSpec(memory_space=pltpu.SMEM)
    tok, stat = pl.pallas_call(
        functools.partial(kernel, cfg),
        out_shape=(
            jax.ShapeDtypeStruct((1, rows), f32),
            jax.ShapeDtypeStruct((4, reqs), f32),
        ),
        in_specs=[vmem, vmem, smem, vmem, vmem, pl.BlockSpec(memory_space=pl.ANY)],
        out_specs=(vmem, vmem),
        scratch_shapes=[
            pltpu.VMEM((D // LANES, LANES), f32),
            pltpu.VMEM((WIDTH, 2, bwp), jnp.int32),
            pltpu.VMEM((tokens, LANES), jnp.int32),
            pltpu.VMEM((rows, feats), bf16),
            pltpu.VMEM((2 * rows, 2 * feats), bf16),
            pltpu.VMEM((rows, LANES), f32),
            pltpu.VMEM((tokens, LANES), f32),
            pltpu.VMEM((WIDTH, 1, LANES), f32),
            pltpu.VMEM((V, 1, LANES), f32),
            pltpu.VMEM((tokens, 2 * feats), bf16),
            pltpu.VMEM((2 * n, 2 * feats, cn), bf16),
            pltpu.VMEM((n, tokens, cn), jnp.int16),
            pltpu.VMEM((n, tokens, cn), jnp.int16),
            pltpu.VMEM((tokens, cn), f32),
            pltpu.VMEM((tokens, cn), f32),
            pltpu.VMEM((2 * n, 1, cn), f32),
            pltpu.VMEM((2 * n, 1, cn), f32),
            pltpu.VMEM((tokens, LANES), f32),
            pltpu.VMEM((tokens, LANES), f32),
            pltpu.VMEM((tokens, LANES), f32),
            pltpu.VMEM((tokens, LANES), f32),
            pltpu.VMEM((WIDTH, 4, tokens), f32),
            pltpu.VMEM((V, 4, tokens), f32),
            dma((12,)),
            dma,
            dma((WIDTH,)),
            dma((2,)),
            dma((V,)),
            dma((V,)),
            dma((V,)),
            dma((2 * n,)),
            dma((2 * n,)),
            dma((n,)),
            dma((2 * n,)),
            dma((n,)),
            dma((WIDTH,)),
            dma((V,)),
        ],
        compiler_params=pltpu.CompilerParams(
            collective_id=0, has_side_effects=True, vmem_limit_bytes=58 << 20
        ),
    )(targets[None], deal[None], lengths, gain, hidden, head_weight)
    return tok[0], stat


def solution(mesh):
    return jax.shard_map(
        body,
        mesh=mesh,
        in_specs=(P("vocab", "width"), P(), P("width", "vocab"), P(), P("width"), P("width")),
        out_specs=(P("vocab"), P()),
        check_vma=False,
    )
```

```python
import functools

import jax
import jax.numpy as jnp
from jax import lax
from jax.experimental import pallas as pl
from jax.experimental.pallas import tpu as pltpu
from jax.sharding import PartitionSpec as P

D = 2048
epsilon = 1e-06
LOW = -1e30
TINY = 1e-30
STEPS = 32767.0
DEPTH = 3
LANES = 128
REQ_LANE = 64
WIDTH = 4


def kernel(
    cfg,
    aim_ref,
    deal_ref,
    lens_ref,
    gain_ref,
    hid_ref,
    w_ref,
    out_ref,
    gains,
    ints_all,
    ints_cols,
    mate_hid,
    raw,
    split_rows,
    chip_scale,
    ratio,
    sq_all,
    msq_all,
    nrm,
    wbuf,
    sbuf,
    rbuf,
    xbuf,
    ybuf,
    zsend,
    zrecv,
    m_acc,
    t_acc,
    g_acc,
    p_acc,
    st1,
    st2,
    pick,
    fixed,
    once_send,
    x_recv,
    i_recv,
    q_recv,
    h_recv,
    f_recv,
    r_recv,
    wl_sem,
    w_recv,
    y_recv,
    z_recv,
    ya_recv,
    a_recv,
    b_recv,
):
    V, rows, tokens, feats, slab, quarter, cn, n, mb, mb_late, reqs = cfg
    v = lax.axis_index("vocab")
    w = lax.axis_index("width")
    lo = lax.rem(w, 2)
    hi = w // 2
    mate = w + 1 - 2 * lo
    far = w + 2 - 4 * hi
    bw = tokens // WIDTH
    x_send, i_send, q_send, h_send, f_send, r_send = [once_send.at[k] for k in range(6)]
    w_send, y_send, z_send, ya_send, a_send, b_send = [once_send.at[k] for k in range(6, 12)]

    def rcopy(src, dst, ss, rs, where):
        return pltpu.make_async_remote_copy(
            src_ref=src,
            dst_ref=dst,
            send_sem=ss,
            recv_sem=rs,
            device_id=where,
            device_id_type=pl.DeviceIdType.MESH,
        )

    def drained(ref, sem):
        rcopy(ref, ref, sem, x_recv, (v, mate)).wait_send()

    def landed(ref, sem):
        rcopy(ref, ref, x_send, sem, (v, mate)).wait_recv()

    def flipped(d):
        other, bit = 0, 1
        while bit < V:
            other = other + lax.rem(v // bit + d // bit, 2) * bit
            bit *= 2
        return other

    even = V & (V - 1) == 0

    def vpeer(d):
        return flipped(d) if even else lax.rem(v + d, V)

    def vsource(d):
        return flipped(d) if even else lax.rem(v + V - d, V)

    def wpeer(d):
        return lax.rem(w + d, WIDTH)

    def wsource(d):
        return lax.rem(w + WIDTH - d, WIDTH)

    def wcols(k, is_keep, dev):
        dev_far = dev + 2 - 4 * (dev // 2)
        q = dev if is_keep else dev_far
        base = k - n if is_keep else k
        return pl.ds(pl.multiple_of(q * quarter + base * cn, LANES), cn)

    own_half = pl.ds(pl.multiple_of(lo * feats, LANES), feats)
    mate_half = pl.ds(pl.multiple_of((1 - lo) * feats, LANES), feats)

    def wlocal(k, is_keep):
        return pltpu.make_async_copy(
            w_ref.at[:, wcols(k, is_keep, w)], wbuf.at[k, own_half, :], wl_sem.at[lax.rem(k, n)]
        )

    def wremote(k, is_keep):
        return rcopy(
            w_ref.at[:, wcols(k, is_keep, mate)],
            wbuf.at[k, own_half, :],
            w_send,
            w_recv.at[lax.rem(k, n)],
            (v, mate),
        )

    def wwait(k, is_keep):
        wlocal(k, is_keep).wait()
        rcopy(
            w_ref.at[:, wcols(k, is_keep, mate)],
            wbuf.at[k, mate_half, :],
            w_send,
            w_recv.at[lax.rem(k, n)],
            (v, mate),
        ).wait_recv()

    barrier = pltpu.get_barrier_semaphore()

    @pl.loop(1, WIDTH)
    def _(d):
        pl.semaphore_signal(
            barrier, inc=1, device_id=(v, wpeer(d)), device_id_type=pl.DeviceIdType.MESH
        )

    @pl.loop(1, V)
    def _(d):
        pl.semaphore_signal(
            barrier, inc=1, device_id=(vpeer(d), w), device_id_type=pl.DeviceIdType.MESH
        )

    @pl.loop(0, n)
    def _(k):
        wlocal(k, False).start()

    def slot(d):
        return pl.ds(pl.multiple_of(d * rows, 16), rows)

    def hcopy(d):
        return rcopy(hid_ref, raw.at[slot(d), own_half], h_send, h_recv.at[d], (vpeer(d), w))

    def squares(x):
        return jnp.sum(x * x, axis=1, keepdims=True)

    def to_row(column, wide):
        height = column.shape[0]
        there = lax.broadcasted_iota(jnp.int32, (height, wide), 1)
        here = lax.broadcasted_iota(jnp.int32, (height, wide), 0)
        return jnp.sum(jnp.where(there == here, column, 0.0), axis=0, keepdims=True)

    def to_column(row, height):
        wide = row.shape[1]
        there = lax.broadcasted_iota(jnp.int32, (height, wide), 1)
        here = lax.broadcasted_iota(jnp.int32, (height, wide), 0)
        return jnp.sum(jnp.where(there == here, row, 0.0), axis=1, keepdims=True)

    x = hid_ref[...].astype(jnp.float32)
    sq = squares(x)
    sq_all[w] = to_row(sq, LANES)
    gains[...] = gain_ref[...].astype(jnp.float32)
    ints_all[w] = jnp.zeros(ints_all.shape[1:], jnp.int32)
    ints_all[w, 0:1, 0:bw] = aim_ref[...]
    ints_all[w, 1:2, 0:bw] = deal_ref[...]
    pl.semaphore_wait(barrier, WIDTH - 1 + V - 1)

    def xcopy():
        return rcopy(hid_ref, mate_hid, x_send, x_recv, (v, mate))

    def icopy(d, dev):
        return rcopy(ints_all.at[w], ints_all.at[dev], i_send, i_recv, (v, wpeer(d)))

    across = far + 1 - 2 * lo

    def qstart(there):
        rcopy(sq_all.at[w], sq_all.at[w], q_send, q_recv.at[lo], (v, there)).start()

    def qwait(there):
        rcopy(
            sq_all.at[w], sq_all.at[there], q_send, q_recv.at[lax.rem(there, 2)], (v, there)
        ).wait_recv()

    xcopy().start()
    qstart(far)
    qstart(across)

    @pl.loop(0, DEPTH)
    def _(k):
        wremote(k, False).start()

    @pl.loop(1, V)
    def _(d):
        hcopy(V - d).start()

    @pl.loop(DEPTH, n)
    def _(k):
        wremote(k, False).start()

    @pl.loop(1, WIDTH)
    def _(d):
        icopy(d, w).start()

    groups = feats // LANES
    xcopy().wait_recv()
    y = mate_hid[...].astype(jnp.float32)
    sq_mate = squares(y)
    sq_all[mate] = to_row(sq_mate, LANES)
    chip_sq = sq + sq_mate
    chip_scale[...] = jnp.broadcast_to(
        lax.rsqrt(chip_sq * (1.0 / (2 * feats)) + epsilon), (rows, LANES)
    )
    for half, dev, value in ((lo, w, x), (1 - lo, mate, y)):
        for g in range(groups):
            column = pl.ds(pl.multiple_of(half * feats + g * LANES, LANES), LANES)
            scaled = value[:, g * LANES : (g + 1) * LANES] * gains[pl.ds(dev * groups + g, 1), :]
            upper = scaled.astype(jnp.bfloat16)
            split_rows[0:rows, column] = upper
            split_rows[rows : 2 * rows, column] = (scaled - upper.astype(jnp.float32)).astype(
                jnp.bfloat16
            )

    def vspan(dev):
        return pl.ds(pl.multiple_of(dev * rows, 16), rows)

    def normalize():
        qwait(far)
        qwait(across)
        total_sq = sq_all[0] + sq_all[1] + sq_all[2] + sq_all[3]
        mean_row = total_sq * (1.0 / D)
        msq_all[v] = mean_row
        mean_sq = to_column(mean_row, rows)
        scale = lax.rsqrt(mean_sq + epsilon)
        far_sq = to_column(sq_all[far] + sq_all[across], rows)
        far_scale = lax.rsqrt(far_sq * (1.0 / (2 * feats)) + epsilon)
        ratio[0:rows, :] = jnp.broadcast_to(scale / far_scale, (rows, LANES))
        for half, dev, source in ((lo, w, hid_ref), (1 - lo, mate, mate_hid)):
            for g in range(groups):
                column = pl.ds(pl.multiple_of(half * feats + g * LANES, LANES), LANES)
                value = source[:, g * LANES : (g + 1) * LANES].astype(jnp.float32)
                nrm[0:rows, column] = (
                    value * scale * gains[pl.ds(dev * groups + g, 1), :]
                ).astype(jnp.bfloat16)

    def fcopy(d, half):
        part = raw.at[slot(d), half]
        return rcopy(part, part, f_send, f_recv, (v, mate))

    def rmscopy(d, dev):
        return rcopy(msq_all.at[v], msq_all.at[dev], r_send, r_recv, (vpeer(d), w))

    ratio[pl.ds(rows, tokens - rows), :] = jnp.ones((tokens - rows, LANES), jnp.float32)
    m_acc[...] = jnp.full((tokens, LANES), LOW, jnp.float32)
    t_acc[...] = jnp.zeros((tokens, LANES), jnp.float32)
    g_acc[...] = jnp.zeros((tokens, LANES), jnp.float32)
    p_acc[...] = jnp.zeros((tokens, LANES), jnp.float32)

    late = tokens - rows

    def ycopy(i):
        part = pl.ds(rows, late)
        return rcopy(
            sbuf.at[i, part, :], rbuf.at[i, part, :], y_send, y_recv.at[i], (v, far)
        )

    def yacopy(i):
        part = pl.ds(0, rows)
        return rcopy(
            sbuf.at[i, part, :], rbuf.at[i, part, :], ya_send, ya_recv.at[i], (v, far)
        )

    def zcopy(k):
        return rcopy(zsend.at[k], zrecv.at[k], z_send, z_recv.at[k], (v, far))

    def ystart(i):
        zcopy(n + i).start()
        ycopy(i).start()

    def yarrive(i):
        zcopy(i).wait_recv()
        yacopy(i).wait_recv()
        zcopy(n + i).wait_recv()
        ycopy(i).wait_recv()

    def lanes_peak(z):
        peak = jnp.max(jnp.abs(z), axis=0, keepdims=True)
        parts = [peak[:, g * LANES : (g + 1) * LANES] for g in range(cn // LANES)]
        return functools.reduce(jnp.maximum, parts)

    def quantize(i, span, rate, z):
        for g in range(cn // LANES):
            part = slice(g * LANES, (g + 1) * LANES)
            sbuf[i, span, part] = (
                jnp.round(z[:, part] * rate).astype(jnp.int32).astype(jnp.int16)
            )

    def first_dot(i):
        wwait(i, False)
        both = jnp.dot(split_rows[...], wbuf[i], preferred_element_type=jnp.float32)
        z = (both[0:rows] + both[rows : 2 * rows]) * chip_scale[:, 0:1]
        peak = jnp.maximum(TINY, lanes_peak(z))
        zsend[i] = peak * (1.0 / STEPS)
        quantize(i, pl.ds(0, rows), STEPS / peak, z)
        zcopy(i).start()
        yacopy(i).start()

    def send_dot(i):
        def multiply(r, peak):
            span = pl.ds(pl.multiple_of(rows + r * mb_late, 16), mb_late)
            z = jnp.dot(nrm[span, :], wbuf[i], preferred_element_type=jnp.float32)
            ybuf[span, :] = z
            return jnp.maximum(peak, lanes_peak(z))

        peak = lax.fori_loop(
            0, late // mb_late, multiply, jnp.full((1, LANES), TINY, jnp.float32)
        )
        zsend[n + i] = peak * (1.0 / STEPS)
        rate = STEPS / peak

        @pl.loop(1, V)
        def _(r):
            quantize(i, slot(r), rate, ybuf[slot(r), :])

    def keep_dot(i):
        wwait(n + i, True)

        @pl.loop(0, tokens // mb)
        def _(r):
            span = pl.ds(pl.multiple_of(r * mb, 16), mb)
            xbuf[span, :] = jnp.dot(
                nrm[span, :], wbuf[n + i], preferred_element_type=jnp.float32
            )

    rb = rows
    first_column = v * slab + w * quarter

    def stats(i):
        @pl.loop(0, V)
        def _(r):
            held = slot(r)
            span = vspan(vsource(r))
            late_z = n * ((r + V - 1) // V) + i
            target = ints_cols[span, 0:1]
            factor = zrecv[late_z] * ratio[held, :]
            lane = lax.broadcasted_iota(jnp.int32, (rb, LANES), 1)
            aim = jnp.broadcast_to(target, (rb, LANES)) - lane - (first_column + i * cn)
            xs = [
                xbuf[held, g * LANES : (g + 1) * LANES]
                + rbuf[i, held, g * LANES : (g + 1) * LANES].astype(jnp.int32).astype(jnp.float32)
                * factor
                for g in range(cn // LANES)
            ]
            m_old = m_acc[span, :]
            m_new = functools.reduce(jnp.maximum, xs, m_old)
            decay = jnp.exp(m_old - m_new)
            t = t_acc[span, :] * decay
            g_ = g_acc[span, :] * decay
            p = p_acc[span, :]
            for g, z in enumerate(xs):
                e = jnp.exp(z - m_new)
                t = t + e
                g_ = g_ + e * z
                p = p + jnp.where(aim == g * LANES, z, 0.0)
            m_acc[span, :] = m_new
            t_acc[span, :] = t
            g_acc[span, :] = g_
            p_acc[span, :] = p

    def relay(d):
        hcopy(d).wait_recv()
        fcopy(d, own_half).start()

    head = min(2, n)

    @pl.loop(0, head)
    def _(i):
        first_dot(i)

    normalize()

    @pl.loop(1, V)
    def _(d):
        rmscopy(d, v).start()

    turns = min(n - head, V - 2)

    @pl.loop(0, turns)
    def _(i):
        first_dot(head + i)
        relay(V - 1 - i)

    @pl.loop(head + turns, n)
    def _(i):
        first_dot(i)

    @pl.loop(1 + turns, V)
    def _(d):
        relay(V - d)

    landed(msq_all.at[0 : V - 1], r_recv)
    landed(raw.at[pl.ds(rows, late), mate_half], f_recv)

    @pl.loop(1, V)
    def _(d):
        scale = lax.rsqrt(to_column(msq_all[vsource(d)], rows) + epsilon)
        for g in range(2 * groups):
            column = slice(g * LANES, (g + 1) * LANES)
            gain_row = gains[pl.ds((w - lo) * groups + g, 1), :]
            nrm[slot(d), column] = (
                raw[slot(d), column].astype(jnp.float32) * scale * gain_row
            ).astype(jnp.bfloat16)

    @pl.loop(0, DEPTH)
    def _(i):
        send_dot(i)
        ystart(i)

    @pl.loop(0, n)
    def _(k):
        wremote(n + k, True).start()
        wlocal(n + k, True).start()

    landed(ints_all.at[0 : WIDTH - 1], i_recv)

    for q in range(WIDTH):
        columns = [
            jnp.broadcast_to(to_column(ints_all[q, k : k + 1, :].astype(jnp.float32), bw), (bw, LANES))
            for k in range(2)
        ]
        pick_lane = lax.broadcasted_iota(jnp.int32, (bw, LANES), 1)
        ints_cols[q * bw : (q + 1) * bw, :] = jnp.where(
            pick_lane == 0, columns[0], columns[1]
        ).astype(jnp.int32)

    r_row = lax.broadcasted_iota(jnp.int32, (1, LANES), 1)
    ends = jnp.zeros((1, LANES), jnp.int32)
    counts = jnp.ones((1, LANES), jnp.int32)
    for r in range(reqs):
        ends = ends + jnp.where(r_row >= REQ_LANE + r, lens_ref[r], 0)
        counts = jnp.where(r_row == REQ_LANE + r, lens_ref[r], counts)
    asked = (r_row >= REQ_LANE) & (r_row < REQ_LANE + reqs)
    starts = jnp.where(asked, ends - counts, tokens).astype(jnp.float32)
    ends = ends.astype(jnp.float32)
    counts = counts.astype(jnp.float32)
    place = ints_cols[:, 1:2].astype(jnp.float32)
    spot = jnp.where(r_row < rows, v * rows + r_row, tokens).astype(jnp.float32)
    member = (place >= starts) & (place < ends)
    pick[...] = jnp.where(member | (place == spot), 1.0, 0.0)
    rms = jnp.concatenate(
        [to_column(jnp.sqrt(msq_all[q] + epsilon), rows) for q in range(V)], axis=0
    )
    fixed[0:1, :] = counts
    fixed[1:2, :] = jnp.sum(jnp.where(member, rms, 0.0), axis=0, keepdims=True) / counts
    st1[w, :, pl.ds(tokens, LANES)] = jnp.zeros((4, LANES), jnp.float32)

    @pl.loop(0, n - DEPTH)
    def _(i):
        keep_dot(i)
        send_dot(i + DEPTH)
        yarrive(i)
        ystart(i + DEPTH)
        stats(i)

    @pl.loop(n - DEPTH, n)
    def _(i):
        keep_dot(i)
        yarrive(i)
        stats(i)

    m = m_acc[...]
    top = jnp.max(m, axis=1, keepdims=True)
    share = jnp.exp(m - top)
    tot = jnp.sum(t_acc[...] * share, axis=1, keepdims=True)
    wei = jnp.sum(g_acc[...] * share, axis=1, keepdims=True)
    pic = jnp.sum(p_acc[...], axis=1, keepdims=True)
    lane = lax.broadcasted_iota(jnp.int32, (tokens, LANES), 1)
    table = jnp.where(
        lane == 0, top, jnp.where(lane == 1, tot, jnp.where(lane == 2, wei, pic))
    )
    st1[w, :, 0:tokens] = jnp.transpose(table)[0:4, :]
    inside = (pick[...] > 0.5) & (lane >= REQ_LANE)
    st1[w, 0:1, pl.ds(tokens, LANES)] = jnp.max(
        jnp.where(inside, top, LOW), axis=0, keepdims=True
    )

    def acopy(d, dev):
        return rcopy(st1.at[w], st1.at[dev], a_send, a_recv, (v, wpeer(d)))

    def bcopy(d, dev):
        return rcopy(st2.at[v], st2.at[dev], b_send, b_recv, (vpeer(d), w))

    def joined(parts):
        top = functools.reduce(jnp.maximum, [s[0:1, :] for s in parts])
        tot = jnp.zeros_like(top)
        wei = jnp.zeros_like(top)
        pic = jnp.zeros_like(top)
        for s in parts:
            share = jnp.exp(s[0:1, :] - top)
            tot = tot + s[1:2, :] * share
            wei = wei + s[2:3, :] * share
            pic = pic + s[3:4, :]
        return top, tot, wei, pic

    @pl.loop(1, WIDTH)
    def _(d):
        acopy(d, w).start()

    xcopy().wait_send()
    drained(sq_all.at[0:2], q_send)
    drained(ints_all.at[0 : WIDTH - 1], i_send)
    drained(msq_all.at[0 : V - 1], r_send)
    drained(raw.at[pl.ds(rows, late), own_half], h_send)
    drained(raw.at[pl.ds(rows, late), own_half], f_send)
    drained(wbuf.at[:, own_half, :], w_send)
    drained(sbuf.at[:, pl.ds(rows, late), :], y_send)
    drained(sbuf.at[:, 0:rows, :], ya_send)
    drained(zsend, z_send)
    landed(st1.at[0 : WIDTH - 1], a_recv)

    sub = lax.broadcasted_iota(jnp.int32, (4, tokens + LANES), 0)
    top, tot, wei, pic = joined([st1[q] for q in range(WIDTH)])
    st2[v] = jnp.where(sub == 0, top, jnp.where(sub == 1, tot, jnp.where(sub == 2, wei, pic)))

    @pl.loop(1, V)
    def _(d):
        bcopy(d, v).start()

    landed(st2.at[0 : V - 1], b_recv)

    top, tot, wei, pic = joined([st2[q] for q in range(V)])
    highest = top[:, tokens : tokens + LANES]
    largest, tot, wei, pic = [row[:, 0:tokens] for row in (top, tot, wei, pic)]
    log_total = jnp.log(tot)
    place = lax.broadcasted_iota(jnp.int32, (8, tokens), 0)
    spread = jnp.zeros((8, tokens), jnp.float32)
    for k, rest in enumerate(
        (pic - largest - log_total, largest + log_total - wei / tot)
    ):
        for part in range(3):
            upper = rest.astype(jnp.bfloat16).astype(jnp.float32)
            spread = jnp.where(place == 2 * part + k, upper, spread)
            rest = rest - upper
    dealt = jnp.dot(
        spread.astype(jnp.bfloat16),
        pick[...].astype(jnp.bfloat16),
        preferred_element_type=jnp.float32,
    )
    sums = dealt[0:2] + dealt[2:4] + dealt[4:6]
    out_ref[0:1, :] = sums[0:1]
    out_ref[4:6, :] = sums / fixed[0:1, :]
    out_ref[6:7, :] = fixed[1:2, :]
    out_ref[7:8, :] = highest
    drained(st1.at[0 : WIDTH - 1], a_send)
    drained(st2.at[0 : V - 1], b_send)


def finish(rows, reqs, res_ref, tok_ref, stat_ref):
    tok_ref[...] = res_ref[0:1, 0:rows]
    stat_ref[...] = res_ref[4:8, REQ_LANE : REQ_LANE + reqs]


def body(hidden, norm_gain, head_weight, lengths, deal, targets):
    rows, feats = hidden.shape
    V = lax.axis_size("vocab")
    tokens = rows * V
    slab = head_weight.shape[1]
    quarter = slab // WIDTH
    cn = next(c for c in (512, 256, 128) if quarter % c == 0)
    n = quarter // cn
    mb = next(c for c in (384, 256, 192, 128, 64, 48, 16) if tokens % c == 0)
    reqs = lengths.shape[0]
    bw = tokens // WIDTH

    gain = norm_gain.reshape(-1, LANES)
    bwp = -(-bw // LANES) * LANES
    late = tokens - rows
    mb_late = next(c for c in (336, 192, 144, 96, 48, 16) if late % c == 0)

    cfg = (V, rows, tokens, feats, slab, quarter, cn, n, mb, mb_late, reqs)
    f32, bf16 = jnp.float32, jnp.bfloat16
    dma = pltpu.SemaphoreType.DMA
    vmem = pl.BlockSpec(memory_space=pltpu.VMEM)
    smem = pl.BlockSpec(memory_space=pltpu.SMEM)
    res = pl.pallas_call(
        functools.partial(kernel, cfg),
        out_shape=jax.ShapeDtypeStruct((8, LANES), f32),
        in_specs=[vmem, vmem, smem, vmem, vmem, pl.BlockSpec(memory_space=pl.ANY)],
        out_specs=vmem,
        scratch_shapes=[
            pltpu.VMEM((D // LANES, LANES), f32),
            pltpu.VMEM((WIDTH, 2, bwp), jnp.int32),
            pltpu.VMEM((tokens, LANES), jnp.int32),
            pltpu.VMEM((rows, feats), bf16),
            pltpu.VMEM((tokens, 2 * feats), bf16),
            pltpu.VMEM((2 * rows, 2 * feats), bf16),
            pltpu.VMEM((rows, LANES), f32),
            pltpu.VMEM((tokens, LANES), f32),
            pltpu.VMEM((WIDTH, 1, LANES), f32),
            pltpu.VMEM((V, 1, LANES), f32),
            pltpu.VMEM((tokens, 2 * feats), bf16),
            pltpu.VMEM((2 * n, 2 * feats, cn), bf16),
            pltpu.VMEM((n, tokens, cn), jnp.int16),
            pltpu.VMEM((n, tokens, cn), jnp.int16),
            pltpu.VMEM((tokens, cn), f32),
            pltpu.VMEM((tokens, cn), f32),
            pltpu.VMEM((2 * n, 1, LANES), f32),
            pltpu.VMEM((2 * n, 1, LANES), f32),
            pltpu.VMEM((tokens, LANES), f32),
            pltpu.VMEM((tokens, LANES), f32),
            pltpu.VMEM((tokens, LANES), f32),
            pltpu.VMEM((tokens, LANES), f32),
            pltpu.VMEM((WIDTH, 4, tokens + LANES), f32),
            pltpu.VMEM((V, 4, tokens + LANES), f32),
            pltpu.VMEM((tokens, LANES), f32),
            pltpu.VMEM((8, LANES), f32),
            dma((12,)),
            dma,
            dma,
            dma((2,)),
            dma((V,)),
            dma,
            dma,
            dma((n,)),
            dma((n,)),
            dma((n,)),
            dma((2 * n,)),
            dma((n,)),
            dma,
            dma,
        ],
        compiler_params=pltpu.CompilerParams(
            collective_id=0, has_side_effects=True, vmem_limit_bytes=58 << 20
        ),
    )(targets[None], deal[None], lengths, gain, hidden, head_weight)
    tok, stat = pl.pallas_call(
        functools.partial(finish, rows, reqs),
        out_shape=(
            jax.ShapeDtypeStruct((1, rows), f32),
            jax.ShapeDtypeStruct((4, reqs), f32),
        ),
        in_specs=[vmem],
        out_specs=(vmem, vmem),
    )(res)
    return tok[0], stat


def solution(mesh):
    return jax.shard_map(
        body,
        mesh=mesh,
        in_specs=(P("vocab", "width"), P(), P("width", "vocab"), P(), P("width"), P("width")),
        out_specs=(P("vocab"), P()),
        check_vma=False,
    )
```

```python
import functools

import jax
import jax.numpy as jnp
from jax import lax
from jax.experimental import pallas as pl
from jax.experimental.pallas import tpu as pltpu
from jax.sharding import PartitionSpec as P

D = 2048
epsilon = 1e-06
LOW = -1e30
TINY = 1e-30
STEPS = 32767.0
DEPTH = 3
LANES = 128
REQ_LANE = 64
WIDTH = 4


def kernel(
    cfg,
    aim_hbm,
    deal_hbm,
    lens_ref,
    gain_hbm,
    hid_hbm,
    w_ref,
    out_ref,
    aim_ref,
    deal_ref,
    gain_ref,
    hid_ref,
    gains,
    ints_all,
    ints_cols,
    mate_hid,
    raw,
    split_rows,
    chip_scale,
    ratio,
    sq_all,
    msq_all,
    nrm,
    wbuf,
    sbuf,
    rbuf,
    xbuf,
    ybuf,
    zsend,
    zrecv,
    zfirst,
    zfull,
    m_acc,
    t_acc,
    g_acc,
    p_acc,
    st1,
    st2,
    pick,
    fixed,
    once_send,
    in_sem,
    x_recv,
    s_recv,
    i_recv,
    q_recv,
    h_recv,
    f_recv,
    r_recv,
    wl_sem,
    w_recv,
    piece_recv,
    y_recv,
    block_recv,
    z_recv,
    zp_recv,
    ya_recv,
    a_recv,
    b_recv,
):
    V, rows, tokens, feats, slab, quarter, cn, n, mb, mb_late, reqs = cfg
    v = lax.axis_index("vocab")
    w = lax.axis_index("width")
    lo = lax.rem(w, 2)
    hi = w // 2
    mate = w + 1 - 2 * lo
    far = w + 2 - 4 * hi
    bw = tokens // WIDTH
    x_send, i_send, q_send, h_send, f_send, r_send = [once_send.at[k] for k in range(6)]
    w_send, y_send, z_send, ya_send, a_send, b_send, s_send, zp_send = [
        once_send.at[k] for k in range(6, 14)
    ]
    pieces = cn // LANES

    def rcopy(src, dst, ss, rs, where):
        return pltpu.make_async_remote_copy(
            src_ref=src,
            dst_ref=dst,
            send_sem=ss,
            recv_sem=rs,
            device_id=where,
            device_id_type=pl.DeviceIdType.MESH,
        )

    def drained(ref, sem):
        rcopy(ref, ref, sem, x_recv, (v, mate)).wait_send()

    def landed(ref, sem):
        rcopy(ref, ref, x_send, sem, (v, mate)).wait_recv()

    def flipped(d):
        other, bit = 0, 1
        while bit < V:
            other = other + lax.rem(v // bit + d // bit, 2) * bit
            bit *= 2
        return other

    even = V & (V - 1) == 0

    def vpeer(d):
        return flipped(d) if even else lax.rem(v + d, V)

    def vsource(d):
        return flipped(d) if even else lax.rem(v + V - d, V)

    def wpeer(d):
        return lax.rem(w + d, WIDTH)

    def wsource(d):
        return lax.rem(w + WIDTH - d, WIDTH)

    def wcols(k, is_keep, dev):
        dev_far = dev + 2 - 4 * (dev // 2)
        q = dev if is_keep else dev_far
        base = k - n if is_keep else k
        return pl.ds(pl.multiple_of(q * quarter + base * cn, LANES), cn)

    own_half = pl.ds(pl.multiple_of(lo * feats, LANES), feats)
    mate_half = pl.ds(pl.multiple_of((1 - lo) * feats, LANES), feats)

    def wlocal(k, is_keep):
        return pltpu.make_async_copy(
            w_ref.at[:, wcols(k, is_keep, w)], wbuf.at[k, own_half, :], wl_sem.at[lax.rem(k, n)]
        )

    def wremote(k, is_keep):
        return rcopy(
            w_ref.at[:, wcols(k, is_keep, mate)],
            wbuf.at[k, own_half, :],
            w_send,
            w_recv.at[lax.rem(k, n)],
            (v, mate),
        )

    def wpiece(p, there):
        columns = wcols(0, False, mate).start + p * LANES
        return rcopy(
            w_ref.at[:, pl.ds(pl.multiple_of(columns, LANES), LANES)],
            wbuf.at[0, there, pl.ds(p * LANES, LANES)],
            w_send,
            piece_recv.at[p],
            (v, mate),
        )

    def wwait(k, is_keep):
        wlocal(k, is_keep).wait()
        rcopy(
            w_ref.at[:, wcols(k, is_keep, mate)],
            wbuf.at[k, mate_half, :],
            w_send,
            w_recv.at[lax.rem(k, n)],
            (v, mate),
        ).wait_recv()

    barrier = pltpu.get_barrier_semaphore()

    @pl.loop(1, WIDTH)
    def _(d):
        pl.semaphore_signal(
            barrier, inc=1, device_id=(v, wpeer(d)), device_id_type=pl.DeviceIdType.MESH
        )

    @pl.loop(1, V)
    def _(d):
        pl.semaphore_signal(
            barrier, inc=1, device_id=(vpeer(d), w), device_id_type=pl.DeviceIdType.MESH
        )

    loads = [
        pltpu.make_async_copy(source, there, in_sem.at[k])
        for k, (source, there) in enumerate(
            ((hid_hbm, hid_ref), (gain_hbm, gain_ref), (aim_hbm, aim_ref), (deal_hbm, deal_ref))
        )
    ]
    for load in loads:
        load.start()

    @pl.loop(0, n)
    def _(k):
        wlocal(k, False).start()

    late = tokens - rows
    groups = feats // LANES
    ratio[pl.ds(rows, late), :] = jnp.ones((late, LANES), jnp.float32)
    m_acc[...] = jnp.full((tokens, LANES), LOW, jnp.float32)
    t_acc[...] = jnp.zeros((tokens, LANES), jnp.float32)
    g_acc[...] = jnp.zeros((tokens, LANES), jnp.float32)
    p_acc[...] = jnp.zeros((tokens, LANES), jnp.float32)

    def slot(d):
        return pl.ds(pl.multiple_of(d * rows, 16), rows)

    def hcopy(d):
        return rcopy(hid_ref, raw.at[slot(d), own_half], h_send, h_recv.at[d], (vpeer(d), w))

    def squares(x):
        return jnp.sum(x * x, axis=1, keepdims=True)

    def to_row(column, wide):
        height = column.shape[0]
        there = lax.broadcasted_iota(jnp.int32, (height, wide), 1)
        here = lax.broadcasted_iota(jnp.int32, (height, wide), 0)
        return jnp.sum(jnp.where(there == here, column, 0.0), axis=0, keepdims=True)

    def to_column(row, height):
        wide = row.shape[1]
        there = lax.broadcasted_iota(jnp.int32, (height, wide), 1)
        here = lax.broadcasted_iota(jnp.int32, (height, wide), 0)
        return jnp.sum(jnp.where(there == here, row, 0.0), axis=1, keepdims=True)

    for load in loads:
        load.wait()
    gains[...] = gain_ref[...].astype(jnp.float32)
    x = hid_ref[...].astype(jnp.float32)
    sq = squares(x)
    sq_all[w] = to_row(sq, LANES)
    for g in range(groups):
        column = pl.ds(pl.multiple_of(lo * feats + g * LANES, LANES), LANES)
        scaled = x[:, g * LANES : (g + 1) * LANES] * gains[pl.ds(w * groups + g, 1), :]
        upper = scaled.astype(jnp.bfloat16)
        split_rows[0:rows, column] = upper
        split_rows[rows : 2 * rows, column] = (scaled - upper.astype(jnp.float32)).astype(
            jnp.bfloat16
        )
    ints_all[w] = jnp.zeros(ints_all.shape[1:], jnp.int32)
    ints_all[w, 0:1, 0:bw] = aim_ref[...]
    ints_all[w, 1:2, 0:bw] = deal_ref[...]
    pl.semaphore_wait(barrier, WIDTH - 1 + V - 1)

    def xcopy():
        return rcopy(hid_ref, mate_hid, x_send, x_recv, (v, mate))

    def icopy(d, dev):
        return rcopy(ints_all.at[w], ints_all.at[dev], i_send, i_recv, (v, wpeer(d)))

    across = far + 1 - 2 * lo

    def scopy(half):
        return rcopy(
            split_rows.at[:, half], split_rows.at[:, half], s_send, s_recv, (v, mate)
        )

    def qstart(there):
        rcopy(sq_all.at[w], sq_all.at[w], q_send, q_recv.at[w], (v, there)).start()

    def qwait(there):
        rcopy(
            sq_all.at[w], sq_all.at[there], q_send, q_recv.at[there], (v, there)
        ).wait_recv()

    scopy(own_half).start()
    qstart(mate)
    for p in range(pieces):
        wpiece(p, own_half).start()
    qstart(far)
    qstart(across)

    @pl.loop(1, DEPTH)
    def _(k):
        wremote(k, False).start()

    xcopy().start()

    @pl.loop(1, V)
    def _(d):
        hcopy(V - d).start()

    @pl.loop(DEPTH, n)
    def _(k):
        wremote(k, False).start()

    @pl.loop(1, WIDTH)
    def _(d):
        icopy(d, w).start()

    qwait(mate)
    chip_sq = sq + to_column(sq_all[mate], rows)
    chip_scale[...] = jnp.broadcast_to(
        lax.rsqrt(chip_sq * (1.0 / (2 * feats)) + epsilon), (rows, LANES)
    )
    scopy(mate_half).wait_recv()

    def vspan(dev):
        return pl.ds(pl.multiple_of(dev * rows, 16), rows)

    def normalize():
        qwait(far)
        qwait(across)
        xcopy().wait_recv()
        total_sq = sq_all[0] + sq_all[1] + sq_all[2] + sq_all[3]
        mean_row = total_sq * (1.0 / D)
        msq_all[v] = mean_row
        mean_sq = to_column(mean_row, rows)
        scale = lax.rsqrt(mean_sq + epsilon)
        far_sq = to_column(sq_all[far] + sq_all[across], rows)
        far_scale = lax.rsqrt(far_sq * (1.0 / (2 * feats)) + epsilon)
        ratio[0:rows, :] = jnp.broadcast_to(scale / far_scale, (rows, LANES))
        for half, dev, source in ((lo, w, hid_ref), (1 - lo, mate, mate_hid)):
            for g in range(groups):
                column = pl.ds(pl.multiple_of(half * feats + g * LANES, LANES), LANES)
                value = source[:, g * LANES : (g + 1) * LANES].astype(jnp.float32)
                nrm[0:rows, column] = (
                    value * scale * gains[pl.ds(dev * groups + g, 1), :]
                ).astype(jnp.bfloat16)

    def fcopy(d, half):
        part = raw.at[slot(d), half]
        return rcopy(part, part, f_send, f_recv, (v, mate))

    def rmscopy(d, dev):
        return rcopy(msq_all.at[v], msq_all.at[dev], r_send, r_recv, (vpeer(d), w))

    def ycopy(i):
        part = pl.ds(rows, late)
        return rcopy(
            sbuf.at[i, part, :], rbuf.at[i, part, :], y_send, y_recv.at[i], (v, far)
        )

    def yacopy(i):
        part = pl.ds(0, rows)
        return rcopy(
            sbuf.at[i, part, :], rbuf.at[i, part, :], ya_send, ya_recv.at[i], (v, far)
        )

    def zcopy(k):
        return rcopy(zsend.at[k], zrecv.at[k], z_send, z_recv.at[k], (v, far))

    def zpiece(p):
        return rcopy(zfirst.at[0, p], zfirst.at[1, p], zp_send, zp_recv, (v, far))

    def yapiece(p):
        part = pl.ds(0, rows)
        columns = pl.ds(p * LANES, LANES)
        return rcopy(
            sbuf.at[0, part, columns], rbuf.at[0, part, columns], ya_send, ya_recv.at[0], (v, far)
        )

    def yblock(d):
        return rcopy(
            sbuf.at[n - 1, slot(d), :], rbuf.at[n - 1, slot(d), :], y_send, block_recv.at[d], (v, far)
        )

    def ystart(i):
        zcopy(n + i).start()
        ycopy(i).start()

    def zspread(k):
        scale = zrecv[k]
        for p in range(pieces):
            zfull[k, p] = scale

    def yarrive(i):
        yacopy(i).wait_recv()

        @pl.when(i > 0)
        def _():
            zcopy(i).wait_recv()
            zspread(i)

        zcopy(n + i).wait_recv()
        zspread(n + i)

    def lanes_peak(z):
        peak = jnp.max(jnp.abs(z), axis=0, keepdims=True)
        parts = [peak[:, g * LANES : (g + 1) * LANES] for g in range(cn // LANES)]
        return functools.reduce(jnp.maximum, parts)

    def quantize(i, span, rate, z):
        for g in range(cn // LANES):
            part = slice(g * LANES, (g + 1) * LANES)
            sbuf[i, span, part] = (
                jnp.round(z[:, part] * rate).astype(jnp.int32).astype(jnp.int16)
            )

    def first_rows(weights):
        both = jnp.dot(split_rows[...], weights, preferred_element_type=jnp.float32)
        return (both[0:rows] + both[rows : 2 * rows]) * chip_scale[:, 0:1]

    def first_pieces():
        wlocal(0, False).wait()
        for p in range(pieces):
            wpiece(p, mate_half).wait_recv()
            columns = slice(p * LANES, (p + 1) * LANES)
            z = first_rows(wbuf[0, :, columns])
            peak = jnp.maximum(TINY, jnp.max(jnp.abs(z), axis=0, keepdims=True))
            zfirst[0, p] = peak * (1.0 / STEPS)
            sbuf[0, 0:rows, columns] = (
                jnp.round(z * (STEPS / peak)).astype(jnp.int32).astype(jnp.int16)
            )
            yapiece(p).start()
            zpiece(p).start()

    def first_dot(i):
        wwait(i, False)
        z = first_rows(wbuf[i])
        peak = jnp.maximum(TINY, lanes_peak(z))
        zsend[i] = peak * (1.0 / STEPS)
        quantize(i, pl.ds(0, rows), STEPS / peak, z)
        zcopy(i).start()
        yacopy(i).start()

    def send_dot(i):
        def multiply(r, peak):
            span = pl.ds(pl.multiple_of(rows + r * mb_late, 16), mb_late)
            z = jnp.dot(nrm[span, :], wbuf[i], preferred_element_type=jnp.float32)
            ybuf[span, :] = z
            return jnp.maximum(peak, lanes_peak(z))

        peak = lax.fori_loop(
            0, late // mb_late, multiply, jnp.full((1, LANES), TINY, jnp.float32)
        )
        zsend[n + i] = peak * (1.0 / STEPS)
        rate = STEPS / peak

        @pl.loop(1, V)
        def _(r):
            quantize(i, slot(r), rate, ybuf[slot(r), :])

    def keep_dot(i):
        wwait(n + i, True)

        @pl.loop(0, tokens // mb)
        def _(r):
            span = pl.ds(pl.multiple_of(r * mb, 16), mb)
            xbuf[span, :] = jnp.dot(
                nrm[span, :], wbuf[n + i], preferred_element_type=jnp.float32
            )

    rb = rows
    first_column = v * slab + w * quarter

    def stats(i):
        @pl.loop(0, V)
        def _(r):
            block_stats(i, r)

    def block_stats(i, r):
        held = slot(r)
        span = vspan(vsource(r))
        late_z = n * ((r + V - 1) // V) + i
        target = ints_cols[span, 0:1]
        factor = ratio[held, :]
        lane = lax.broadcasted_iota(jnp.int32, (rb, LANES), 1)
        aim = jnp.broadcast_to(target, (rb, LANES)) - lane - (first_column + i * cn)
        xs = [
            xbuf[held, g * LANES : (g + 1) * LANES]
            + rbuf[i, held, g * LANES : (g + 1) * LANES].astype(jnp.int32).astype(jnp.float32)
            * (zfull[late_z, g] * factor)
            for g in range(cn // LANES)
        ]
        m_old = m_acc[span, :]
        m_new = functools.reduce(jnp.maximum, xs, m_old)
        decay = jnp.exp(m_old - m_new)
        t = t_acc[span, :] * decay
        g_ = g_acc[span, :] * decay
        p = p_acc[span, :]
        for g, z in enumerate(xs):
            e = jnp.exp(z - m_new)
            t = t + e
            g_ = g_ + e * z
            p = p + jnp.where(aim == g * LANES, z, 0.0)
        m_acc[span, :] = m_new
        t_acc[span, :] = t
        g_acc[span, :] = g_
        p_acc[span, :] = p

    def relay(d):
        hcopy(d).wait_recv()
        fcopy(d, own_half).start()

    head = min(2, n)
    first_pieces()

    @pl.loop(1, head)
    def _(i):
        first_dot(i)

    normalize()

    @pl.loop(1, V)
    def _(d):
        rmscopy(d, v).start()

    turns = min(n - head, V - 2)

    @pl.loop(0, turns)
    def _(i):
        first_dot(head + i)
        relay(V - 1 - i)

    @pl.loop(head + turns, n)
    def _(i):
        first_dot(i)

    @pl.loop(1 + turns, V)
    def _(d):
        relay(V - d)

    landed(msq_all.at[0 : V - 1], r_recv)
    landed(raw.at[pl.ds(rows, late), mate_half], f_recv)

    @pl.loop(1, V)
    def _(d):
        scale = lax.rsqrt(to_column(msq_all[vsource(d)], rows) + epsilon)
        for g in range(2 * groups):
            column = slice(g * LANES, (g + 1) * LANES)
            gain_row = gains[pl.ds((w - lo) * groups + g, 1), :]
            nrm[slot(d), column] = (
                raw[slot(d), column].astype(jnp.float32) * scale * gain_row
            ).astype(jnp.bfloat16)

    @pl.loop(0, DEPTH)
    def _(i):
        send_dot(i)
        ystart(i)

    @pl.loop(0, n)
    def _(k):
        wremote(n + k, True).start()
        wlocal(n + k, True).start()

    landed(ints_all.at[0 : WIDTH - 1], i_recv)

    for q in range(WIDTH):
        columns = [
            jnp.broadcast_to(to_column(ints_all[q, k : k + 1, :].astype(jnp.float32), bw), (bw, LANES))
            for k in range(2)
        ]
        pick_lane = lax.broadcasted_iota(jnp.int32, (bw, LANES), 1)
        ints_cols[q * bw : (q + 1) * bw, :] = jnp.where(
            pick_lane == 0, columns[0], columns[1]
        ).astype(jnp.int32)

    r_row = lax.broadcasted_iota(jnp.int32, (1, LANES), 1)
    ends = jnp.zeros((1, LANES), jnp.int32)
    counts = jnp.ones((1, LANES), jnp.int32)
    for r in range(reqs):
        ends = ends + jnp.where(r_row >= REQ_LANE + r, lens_ref[r], 0)
        counts = jnp.where(r_row == REQ_LANE + r, lens_ref[r], counts)
    asked = (r_row >= REQ_LANE) & (r_row < REQ_LANE + reqs)
    starts = jnp.where(asked, ends - counts, tokens).astype(jnp.float32)
    ends = ends.astype(jnp.float32)
    counts = counts.astype(jnp.float32)
    place = ints_cols[:, 1:2].astype(jnp.float32)
    spot = jnp.where(r_row < rows, v * rows + r_row, tokens).astype(jnp.float32)
    member = (place >= starts) & (place < ends)
    pick[...] = jnp.where(member | (place == spot), 1.0, 0.0)
    rms = jnp.concatenate(
        [to_column(jnp.sqrt(msq_all[q] + epsilon), rows) for q in range(V)], axis=0
    )
    fixed[0:1, :] = counts
    fixed[1:2, :] = jnp.sum(jnp.where(member, rms, 0.0), axis=0, keepdims=True) / counts
    st1[w, :, pl.ds(tokens, LANES)] = jnp.zeros((4, LANES), jnp.float32)

    landed(zfirst.at[1], zp_recv)
    zfull[0] = zfirst[1]

    @pl.loop(0, n - 1 - DEPTH)
    def _(i):
        keep_dot(i)
        send_dot(i + DEPTH)
        yarrive(i)
        ycopy(i).wait_recv()
        ystart(i + DEPTH)
        stats(i)

    def last_start():
        zcopy(2 * n - 1).start()

        @pl.loop(1, V)
        def _(d):
            yblock(d).start()

    keep_dot(n - 1 - DEPTH)
    send_dot(n - 1)
    yarrive(n - 1 - DEPTH)
    ycopy(n - 1 - DEPTH).wait_recv()
    last_start()
    stats(n - 1 - DEPTH)

    @pl.loop(n - DEPTH, n - 1)
    def _(i):
        keep_dot(i)
        yarrive(i)
        ycopy(i).wait_recv()
        stats(i)

    keep_dot(n - 1)
    yarrive(n - 1)
    block_stats(n - 1, 0)

    @pl.loop(1, V)
    def _(d):
        yblock(d).wait_recv()
        block_stats(n - 1, d)

    m = m_acc[...]
    top = jnp.max(m, axis=1, keepdims=True)
    share = jnp.exp(m - top)
    tot = jnp.sum(t_acc[...] * share, axis=1, keepdims=True)
    wei = jnp.sum(g_acc[...] * share, axis=1, keepdims=True)
    pic = jnp.sum(p_acc[...], axis=1, keepdims=True)
    lane = lax.broadcasted_iota(jnp.int32, (tokens, LANES), 1)
    table = jnp.where(
        lane == 0, top, jnp.where(lane == 1, tot, jnp.where(lane == 2, wei, pic))
    )
    st1[w, :, 0:tokens] = jnp.transpose(table)[0:4, :]
    inside = (pick[...] > 0.5) & (lane >= REQ_LANE)
    st1[w, 0:1, pl.ds(tokens, LANES)] = jnp.max(
        jnp.where(inside, top, LOW), axis=0, keepdims=True
    )

    def acopy(d, dev):
        return rcopy(st1.at[w], st1.at[dev], a_send, a_recv, (v, wpeer(d)))

    def bcopy(d, dev):
        return rcopy(st2.at[v], st2.at[dev], b_send, b_recv, (vpeer(d), w))

    def joined(parts):
        top = functools.reduce(jnp.maximum, [s[0:1, :] for s in parts])
        tot = jnp.zeros_like(top)
        wei = jnp.zeros_like(top)
        pic = jnp.zeros_like(top)
        for s in parts:
            share = jnp.exp(s[0:1, :] - top)
            tot = tot + s[1:2, :] * share
            wei = wei + s[2:3, :] * share
            pic = pic + s[3:4, :]
        return top, tot, wei, pic

    @pl.loop(1, WIDTH)
    def _(d):
        acopy(d, w).start()

    xcopy().wait_send()
    drained(sq_all.at[0 : WIDTH - 1], q_send)
    scopy(own_half).wait_send()
    drained(ints_all.at[0 : WIDTH - 1], i_send)
    drained(msq_all.at[0 : V - 1], r_send)
    drained(raw.at[pl.ds(rows, late), own_half], h_send)
    drained(raw.at[pl.ds(rows, late), own_half], f_send)
    drained(wbuf.at[:, own_half, :], w_send)
    drained(sbuf.at[:, pl.ds(rows, late), :], y_send)
    drained(sbuf.at[:, 0:rows, :], ya_send)
    drained(zsend.at[pl.ds(1, 2 * n - 1)], z_send)
    drained(zfirst.at[0], zp_send)
    landed(st1.at[0 : WIDTH - 1], a_recv)

    sub = lax.broadcasted_iota(jnp.int32, (4, tokens + LANES), 0)
    top, tot, wei, pic = joined([st1[q] for q in range(WIDTH)])
    st2[v] = jnp.where(sub == 0, top, jnp.where(sub == 1, tot, jnp.where(sub == 2, wei, pic)))

    @pl.loop(1, V)
    def _(d):
        bcopy(d, v).start()

    landed(st2.at[0 : V - 1], b_recv)

    top, tot, wei, pic = joined([st2[q] for q in range(V)])
    highest = top[:, tokens : tokens + LANES]
    largest, tot, wei, pic = [row[:, 0:tokens] for row in (top, tot, wei, pic)]
    log_total = jnp.log(tot)
    place = lax.broadcasted_iota(jnp.int32, (8, tokens), 0)
    spread = jnp.zeros((8, tokens), jnp.float32)
    for k, rest in enumerate(
        (pic - largest - log_total, largest + log_total - wei / tot)
    ):
        for part in range(3):
            upper = rest.astype(jnp.bfloat16).astype(jnp.float32)
            spread = jnp.where(place == 2 * part + k, upper, spread)
            rest = rest - upper
    dealt = jnp.dot(
        spread.astype(jnp.bfloat16),
        pick[...].astype(jnp.bfloat16),
        preferred_element_type=jnp.float32,
    )
    sums = dealt[0:2] + dealt[2:4] + dealt[4:6]
    out_ref[0:1, :] = sums[0:1]
    out_ref[4:6, :] = sums / fixed[0:1, :]
    out_ref[6:7, :] = fixed[1:2, :]
    out_ref[7:8, :] = highest
    drained(st1.at[0 : WIDTH - 1], a_send)
    drained(st2.at[0 : V - 1], b_send)


def finish(rows, reqs, res_ref, tok_ref, stat_ref):
    tok_ref[...] = res_ref[0:1, 0:rows]
    stat_ref[...] = res_ref[4:8, REQ_LANE : REQ_LANE + reqs]


def body(hidden, norm_gain, head_weight, lengths, deal, targets):
    rows, feats = hidden.shape
    V = lax.axis_size("vocab")
    tokens = rows * V
    slab = head_weight.shape[1]
    quarter = slab // WIDTH
    cn = next(c for c in (512, 256, 128) if quarter % c == 0)
    n = quarter // cn
    mb = next(c for c in (384, 256, 192, 128, 64, 48, 16) if tokens % c == 0)
    reqs = lengths.shape[0]
    bw = tokens // WIDTH

    gain = norm_gain.reshape(-1, LANES)
    bwp = -(-bw // LANES) * LANES
    late = tokens - rows
    mb_late = next(c for c in (336, 192, 144, 96, 48, 16) if late % c == 0)

    cfg = (V, rows, tokens, feats, slab, quarter, cn, n, mb, mb_late, reqs)
    f32, bf16 = jnp.float32, jnp.bfloat16
    dma = pltpu.SemaphoreType.DMA
    vmem = pl.BlockSpec(memory_space=pltpu.VMEM)
    smem = pl.BlockSpec(memory_space=pltpu.SMEM)
    hbm = pl.BlockSpec(memory_space=pltpu.HBM)
    res = pl.pallas_call(
        functools.partial(kernel, cfg),
        out_shape=jax.ShapeDtypeStruct((8, LANES), f32),
        in_specs=[hbm, hbm, smem, hbm, hbm, hbm],
        out_specs=vmem,
        scratch_shapes=[
            pltpu.VMEM((1, bw), jnp.int32),
            pltpu.VMEM((1, bw), jnp.int32),
            pltpu.VMEM((D // LANES, LANES), bf16),
            pltpu.VMEM((rows, feats), bf16),
            pltpu.VMEM((D // LANES, LANES), f32),
            pltpu.VMEM((WIDTH, 2, bwp), jnp.int32),
            pltpu.VMEM((tokens, LANES), jnp.int32),
            pltpu.VMEM((rows, feats), bf16),
            pltpu.VMEM((tokens, 2 * feats), bf16),
            pltpu.VMEM((2 * rows, 2 * feats), bf16),
            pltpu.VMEM((rows, LANES), f32),
            pltpu.VMEM((tokens, LANES), f32),
            pltpu.VMEM((WIDTH, 1, LANES), f32),
            pltpu.VMEM((V, 1, LANES), f32),
            pltpu.VMEM((tokens, 2 * feats), bf16),
            pltpu.VMEM((2 * n, 2 * feats, cn), bf16),
            pltpu.VMEM((n, tokens, cn), jnp.int16),
            pltpu.VMEM((n, tokens, cn), jnp.int16),
            pltpu.VMEM((tokens, cn), f32),
            pltpu.VMEM((tokens, cn), f32),
            pltpu.VMEM((2 * n, 1, LANES), f32),
            pltpu.VMEM((2 * n, 1, LANES), f32),
            pltpu.VMEM((2, cn // LANES, 1, LANES), f32),
            pltpu.VMEM((2 * n, cn // LANES, 1, LANES), f32),
            pltpu.VMEM((tokens, LANES), f32),
            pltpu.VMEM((tokens, LANES), f32),
            pltpu.VMEM((tokens, LANES), f32),
            pltpu.VMEM((tokens, LANES), f32),
            pltpu.VMEM((WIDTH, 4, tokens + LANES), f32),
            pltpu.VMEM((V, 4, tokens + LANES), f32),
            pltpu.VMEM((tokens, LANES), f32),
            pltpu.VMEM((8, LANES), f32),
            dma((14,)),
            dma((4,)),
            dma,
            dma,
            dma,
            dma((WIDTH,)),
            dma((V,)),
            dma,
            dma,
            dma((n,)),
            dma((n,)),
            dma((cn // LANES,)),
            dma((n,)),
            dma((V,)),
            dma((2 * n,)),
            dma,
            dma((n,)),
            dma,
            dma,
        ],
        compiler_params=pltpu.CompilerParams(
            collective_id=0, has_side_effects=True, vmem_limit_bytes=58 << 20
        ),
    )(targets[None], deal[None], lengths, gain, hidden, head_weight)
    tok, stat = pl.pallas_call(
        functools.partial(finish, rows, reqs),
        out_shape=(
            jax.ShapeDtypeStruct((1, rows), f32),
            jax.ShapeDtypeStruct((4, reqs), f32),
        ),
        in_specs=[vmem],
        out_specs=(vmem, vmem),
    )(res)
    return tok[0], stat


def solution(mesh):
    return jax.shard_map(
        body,
        mesh=mesh,
        in_specs=(P("vocab", "width"), P(), P("width", "vocab"), P(), P("width"), P("width")),
        out_specs=(P("vocab"), P()),
        check_vma=False,
    )
```

```python
import functools

import jax
import jax.numpy as jnp
from jax import lax
from jax.experimental import pallas as pl
from jax.experimental.pallas import tpu as pltpu
from jax.sharding import PartitionSpec as P

D = 2048
epsilon = 1e-06
LOW = -1e30
TINY = 1e-30
STEPS = 32767.0
DEPTH = 3
LANES = 128
REQ_LANE = 64
WIDTH = 4


def kernel(
    cfg,
    aim_hbm,
    deal_hbm,
    lens_hbm,
    gain_hbm,
    hid_hbm,
    w_ref,
    out_ref,
    lens_ref,
    aim_ref,
    deal_ref,
    gain_ref,
    hid_ref,
    gains,
    ints_all,
    ints_cols,
    mate_hid,
    raw,
    split_rows,
    chip_scale,
    ratio,
    sq_all,
    msq_all,
    nrm,
    wbuf,
    sbuf,
    rbuf,
    xbuf,
    ybuf,
    zsend,
    zrecv,
    wmate,
    sown,
    rown,
    zown_send,
    zown,
    own_ratio,
    m_acc,
    t_acc,
    g_acc,
    p_acc,
    st1,
    st2,
    pick,
    fixed,
    once_send,
    x_recv,
    s_recv,
    i_recv,
    q_recv,
    h_recv,
    f_recv,
    r_recv,
    wl_sem,
    w_recv,
    y_recv,
    z_recv,
    own_recv,
    ya_recv,
    za_recv,
    a_recv,
    b_recv,
):
    V, rows, tokens, feats, slab, quarter, cn, n, mb, mb_late, reqs = cfg
    v = lax.axis_index("vocab")
    w = lax.axis_index("width")
    lo = lax.rem(w, 2)
    hi = w // 2
    mate = w + 1 - 2 * lo
    far = w + 2 - 4 * hi
    bw = tokens // WIDTH
    x_send, i_send, q_send, h_send, f_send, r_send = [once_send.at[k] for k in range(6)]
    w_send, y_send, z_send, ya_send, a_send, b_send, s_send, own_send, zo_send = [
        once_send.at[k] for k in range(6, 15)
    ]

    def rcopy(src, dst, ss, rs, where):
        return pltpu.make_async_remote_copy(
            src_ref=src,
            dst_ref=dst,
            send_sem=ss,
            recv_sem=rs,
            device_id=where,
            device_id_type=pl.DeviceIdType.MESH,
        )

    def drained(ref, sem):
        rcopy(ref, ref, sem, x_recv, (v, mate)).wait_send()

    def landed(ref, sem):
        rcopy(ref, ref, x_send, sem, (v, mate)).wait_recv()

    def flipped(d):
        other, bit = 0, 1
        while bit < V:
            other = other + lax.rem(v // bit + d // bit, 2) * bit
            bit *= 2
        return other

    even = V & (V - 1) == 0

    def vpeer(d):
        return flipped(d) if even else lax.rem(v + d, V)

    def vsource(d):
        return flipped(d) if even else lax.rem(v + V - d, V)

    def wpeer(d):
        return lax.rem(w + d, WIDTH)

    def wsource(d):
        return lax.rem(w + WIDTH - d, WIDTH)

    def wcols(k, is_keep, dev):
        dev_far = dev + 2 - 4 * (dev // 2)
        q = dev if is_keep else dev_far
        base = k - n if is_keep else k
        return pl.ds(pl.multiple_of(q * quarter + base * cn, LANES), cn)

    own_half = pl.ds(pl.multiple_of(lo * feats, LANES), feats)
    mate_half = pl.ds(pl.multiple_of((1 - lo) * feats, LANES), feats)

    def wlocal(k, is_keep, sem):
        return pltpu.make_async_copy(
            w_ref.at[:, wcols(k, is_keep, w)], wbuf.at[k, own_half, :], wl_sem.at[sem]
        )

    def wloaded(part, sem):
        pltpu.make_async_copy(part, part, wl_sem.at[sem]).wait()

    def wremote(k, is_keep):
        return rcopy(
            w_ref.at[:, wcols(k, is_keep, mate)],
            wbuf.at[k, own_half, :],
            w_send,
            w_recv.at[lax.rem(k, n)],
            (v, mate),
        )

    def wwait(k, is_keep):
        rcopy(
            w_ref.at[:, wcols(k, is_keep, mate)],
            wbuf.at[k, mate_half, :],
            w_send,
            w_recv.at[lax.rem(k, n)],
            (v, mate),
        ).wait_recv()

    barrier = pltpu.get_barrier_semaphore()

    @pl.loop(1, WIDTH)
    def _(d):
        pl.semaphore_signal(
            barrier, inc=1, device_id=(v, wpeer(d)), device_id_type=pl.DeviceIdType.MESH
        )

    @pl.loop(1, V)
    def _(d):
        pl.semaphore_signal(
            barrier, inc=1, device_id=(vpeer(d), w), device_id_type=pl.DeviceIdType.MESH
        )

    loads = [
        pltpu.make_async_copy(source, there, once_send.at[k])
        for k, (source, there) in enumerate(
            (
                (hid_hbm, hid_ref),
                (gain_hbm, gain_ref),
                (aim_hbm, aim_ref),
                (deal_hbm, deal_ref),
                (lens_hbm, lens_ref),
            )
        )
    ]
    for load in loads:
        load.start()

    mate_first = pltpu.make_async_copy(w_ref.at[:, wcols(0, False, mate)], wmate, wl_sem.at[3])
    wlocal(0, False, 0).start()
    mate_first.start()

    @pl.loop(1, n)
    def _(k):
        wlocal(k, False, 1).start()

    late = tokens - rows
    groups = feats // LANES
    ratio[pl.ds(rows, late), :] = jnp.ones((late, LANES), jnp.float32)
    m_acc[...] = jnp.full((tokens, LANES), LOW, jnp.float32)
    t_acc[...] = jnp.zeros((tokens, LANES), jnp.float32)
    g_acc[...] = jnp.zeros((tokens, LANES), jnp.float32)
    p_acc[...] = jnp.zeros((tokens, LANES), jnp.float32)

    def slot(d):
        return pl.ds(pl.multiple_of(d * rows, 16), rows)

    def hcopy(d):
        return rcopy(hid_ref, raw.at[slot(d), own_half], h_send, h_recv.at[d], (vpeer(d), w))

    def squares(x):
        return jnp.sum(x * x, axis=1, keepdims=True)

    def to_row(column, wide):
        height = column.shape[0]
        there = lax.broadcasted_iota(jnp.int32, (height, wide), 1)
        here = lax.broadcasted_iota(jnp.int32, (height, wide), 0)
        return jnp.sum(jnp.where(there == here, column, 0.0), axis=0, keepdims=True)

    def to_column(row, height):
        wide = row.shape[1]
        there = lax.broadcasted_iota(jnp.int32, (height, wide), 1)
        here = lax.broadcasted_iota(jnp.int32, (height, wide), 0)
        return jnp.sum(jnp.where(there == here, row, 0.0), axis=1, keepdims=True)

    for load in loads:
        load.wait()
    gains[...] = gain_ref[...].astype(jnp.float32)
    x = hid_ref[...].astype(jnp.float32)
    sq = squares(x)
    sq_all[w] = to_row(sq, LANES)
    for g in range(groups):
        column = pl.ds(pl.multiple_of(lo * feats + g * LANES, LANES), LANES)
        scaled = x[:, g * LANES : (g + 1) * LANES] * gains[pl.ds(w * groups + g, 1), :]
        upper = scaled.astype(jnp.bfloat16)
        split_rows[0:rows, column] = upper
        split_rows[rows : 2 * rows, column] = (scaled - upper.astype(jnp.float32)).astype(
            jnp.bfloat16
        )
    ints_all[w] = jnp.zeros(ints_all.shape[1:], jnp.int32)
    ints_all[w, 0:1, 0:bw] = aim_ref[...]
    ints_all[w, 1:2, 0:bw] = deal_ref[...]
    def lanes_peak(z):
        peak = jnp.max(jnp.abs(z), axis=0, keepdims=True)
        parts = [peak[:, g * LANES : (g + 1) * LANES] for g in range(cn // LANES)]
        return functools.reduce(jnp.maximum, parts)

    def quantized(z, rate):
        for g in range(cn // LANES):
            part = slice(g * LANES, (g + 1) * LANES)
            yield part, jnp.round(z[:, part] * rate).astype(jnp.int32).astype(jnp.int16)

    def folded(both, scale):
        return (both[0:rows] + both[rows : 2 * rows]) * scale

    core_scale = lax.rsqrt(sq * (1.0 / feats) + epsilon)
    wlocal(0, False, 0).wait()
    mate_first.wait()
    for k, weights in enumerate((wbuf[0, own_half, :], wmate[...])):
        z = folded(
            jnp.dot(split_rows[:, own_half], weights, preferred_element_type=jnp.float32),
            core_scale,
        )
        peak = jnp.maximum(TINY, lanes_peak(z))
        zown_send[k] = peak * (1.0 / STEPS)
        for part, value in quantized(z, STEPS / peak):
            sown[k, :, part] = value
    pl.semaphore_wait(barrier, WIDTH - 1 + V - 1)

    def xcopy():
        return rcopy(hid_ref, mate_hid, x_send, x_recv, (v, mate))

    def icopy(d, dev):
        return rcopy(ints_all.at[w], ints_all.at[dev], i_send, i_recv, (v, wpeer(d)))

    across = far + 1 - 2 * lo

    def scopy(half):
        return rcopy(
            split_rows.at[:, half], split_rows.at[:, half], s_send, s_recv, (v, mate)
        )

    def qstart(there, sem):
        rcopy(sq_all.at[w], sq_all.at[w], q_send, q_recv.at[sem], (v, there)).start()

    def owncopy(k, there):
        return rcopy(sown.at[k], rown.at[lo], own_send, own_recv.at[0], (v, there))

    def zocopy(k, there):
        return rcopy(zown_send.at[k], zown.at[lo], zo_send, own_recv.at[1], (v, there))

    for k, there in enumerate((far, across)):
        owncopy(k, there).start()
        zocopy(k, there).start()
    scopy(own_half).start()
    qstart(mate, 0)
    wremote(1, False).start()
    qstart(far, 1)
    qstart(across, 1)

    @pl.loop(2, DEPTH)
    def _(k):
        wremote(k, False).start()

    xcopy().start()

    @pl.loop(1, V)
    def _(d):
        hcopy(V - d).start()

    @pl.loop(DEPTH, n)
    def _(k):
        wremote(k, False).start()

    wremote(0, False).start()

    @pl.loop(1, WIDTH)
    def _(d):
        icopy(d, w).start()

    landed(sq_all.at[mate], q_recv.at[0])
    chip_sq = sq + to_column(sq_all[mate], rows)
    chip_scale[...] = jnp.broadcast_to(
        lax.rsqrt(chip_sq * (1.0 / (2 * feats)) + epsilon), (rows, LANES)
    )
    scopy(mate_half).wait_recv()

    def vspan(dev):
        return pl.ds(pl.multiple_of(dev * rows, 16), rows)

    def normalize():
        landed(sq_all.at[0:2], q_recv.at[1])
        xcopy().wait_recv()
        total_sq = sq_all[0] + sq_all[1] + sq_all[2] + sq_all[3]
        mean_row = total_sq * (1.0 / D)
        msq_all[v] = mean_row
        mean_sq = to_column(mean_row, rows)
        scale = lax.rsqrt(mean_sq + epsilon)
        far_sq = to_column(sq_all[far] + sq_all[across], rows)
        far_scale = lax.rsqrt(far_sq * (1.0 / (2 * feats)) + epsilon)
        ratio[0:rows, :] = jnp.broadcast_to(scale / far_scale, (rows, LANES))
        for core, dev in ((lo, far), (1 - lo, across)):
            dev_sq = to_column(sq_all[dev], rows)
            dev_scale = lax.rsqrt(dev_sq * (1.0 / feats) + epsilon)
            own_ratio[core] = jnp.broadcast_to(scale / dev_scale, (rows, LANES))
        for half, dev, source in ((lo, w, hid_ref), (1 - lo, mate, mate_hid)):
            for g in range(groups):
                column = pl.ds(pl.multiple_of(half * feats + g * LANES, LANES), LANES)
                value = source[:, g * LANES : (g + 1) * LANES].astype(jnp.float32)
                nrm[0:rows, column] = (
                    value * scale * gains[pl.ds(dev * groups + g, 1), :]
                ).astype(jnp.bfloat16)

    def fcopy(d, half):
        part = raw.at[slot(d), half]
        return rcopy(part, part, f_send, f_recv, (v, mate))

    def rmscopy(d, dev):
        return rcopy(msq_all.at[v], msq_all.at[dev], r_send, r_recv, (vpeer(d), w))

    def ycopy(i):
        part = pl.ds(rows, late)
        return rcopy(
            sbuf.at[i, part, :], rbuf.at[i, part, :], y_send, y_recv.at[i], (v, far)
        )

    def yacopy(i):
        part = pl.ds(0, rows)
        return rcopy(
            sbuf.at[i, part, :], rbuf.at[i, part, :], ya_send, ya_recv, (v, far)
        )

    def zcopy(k):
        return rcopy(zsend.at[k], zrecv.at[k], z_send, z_recv.at[k - n], (v, far))

    def zacopy(k):
        return rcopy(zsend.at[k], zrecv.at[k], z_send, za_recv, (v, far))

    def yblock(d):
        return rcopy(
            sbuf.at[n - 1, slot(d), :], rbuf.at[n - 1, slot(d), :], y_send, h_recv.at[d], (v, far)
        )

    def ystart(i):
        zcopy(n + i).start()
        ycopy(i).start()

    def yarrive(i):
        zcopy(n + i).wait_recv()

    def quantize(i, span, rate, z):
        for part, value in quantized(z, rate):
            sbuf[i, span, part] = value

    def first_dot(i):
        wwait(i, False)
        z = folded(
            jnp.dot(split_rows[...], wbuf[i], preferred_element_type=jnp.float32),
            chip_scale[:, 0:1],
        )
        peak = jnp.maximum(TINY, lanes_peak(z))
        zsend[i] = peak * (1.0 / STEPS)
        quantize(i, pl.ds(0, rows), STEPS / peak, z)
        zacopy(i).start()
        yacopy(i).start()

    def add_own():
        for core in range(2):
            scale = own_ratio[core] * zown[core]
            for g in range(cn // LANES):
                part = slice(g * LANES, (g + 1) * LANES)
                xbuf[0:rows, part] += rown[core, :, part].astype(jnp.int32).astype(jnp.float32) * scale

    def send_dot(i):
        def multiply(r, peak):
            span = pl.ds(pl.multiple_of(rows + r * mb_late, 16), mb_late)
            z = jnp.dot(nrm[span, :], wbuf[i], preferred_element_type=jnp.float32)
            ybuf[span, :] = z
            return jnp.maximum(peak, lanes_peak(z))

        peak = lax.fori_loop(
            0, late // mb_late, multiply, jnp.full((1, LANES), TINY, jnp.float32)
        )
        zsend[n + i] = peak * (1.0 / STEPS)
        rate = STEPS / peak

        @pl.loop(1, V)
        def _(r):
            quantize(i, slot(r), rate, ybuf[slot(r), :])

    def keep_dot(i):
        wwait(n + i, True)

        @pl.loop(0, tokens // mb)
        def _(r):
            span = pl.ds(pl.multiple_of(r * mb, 16), mb)
            xbuf[span, :] = jnp.dot(
                nrm[span, :], wbuf[n + i], preferred_element_type=jnp.float32
            )

    rb = rows
    first_column = v * slab + w * quarter

    def stats(i):
        @pl.loop(0, V)
        def _(r):
            block_stats(i, r)

    def block_stats(i, r):
        held = slot(r)
        span = vspan(vsource(r))
        late_z = n * ((r + V - 1) // V) + i
        target = ints_cols[span, 0:1]
        factor = zrecv[late_z] * ratio[held, :]
        lane = lax.broadcasted_iota(jnp.int32, (rb, LANES), 1)
        aim = jnp.broadcast_to(target, (rb, LANES)) - lane - (first_column + i * cn)
        xs = [
            xbuf[held, g * LANES : (g + 1) * LANES]
            + rbuf[i, held, g * LANES : (g + 1) * LANES].astype(jnp.int32).astype(jnp.float32)
            * factor
            for g in range(cn // LANES)
        ]
        m_old = m_acc[span, :]
        m_new = functools.reduce(jnp.maximum, xs, m_old)
        decay = jnp.exp(m_old - m_new)
        t = t_acc[span, :] * decay
        g_ = g_acc[span, :] * decay
        p = p_acc[span, :]
        for g, z in enumerate(xs):
            e = jnp.exp(z - m_new)
            t = t + e
            g_ = g_ + e * z
            p = p + jnp.where(aim == g * LANES, z, 0.0)
        m_acc[span, :] = m_new
        t_acc[span, :] = t
        g_acc[span, :] = g_
        p_acc[span, :] = p

    def relay(d):
        hcopy(d).wait_recv()
        fcopy(d, own_half).start()

    head = min(3, n)
    wloaded(wbuf.at[1:n, own_half, :], 1)

    @pl.loop(1, head)
    def _(i):
        first_dot(i)

    normalize()

    @pl.loop(1, V)
    def _(d):
        rmscopy(d, v).start()

    turns = min(n - head, V - 2)

    @pl.loop(0, turns)
    def _(i):
        first_dot(head + i)
        relay(V - 1 - i)

    @pl.loop(head + turns, n)
    def _(i):
        first_dot(i)

    wwait(0, False)

    @pl.loop(1 + turns, V)
    def _(d):
        relay(V - d)

    landed(msq_all.at[0 : V - 1], r_recv)
    landed(raw.at[pl.ds(rows, late), mate_half], f_recv)

    @pl.loop(1, V)
    def _(d):
        scale = lax.rsqrt(to_column(msq_all[vsource(d)], rows) + epsilon)
        for g in range(2 * groups):
            column = slice(g * LANES, (g + 1) * LANES)
            gain_row = gains[pl.ds((w - lo) * groups + g, 1), :]
            nrm[slot(d), column] = (
                raw[slot(d), column].astype(jnp.float32) * scale * gain_row
            ).astype(jnp.bfloat16)

    @pl.loop(0, DEPTH)
    def _(i):
        send_dot(i)
        ystart(i)

    @pl.loop(0, n)
    def _(k):
        wremote(n + k, True).start()
        wlocal(n + k, True, 2).start()

    landed(ints_all.at[0 : WIDTH - 1], i_recv)

    for q in range(WIDTH):
        columns = [
            jnp.broadcast_to(to_column(ints_all[q, k : k + 1, :].astype(jnp.float32), bw), (bw, LANES))
            for k in range(2)
        ]
        pick_lane = lax.broadcasted_iota(jnp.int32, (bw, LANES), 1)
        ints_cols[q * bw : (q + 1) * bw, :] = jnp.where(
            pick_lane == 0, columns[0], columns[1]
        ).astype(jnp.int32)

    r_row = lax.broadcasted_iota(jnp.int32, (1, LANES), 1)
    ends = jnp.zeros((1, LANES), jnp.int32)
    counts = jnp.ones((1, LANES), jnp.int32)
    for r in range(reqs):
        ends = ends + jnp.where(r_row >= REQ_LANE + r, lens_ref[r], 0)
        counts = jnp.where(r_row == REQ_LANE + r, lens_ref[r], counts)
    asked = (r_row >= REQ_LANE) & (r_row < REQ_LANE + reqs)
    starts = jnp.where(asked, ends - counts, tokens).astype(jnp.float32)
    ends = ends.astype(jnp.float32)
    counts = counts.astype(jnp.float32)
    place = ints_cols[:, 1:2].astype(jnp.float32)
    spot = jnp.where(r_row < rows, v * rows + r_row, tokens).astype(jnp.float32)
    member = (place >= starts) & (place < ends)
    pick[...] = jnp.where(member | (place == spot), 1.0, 0.0)
    rms = jnp.concatenate(
        [to_column(jnp.sqrt(msq_all[q] + epsilon), rows) for q in range(V)], axis=0
    )
    fixed[0:1, :] = counts
    fixed[1:2, :] = jnp.sum(jnp.where(member, rms, 0.0), axis=0, keepdims=True) / counts
    st1[w, :, pl.ds(tokens, LANES)] = jnp.zeros((4, LANES), jnp.float32)

    wloaded(wbuf.at[n : 2 * n, own_half, :], 2)
    landed(rbuf.at[1:n, 0:rows, :], ya_recv)
    landed(zrecv.at[1:n], za_recv)
    landed(rown, own_recv.at[0])
    landed(zown, own_recv.at[1])
    rbuf[0, 0:rows, :] = jnp.zeros((rows, cn), jnp.int16)
    zrecv[0] = jnp.zeros((1, LANES), jnp.float32)

    @pl.loop(0, n - 1 - DEPTH)
    def _(i):
        keep_dot(i)

        @pl.when(i == 0)
        def _():
            add_own()

        send_dot(i + DEPTH)
        yarrive(i)
        ycopy(i).wait_recv()
        ystart(i + DEPTH)
        stats(i)

    def last_start():
        zcopy(2 * n - 1).start()

        @pl.loop(1, V)
        def _(d):
            yblock(d).start()

    keep_dot(n - 1 - DEPTH)
    send_dot(n - 1)
    yarrive(n - 1 - DEPTH)
    ycopy(n - 1 - DEPTH).wait_recv()
    last_start()
    stats(n - 1 - DEPTH)

    @pl.loop(n - DEPTH, n - 1)
    def _(i):
        keep_dot(i)
        yarrive(i)
        ycopy(i).wait_recv()
        stats(i)

    keep_dot(n - 1)
    yarrive(n - 1)
    block_stats(n - 1, 0)

    @pl.loop(1, V)
    def _(d):
        yblock(d).wait_recv()
        block_stats(n - 1, d)

    m = m_acc[...]
    top = jnp.max(m, axis=1, keepdims=True)
    share = jnp.exp(m - top)
    tot = jnp.sum(t_acc[...] * share, axis=1, keepdims=True)
    wei = jnp.sum(g_acc[...] * share, axis=1, keepdims=True)
    pic = jnp.sum(p_acc[...], axis=1, keepdims=True)
    lane = lax.broadcasted_iota(jnp.int32, (tokens, LANES), 1)
    table = jnp.where(
        lane == 0, top, jnp.where(lane == 1, tot, jnp.where(lane == 2, wei, pic))
    )
    st1[w, :, 0:tokens] = jnp.transpose(table)[0:4, :]
    inside = (pick[...] > 0.5) & (lane >= REQ_LANE)
    st1[w, 0:1, pl.ds(tokens, LANES)] = jnp.max(
        jnp.where(inside, top, LOW), axis=0, keepdims=True
    )

    def acopy(d, dev):
        return rcopy(st1.at[w], st1.at[dev], a_send, a_recv, (v, wpeer(d)))

    def bcopy(d, dev):
        return rcopy(st2.at[v], st2.at[dev], b_send, b_recv, (vpeer(d), w))

    def joined(parts):
        top = functools.reduce(jnp.maximum, [s[0:1, :] for s in parts])
        tot = jnp.zeros_like(top)
        wei = jnp.zeros_like(top)
        pic = jnp.zeros_like(top)
        for s in parts:
            share = jnp.exp(s[0:1, :] - top)
            tot = tot + s[1:2, :] * share
            wei = wei + s[2:3, :] * share
            pic = pic + s[3:4, :]
        return top, tot, wei, pic

    @pl.loop(1, WIDTH)
    def _(d):
        acopy(d, w).start()

    xcopy().wait_send()
    drained(sq_all.at[0 : WIDTH - 1], q_send)
    scopy(own_half).wait_send()
    drained(ints_all.at[0 : WIDTH - 1], i_send)
    drained(msq_all.at[0 : V - 1], r_send)
    drained(raw.at[pl.ds(rows, late), own_half], h_send)
    drained(raw.at[pl.ds(rows, late), own_half], f_send)
    drained(wbuf.at[:, own_half, :], w_send)
    drained(sbuf.at[:, pl.ds(rows, late), :], y_send)
    drained(sbuf.at[1:n, 0:rows, :], ya_send)
    drained(zsend.at[pl.ds(1, 2 * n - 1)], z_send)
    drained(sown, own_send)
    drained(zown_send, zo_send)
    landed(st1.at[0 : WIDTH - 1], a_recv)

    sub = lax.broadcasted_iota(jnp.int32, (4, tokens + LANES), 0)
    top, tot, wei, pic = joined([st1[q] for q in range(WIDTH)])
    st2[v] = jnp.where(sub == 0, top, jnp.where(sub == 1, tot, jnp.where(sub == 2, wei, pic)))

    @pl.loop(1, V)
    def _(d):
        bcopy(d, v).start()

    landed(st2.at[0 : V - 1], b_recv)

    top, tot, wei, pic = joined([st2[q] for q in range(V)])
    highest = top[:, tokens : tokens + LANES]
    largest, tot, wei, pic = [row[:, 0:tokens] for row in (top, tot, wei, pic)]
    log_total = jnp.log(tot)
    place = lax.broadcasted_iota(jnp.int32, (8, tokens), 0)
    spread = jnp.zeros((8, tokens), jnp.float32)
    for k, rest in enumerate(
        (pic - largest - log_total, largest + log_total - wei / tot)
    ):
        for part in range(3):
            upper = rest.astype(jnp.bfloat16).astype(jnp.float32)
            spread = jnp.where(place == 2 * part + k, upper, spread)
            rest = rest - upper
    dealt = jnp.dot(
        spread.astype(jnp.bfloat16),
        pick[...].astype(jnp.bfloat16),
        preferred_element_type=jnp.float32,
    )
    sums = dealt[0:2] + dealt[2:4] + dealt[4:6]
    out_ref[0:1, :] = sums[0:1]
    out_ref[4:6, :] = sums / fixed[0:1, :]
    out_ref[6:7, :] = fixed[1:2, :]
    out_ref[7:8, :] = highest
    drained(st1.at[0 : WIDTH - 1], a_send)
    drained(st2.at[0 : V - 1], b_send)


def finish(rows, reqs, res_ref, tok_ref, stat_ref):
    tok_ref[...] = res_ref[0:1, 0:rows]
    stat_ref[...] = res_ref[4:8, REQ_LANE : REQ_LANE + reqs]


def body(hidden, norm_gain, head_weight, lengths, deal, targets):
    rows, feats = hidden.shape
    V = lax.axis_size("vocab")
    tokens = rows * V
    slab = head_weight.shape[1]
    quarter = slab // WIDTH
    cn = next(c for c in (512, 256, 128) if quarter % c == 0)
    n = quarter // cn
    mb = next(c for c in (384, 256, 192, 128, 64, 48, 16) if tokens % c == 0)
    reqs = lengths.shape[0]
    bw = tokens // WIDTH

    gain = norm_gain.reshape(-1, LANES)
    bwp = -(-bw // LANES) * LANES
    late = tokens - rows
    mb_late = next(c for c in (336, 192, 144, 96, 48, 16) if late % c == 0)

    cfg = (V, rows, tokens, feats, slab, quarter, cn, n, mb, mb_late, reqs)
    f32, bf16 = jnp.float32, jnp.bfloat16
    dma = pltpu.SemaphoreType.DMA
    vmem = pl.BlockSpec(memory_space=pltpu.VMEM)
    hbm = pl.BlockSpec(memory_space=pltpu.HBM)
    res = pl.pallas_call(
        functools.partial(kernel, cfg),
        out_shape=jax.ShapeDtypeStruct((8, LANES), f32),
        in_specs=[hbm] * 6,
        out_specs=vmem,
        scratch_shapes=[
            pltpu.SMEM((reqs,), jnp.int32),
            pltpu.VMEM((1, bw), jnp.int32),
            pltpu.VMEM((1, bw), jnp.int32),
            pltpu.VMEM((D // LANES, LANES), bf16),
            pltpu.VMEM((rows, feats), bf16),
            pltpu.VMEM((D // LANES, LANES), f32),
            pltpu.VMEM((WIDTH, 2, bwp), jnp.int32),
            pltpu.VMEM((tokens, LANES), jnp.int32),
            pltpu.VMEM((rows, feats), bf16),
            pltpu.VMEM((tokens, 2 * feats), bf16),
            pltpu.VMEM((2 * rows, 2 * feats), bf16),
            pltpu.VMEM((rows, LANES), f32),
            pltpu.VMEM((tokens, LANES), f32),
            pltpu.VMEM((WIDTH, 1, LANES), f32),
            pltpu.VMEM((V, 1, LANES), f32),
            pltpu.VMEM((tokens, 2 * feats), bf16),
            pltpu.VMEM((2 * n, 2 * feats, cn), bf16),
            pltpu.VMEM((n, tokens, cn), jnp.int16),
            pltpu.VMEM((n, tokens, cn), jnp.int16),
            pltpu.VMEM((tokens, cn), f32),
            pltpu.VMEM((tokens, cn), f32),
            pltpu.VMEM((2 * n, 1, LANES), f32),
            pltpu.VMEM((2 * n, 1, LANES), f32),
            pltpu.VMEM((feats, cn), bf16),
            pltpu.VMEM((2, rows, cn), jnp.int16),
            pltpu.VMEM((2, rows, cn), jnp.int16),
            pltpu.VMEM((2, 1, LANES), f32),
            pltpu.VMEM((2, 1, LANES), f32),
            pltpu.VMEM((2, rows, LANES), f32),
            pltpu.VMEM((tokens, LANES), f32),
            pltpu.VMEM((tokens, LANES), f32),
            pltpu.VMEM((tokens, LANES), f32),
            pltpu.VMEM((tokens, LANES), f32),
            pltpu.VMEM((WIDTH, 4, tokens + LANES), f32),
            pltpu.VMEM((V, 4, tokens + LANES), f32),
            pltpu.VMEM((tokens, LANES), f32),
            pltpu.VMEM((8, LANES), f32),
            dma((15,)),
            dma,
            dma,
            dma,
            dma((2,)),
            dma((V,)),
            dma,
            dma,
            dma((4,)),
            dma((n,)),
            dma((n,)),
            dma((n,)),
            dma((2,)),
            dma,
            dma,
            dma,
            dma,
        ],
        compiler_params=pltpu.CompilerParams(
            collective_id=0, has_side_effects=True, vmem_limit_bytes=58 << 20
        ),
    )(targets[None], deal[None], lengths, gain, hidden, head_weight)
    tok, stat = pl.pallas_call(
        functools.partial(finish, rows, reqs),
        out_shape=(
            jax.ShapeDtypeStruct((1, rows), f32),
            jax.ShapeDtypeStruct((4, reqs), f32),
        ),
        in_specs=[vmem],
        out_specs=(vmem, vmem),
    )(res)
    return tok[0], stat


def solution(mesh):
    return jax.shard_map(
        body,
        mesh=mesh,
        in_specs=(P("vocab", "width"), P(), P("width", "vocab"), P(), P("width"), P("width")),
        out_specs=(P("vocab"), P()),
        check_vma=False,
    )
```

```python
import functools

import jax
import jax.numpy as jnp
from jax import lax
from jax.experimental import pallas as pl
from jax.experimental.pallas import tpu as pltpu
from jax.sharding import PartitionSpec as P

D = 2048
epsilon = 1e-06
LOW = -1e30
TINY = 1e-30
STEPS = 32767.0
DEPTH = 3
LAST = 3
END = 2
LANES = 128
REQ_LANE = 64
WIDTH = 4


def kernel(
    cfg,
    aim_hbm,
    deal_hbm,
    lens_hbm,
    gain_hbm,
    hid_hbm,
    w_ref,
    out_ref,
    lens_ref,
    aim_ref,
    deal_ref,
    gain_ref,
    hid_ref,
    gains,
    ints_all,
    ints_cols,
    mate_hid,
    raw,
    split_rows,
    chip_scale,
    ratio,
    sq_all,
    msq_all,
    nrm,
    wbuf,
    sbuf,
    rbuf,
    xbuf,
    ybuf,
    zsend,
    zrecv,
    wmate,
    sown,
    rown,
    zown_send,
    zown,
    own_ratio,
    m_acc,
    t_acc,
    g_acc,
    p_acc,
    st1,
    st2,
    fin,
    pick,
    asked_rows,
    fixed,
    once_send,
    x_recv,
    s_recv,
    i_recv,
    q_recv,
    h_recv,
    f_recv,
    r_recv,
    wl_sem,
    w_recv,
    y_recv,
    z_recv,
    own_recv,
    ya_recv,
    za_recv,
    a_recv,
    b_recv,
    c_recv,
    last_recv,
):
    V, rows, tokens, feats, slab, quarter, cn, n, mb, mb_late, reqs = cfg
    v = lax.axis_index("vocab")
    w = lax.axis_index("width")
    lo = lax.rem(w, 2)
    hi = w // 2
    mate = w + 1 - 2 * lo
    far = w + 2 - 4 * hi
    bw = tokens // WIDTH
    x_send, i_send, q_send, h_send, f_send, r_send = [once_send.at[k] for k in range(6)]
    w_send, y_send, z_send, ya_send, a_send, b_send, s_send, own_send, zo_send, c_send = [
        once_send.at[k] for k in range(6, 16)
    ]
    plain = n - LAST
    depth = min(DEPTH, plain)
    pair = END * rows
    pairs = V // END
    last_pair = pairs - 1 - v // END

    def rcopy(src, dst, ss, rs, where):
        return pltpu.make_async_remote_copy(
            src_ref=src,
            dst_ref=dst,
            send_sem=ss,
            recv_sem=rs,
            device_id=where,
            device_id_type=pl.DeviceIdType.MESH,
        )

    def drained(ref, sem):
        rcopy(ref, ref, sem, x_recv, (v, mate)).wait_send()

    def landed(ref, sem):
        rcopy(ref, ref, x_send, sem, (v, mate)).wait_recv()

    def flipped(d):
        other, bit = 0, 1
        while bit < V:
            other = other + lax.rem(v // bit + d // bit, 2) * bit
            bit *= 2
        return other

    def vpeer(d):
        return flipped(d)

    def vsource(d):
        return flipped(d)

    def wpeer(d):
        return lax.rem(w + d, WIDTH)

    def wsource(d):
        return lax.rem(w + WIDTH - d, WIDTH)

    def wcols(k, is_keep, dev):
        dev_far = dev + 2 - 4 * (dev // 2)
        q = dev if is_keep else dev_far
        base = k - n if is_keep else k
        return pl.ds(pl.multiple_of(q * quarter + base * cn, LANES), cn)

    own_half = pl.ds(pl.multiple_of(lo * feats, LANES), feats)
    mate_half = pl.ds(pl.multiple_of((1 - lo) * feats, LANES), feats)

    def wlocal(k, is_keep, sem):
        return pltpu.make_async_copy(
            w_ref.at[:, wcols(k, is_keep, w)], wbuf.at[k, own_half, :], wl_sem.at[sem]
        )

    def wloaded(part, sem):
        pltpu.make_async_copy(part, part, wl_sem.at[sem]).wait()

    def wremote(k, is_keep):
        return rcopy(
            w_ref.at[:, wcols(k, is_keep, mate)],
            wbuf.at[k, own_half, :],
            w_send,
            w_recv.at[lax.rem(k, n)],
            (v, mate),
        )

    def wwait(k, is_keep):
        rcopy(
            w_ref.at[:, wcols(k, is_keep, mate)],
            wbuf.at[k, mate_half, :],
            w_send,
            w_recv.at[lax.rem(k, n)],
            (v, mate),
        ).wait_recv()

    barrier = pltpu.get_barrier_semaphore()

    @pl.loop(1, WIDTH)
    def _(d):
        pl.semaphore_signal(
            barrier, inc=1, device_id=(v, wpeer(d)), device_id_type=pl.DeviceIdType.MESH
        )

    @pl.loop(1, V)
    def _(d):
        pl.semaphore_signal(
            barrier, inc=1, device_id=(vpeer(d), w), device_id_type=pl.DeviceIdType.MESH
        )

    loads = [
        pltpu.make_async_copy(source, there, once_send.at[k])
        for k, (source, there) in enumerate(
            (
                (hid_hbm, hid_ref),
                (gain_hbm, gain_ref),
                (aim_hbm, aim_ref),
                (deal_hbm, deal_ref),
                (lens_hbm, lens_ref),
            )
        )
    ]
    for load in loads:
        load.start()

    mate_first = pltpu.make_async_copy(w_ref.at[:, wcols(0, False, mate)], wmate, wl_sem.at[3])
    wlocal(0, False, 0).start()
    mate_first.start()

    @pl.loop(1, n)
    def _(k):
        wlocal(k, False, 1).start()

    late = tokens - rows
    groups = feats // LANES
    ratio[pl.ds(rows, late), :] = jnp.ones((late, LANES), jnp.float32)
    m_acc[...] = jnp.full((tokens, LANES), LOW, jnp.float32)
    t_acc[...] = jnp.zeros((tokens, LANES), jnp.float32)
    g_acc[...] = jnp.zeros((tokens, LANES), jnp.float32)
    p_acc[...] = jnp.zeros((tokens, LANES), jnp.float32)

    def slot(d):
        return pl.ds(pl.multiple_of(d * rows, 16), rows)

    def hcopy(d):
        return rcopy(hid_ref, raw.at[slot(d), own_half], h_send, h_recv.at[d], (vpeer(d), w))

    def squares(x):
        return jnp.sum(x * x, axis=1, keepdims=True)

    def to_row(column, wide):
        height = column.shape[0]
        there = lax.broadcasted_iota(jnp.int32, (height, wide), 1)
        here = lax.broadcasted_iota(jnp.int32, (height, wide), 0)
        return jnp.sum(jnp.where(there == here, column, 0.0), axis=0, keepdims=True)

    def to_column(row, height):
        wide = row.shape[1]
        there = lax.broadcasted_iota(jnp.int32, (height, wide), 1)
        here = lax.broadcasted_iota(jnp.int32, (height, wide), 0)
        return jnp.sum(jnp.where(there == here, row, 0.0), axis=1, keepdims=True)

    for load in loads:
        load.wait()
    gains[...] = gain_ref[...].astype(jnp.float32)
    x = hid_ref[...].astype(jnp.float32)
    sq = squares(x)
    sq_all[w] = to_row(sq, LANES)
    for g in range(groups):
        column = pl.ds(pl.multiple_of(lo * feats + g * LANES, LANES), LANES)
        scaled = x[:, g * LANES : (g + 1) * LANES] * gains[pl.ds(w * groups + g, 1), :]
        upper = scaled.astype(jnp.bfloat16)
        split_rows[0:rows, column] = upper
        split_rows[rows : 2 * rows, column] = (scaled - upper.astype(jnp.float32)).astype(
            jnp.bfloat16
        )
    ints_all[w] = jnp.zeros(ints_all.shape[1:], jnp.int32)
    ints_all[w, 0:1, 0:bw] = aim_ref[...]
    ints_all[w, 1:2, 0:bw] = deal_ref[...]
    def lanes_peak(z):
        peak = jnp.max(jnp.abs(z), axis=0, keepdims=True)
        parts = [peak[:, g * LANES : (g + 1) * LANES] for g in range(cn // LANES)]
        return functools.reduce(jnp.maximum, parts)

    def quantized(z, rate):
        for g in range(cn // LANES):
            part = slice(g * LANES, (g + 1) * LANES)
            yield part, jnp.round(z[:, part] * rate).astype(jnp.int32).astype(jnp.int16)

    def folded(both, scale):
        return (both[0:rows] + both[rows : 2 * rows]) * scale

    core_scale = lax.rsqrt(sq * (1.0 / feats) + epsilon)
    wlocal(0, False, 0).wait()
    mate_first.wait()
    for k, weights in enumerate((wbuf[0, own_half, :], wmate[...])):
        z = folded(
            jnp.dot(split_rows[:, own_half], weights, preferred_element_type=jnp.float32),
            core_scale,
        )
        peak = jnp.maximum(TINY, lanes_peak(z))
        zown_send[k] = peak * (1.0 / STEPS)
        for part, value in quantized(z, STEPS / peak):
            sown[k, :, part] = value
    pl.semaphore_wait(barrier, WIDTH - 1 + V - 1)

    def xcopy():
        return rcopy(hid_ref, mate_hid, x_send, x_recv, (v, mate))

    def icopy(d, dev):
        return rcopy(ints_all.at[w], ints_all.at[dev], i_send, i_recv, (v, wpeer(d)))

    across = far + 1 - 2 * lo

    def scopy(half):
        return rcopy(
            split_rows.at[:, half], split_rows.at[:, half], s_send, s_recv, (v, mate)
        )

    def qstart(there, sem):
        rcopy(sq_all.at[w], sq_all.at[w], q_send, q_recv.at[sem], (v, there)).start()

    def owncopy(k, there):
        return rcopy(sown.at[k], rown.at[lo], own_send, own_recv.at[0], (v, there))

    def zocopy(k, there):
        return rcopy(zown_send.at[k], zown.at[lo], zo_send, own_recv.at[1], (v, there))

    for k, there in enumerate((far, across)):
        owncopy(k, there).start()
        zocopy(k, there).start()
    scopy(own_half).start()
    qstart(mate, 0)
    wremote(1, False).start()
    qstart(far, 1)
    qstart(across, 1)

    @pl.loop(2, DEPTH)
    def _(k):
        wremote(k, False).start()

    xcopy().start()

    @pl.loop(1, V)
    def _(d):
        hcopy(V - d).start()

    @pl.loop(DEPTH, n)
    def _(k):
        wremote(k, False).start()

    wremote(0, False).start()

    @pl.loop(1, WIDTH)
    def _(d):
        icopy(d, w).start()

    landed(sq_all.at[mate], q_recv.at[0])
    chip_sq = sq + to_column(sq_all[mate], rows)
    chip_scale[...] = jnp.broadcast_to(
        lax.rsqrt(chip_sq * (1.0 / (2 * feats)) + epsilon), (rows, LANES)
    )
    scopy(mate_half).wait_recv()

    def vspan(dev):
        return pl.ds(pl.multiple_of(dev * rows, 16), rows)

    def normalize():
        landed(sq_all.at[0:2], q_recv.at[1])
        xcopy().wait_recv()
        total_sq = sq_all[0] + sq_all[1] + sq_all[2] + sq_all[3]
        mean_row = total_sq * (1.0 / D)
        msq_all[v] = mean_row
        mean_sq = to_column(mean_row, rows)
        scale = lax.rsqrt(mean_sq + epsilon)
        far_sq = to_column(sq_all[far] + sq_all[across], rows)
        far_scale = lax.rsqrt(far_sq * (1.0 / (2 * feats)) + epsilon)
        ratio[0:rows, :] = jnp.broadcast_to(scale / far_scale, (rows, LANES))
        for core, dev in ((lo, far), (1 - lo, across)):
            dev_sq = to_column(sq_all[dev], rows)
            dev_scale = lax.rsqrt(dev_sq * (1.0 / feats) + epsilon)
            own_ratio[core] = jnp.broadcast_to(scale / dev_scale, (rows, LANES))
        for half, dev, source in ((lo, w, hid_ref), (1 - lo, mate, mate_hid)):
            for g in range(groups):
                column = pl.ds(pl.multiple_of(half * feats + g * LANES, LANES), LANES)
                value = source[:, g * LANES : (g + 1) * LANES].astype(jnp.float32)
                nrm[0:rows, column] = (
                    value * scale * gains[pl.ds(dev * groups + g, 1), :]
                ).astype(jnp.bfloat16)

    def fcopy(d, half):
        part = raw.at[slot(d), half]
        return rcopy(part, part, f_send, f_recv, (v, mate))

    def rmscopy(d, dev):
        return rcopy(msq_all.at[v], msq_all.at[dev], r_send, r_recv, (vpeer(d), w))

    def ycopy(i):
        part = pl.ds(rows, late)
        return rcopy(
            sbuf.at[i, part, :], rbuf.at[i, part, :], y_send, y_recv.at[i], (v, far)
        )

    def yacopy(i):
        part = pl.ds(0, rows)
        return rcopy(
            sbuf.at[i, part, :], rbuf.at[i, part, :], ya_send, ya_recv, (v, far)
        )

    def zcopy(k):
        return rcopy(zsend.at[k], zrecv.at[k], z_send, z_recv.at[k - n], (v, far))

    def zacopy(k):
        return rcopy(zsend.at[k], zrecv.at[k], z_send, za_recv, (v, far))

    def yblock(c, d, sem):
        return rcopy(sbuf.at[c, slot(d), :], rbuf.at[c, slot(d), :], y_send, sem, (v, far))

    def start_block(d):
        @pl.loop(plain, n)
        def _(c):
            yblock(c, d, h_recv.at[d]).start()

    def wait_block(d):
        landed(rbuf.at[pl.ds(plain, LAST), slot(d), :], h_recv.at[d])

    def ystart(i):
        zcopy(n + i).start()
        ycopy(i).start()

    def yarrive(i):
        zcopy(n + i).wait_recv()

    def quantize(i, span, rate, z):
        for part, value in quantized(z, rate):
            sbuf[i, span, part] = value

    def first_dot(i):
        wwait(i, False)
        z = folded(
            jnp.dot(split_rows[...], wbuf[i], preferred_element_type=jnp.float32),
            chip_scale[:, 0:1],
        )
        peak = jnp.maximum(TINY, lanes_peak(z))
        zsend[i] = peak * (1.0 / STEPS)
        quantize(i, pl.ds(0, rows), STEPS / peak, z)
        zacopy(i).start()
        yacopy(i).start()

    def add_own():
        for core in range(2):
            scale = own_ratio[core] * zown[core]
            for g in range(cn // LANES):
                part = slice(g * LANES, (g + 1) * LANES)
                xbuf[0, 0:rows, part] += rown[core, :, part].astype(jnp.int32).astype(jnp.float32) * scale

    def send_dot(i):
        def multiply(r, peak):
            span = pl.ds(pl.multiple_of(rows + r * mb_late, 16), mb_late)
            z = jnp.dot(nrm[span, :], wbuf[i], preferred_element_type=jnp.float32)
            ybuf[span, :] = z
            return jnp.maximum(peak, lanes_peak(z))

        peak = lax.fori_loop(
            0, late // mb_late, multiply, jnp.full((1, LANES), TINY, jnp.float32)
        )
        zsend[n + i] = peak * (1.0 / STEPS)
        rate = STEPS / peak

        @pl.loop(1, V)
        def _(r):
            quantize(i, slot(r), rate, ybuf[slot(r), :])

    def keep_dot(i, place):
        wwait(n + i, True)

        @pl.loop(0, tokens // mb)
        def _(r):
            span = pl.ds(pl.multiple_of(r * mb, 16), mb)
            xbuf[place, span, :] = jnp.dot(
                nrm[span, :], wbuf[n + i], preferred_element_type=jnp.float32
            )

        @pl.when(i == 0)
        def _():
            add_own()

    rb = rows
    first_column = v * slab + w * quarter

    def stats(i):
        @pl.loop(0, V)
        def _(r):
            block_stats(i, r, 0)

    def block_stats(i, r, kept):
        held = slot(r)
        span = vspan(vsource(r))
        late_z = n * ((r + V - 1) // V) + i
        target = ints_cols[span, 0:1]
        factor = zrecv[late_z] * ratio[held, :]
        lane = lax.broadcasted_iota(jnp.int32, (rb, LANES), 1)
        aim = jnp.broadcast_to(target, (rb, LANES)) - lane - (first_column + i * cn)
        xs = [
            xbuf[kept, held, g * LANES : (g + 1) * LANES]
            + rbuf[i, held, g * LANES : (g + 1) * LANES].astype(jnp.int32).astype(jnp.float32)
            * factor
            for g in range(cn // LANES)
        ]
        m_old = m_acc[span, :]
        m_new = functools.reduce(jnp.maximum, xs, m_old)
        decay = jnp.exp(m_old - m_new)
        t = t_acc[span, :] * decay
        g_ = g_acc[span, :] * decay
        p = p_acc[span, :]
        for g, z in enumerate(xs):
            e = jnp.exp(z - m_new)
            t = t + e
            g_ = g_ + e * z
            p = p + jnp.where(aim == g * LANES, z, 0.0)
        m_acc[span, :] = m_new
        t_acc[span, :] = t
        g_acc[span, :] = g_
        p_acc[span, :] = p

    def relay(d):
        hcopy(d).wait_recv()
        fcopy(d, own_half).start()

    head = min(3, n)
    wloaded(wbuf.at[1:n, own_half, :], 1)

    @pl.loop(1, head)
    def _(i):
        first_dot(i)

    normalize()

    @pl.loop(1, V)
    def _(d):
        rmscopy(d, v).start()

    turns = min(n - head, V - 2)

    @pl.loop(0, turns)
    def _(i):
        first_dot(head + i)
        relay(V - 1 - i)

    @pl.loop(head + turns, n)
    def _(i):
        first_dot(i)

    wwait(0, False)

    @pl.loop(1 + turns, V)
    def _(d):
        relay(V - d)

    landed(msq_all.at[0 : V - 1], r_recv)
    landed(raw.at[pl.ds(rows, late), mate_half], f_recv)

    @pl.loop(1, V)
    def _(d):
        scale = lax.rsqrt(to_column(msq_all[vsource(d)], rows) + epsilon)
        for g in range(2 * groups):
            column = slice(g * LANES, (g + 1) * LANES)
            gain_row = gains[pl.ds((w - lo) * groups + g, 1), :]
            nrm[slot(d), column] = (
                raw[slot(d), column].astype(jnp.float32) * scale * gain_row
            ).astype(jnp.bfloat16)

    @pl.loop(0, depth)
    def _(i):
        send_dot(i)
        ystart(i)

    @pl.loop(0, n)
    def _(k):
        wremote(n + k, True).start()
        wlocal(n + k, True, 2).start()

    def padded(block):
        return jnp.concatenate([block, jnp.zeros((LANES - pair, LANES), jnp.float32)], axis=0)

    landed(ints_all.at[0 : WIDTH - 1], i_recv)

    for q in range(WIDTH):
        columns = [
            jnp.broadcast_to(to_column(ints_all[q, k : k + 1, :].astype(jnp.float32), bw), (bw, LANES))
            for k in range(2)
        ]
        pick_lane = lax.broadcasted_iota(jnp.int32, (bw, LANES), 1)
        ints_cols[q * bw : (q + 1) * bw, :] = jnp.where(
            pick_lane == 0, columns[0], columns[1]
        ).astype(jnp.int32)

    r_row = lax.broadcasted_iota(jnp.int32, (1, LANES), 1)
    ends = jnp.zeros((1, LANES), jnp.int32)
    counts = jnp.ones((1, LANES), jnp.int32)
    for r in range(reqs):
        ends = ends + jnp.where(r_row >= REQ_LANE + r, lens_ref[r], 0)
        counts = jnp.where(r_row == REQ_LANE + r, lens_ref[r], counts)
    asked = (r_row >= REQ_LANE) & (r_row < REQ_LANE + reqs)
    starts = jnp.where(asked, ends - counts, tokens).astype(jnp.float32)
    ends = ends.astype(jnp.float32)
    counts = counts.astype(jnp.float32)
    place = ints_cols[:, 1:2].astype(jnp.float32)
    spot = jnp.where(r_row < rows, v * rows + r_row, tokens).astype(jnp.float32)
    member = (place >= starts) & (place < ends)
    chosen = jnp.where(member | (place == spot), 1.0, 0.0)
    for k in range(pairs):
        part = padded(chosen[k * pair : (k + 1) * pair])
        span = slice(k * LANES, (k + 1) * LANES)
        pick[span, :] = part
        asked_rows[:, span] = jnp.transpose(part)[REQ_LANE : REQ_LANE + reqs]
    rms = jnp.concatenate(
        [to_column(jnp.sqrt(msq_all[q] + epsilon), rows) for q in range(V)], axis=0
    )
    fixed[0:1, :] = counts
    fixed[1:2, :] = jnp.sum(jnp.where(member, rms, 0.0), axis=0, keepdims=True) / counts

    wloaded(wbuf.at[n : 2 * n, own_half, :], 2)
    landed(rbuf.at[1:n, 0:rows, :], ya_recv)
    landed(zrecv.at[1:n], za_recv)
    landed(rown, own_recv.at[0])
    landed(zown, own_recv.at[1])
    rbuf[0, 0:rows, :] = jnp.zeros((rows, cn), jnp.int16)
    zrecv[0] = jnp.zeros((1, LANES), jnp.float32)

    def finished(i):
        yarrive(i)
        ycopy(i).wait_recv()

    @pl.loop(0, plain - depth)
    def _(i):
        keep_dot(i, 0)
        send_dot(i + depth)
        finished(i)
        ystart(i + depth)
        stats(i)

    @pl.loop(plain, n)
    def _(c):
        send_dot(c)
        zcopy(n + c).start()

    @pl.loop(1, 1 + DEPTH)
    def _(d):
        start_block(d)

    @pl.loop(plain - depth, plain)
    def _(i):
        keep_dot(i, 0)
        finished(i)
        stats(i)

    def block_total(d):
        @pl.loop(plain, n)
        def _(c):
            block_stats(c, d, 1 + c - plain)

    @pl.loop(plain, n)
    def _(c):
        keep_dot(c, 1 + c - plain)
        yarrive(c)

    block_total(0)

    @pl.loop(1, V - 1 - END)
    def _(d):
        wait_block(d)

        @pl.when(d + DEPTH < V - 1)
        def _():
            start_block(d + DEPTH)

        block_total(d)

    def last_piece(k):
        return yblock(plain + k, V - 1, last_recv.at[k])

    wait_block(V - 1 - END)
    for k in range(LAST - 1):
        last_piece(k).start()
    block_total(V - 1 - END)

    def columns_of(span, height):
        m = m_acc[span, :]
        top = jnp.max(m, axis=1, keepdims=True)
        share = jnp.exp(m - top)
        tot = jnp.sum(t_acc[span, :] * share, axis=1, keepdims=True)
        wei = jnp.sum(g_acc[span, :] * share, axis=1, keepdims=True)
        pic = jnp.sum(p_acc[span, :], axis=1, keepdims=True)
        lane = lax.broadcasted_iota(jnp.int32, (height, LANES), 1)
        return jnp.where(
            lane == 0, top, jnp.where(lane == 1, tot, jnp.where(lane == 2, wei, pic))
        )

    lane = lax.broadcasted_iota(jnp.int32, (tokens, LANES), 1)
    line = lax.broadcasted_iota(jnp.int32, (tokens, LANES), 0)
    open_row = (line >= last_pair * pair) & (line < (last_pair + 1) * pair)
    table = jnp.where(
        open_row, jnp.where(lane == 0, LOW, 0.0), columns_of(slice(0, tokens), tokens)
    )
    for k in range(pairs):
        part = padded(table[k * pair : (k + 1) * pair])
        st1[w, :, k * LANES : (k + 1) * LANES] = jnp.transpose(part)[0:4]

    def acopy(d, dev):
        return rcopy(st1.at[w], st1.at[dev], a_send, a_recv, (v, wpeer(d)))

    def bcopy(d, dev):
        return rcopy(st2.at[v], st2.at[dev], b_send, b_recv, (vpeer(d), w))

    def joined(parts):
        top = functools.reduce(jnp.maximum, [s[0:1, :] for s in parts])
        tot = jnp.zeros_like(top)
        wei = jnp.zeros_like(top)
        pic = jnp.zeros_like(top)
        for s in parts:
            share = jnp.exp(s[0:1, :] - top)
            tot = tot + s[1:2, :] * share
            wei = wei + s[2:3, :] * share
            pic = pic + s[3:4, :]
        return top, tot, wei, pic

    @pl.loop(1, WIDTH)
    def _(d):
        acopy(d, w).start()

    last_piece(LAST - 1).start()
    wait_block(V - END)
    block_total(V - END)

    def last_stats(k):
        last_piece(k).wait_recv()
        block_stats(plain + k, V - 1, 1 + k)

    for k in range(LAST - 1):
        last_stats(k)

    landed(st1.at[0 : WIDTH - 1], a_recv)

    sub = lax.broadcasted_iota(jnp.int32, (4, pairs * LANES), 0)
    top, tot, wei, pic = joined([st1[q] for q in range(WIDTH)])
    st2[v] = jnp.where(sub == 0, top, jnp.where(sub == 1, tot, jnp.where(sub == 2, wei, pic)))

    @pl.loop(1, V)
    def _(d):
        bcopy(d, v).start()

    last_stats(LAST - 1)
    me = v * WIDTH + w
    span = pl.ds(pl.multiple_of(last_pair * pair, 16), pair)
    fin[me] = jnp.transpose(padded(columns_of(span, pair)))[0:4]

    def ccopy(k):
        return rcopy(
            fin.at[me], fin.at[me], c_send, c_recv, (flipped(k // WIDTH), lax.rem(w + k, WIDTH))
        )

    @pl.loop(1, V * WIDTH)
    def _(k):
        ccopy(k).start()

    xcopy().wait_send()
    drained(sq_all.at[0 : WIDTH - 1], q_send)
    scopy(own_half).wait_send()
    drained(ints_all.at[0 : WIDTH - 1], i_send)
    drained(msq_all.at[0 : V - 1], r_send)
    drained(raw.at[pl.ds(rows, late), own_half], h_send)
    drained(raw.at[pl.ds(rows, late), own_half], f_send)
    drained(wbuf.at[:, own_half, :], w_send)
    drained(sbuf.at[:, pl.ds(rows, late), :], y_send)
    drained(sbuf.at[1:n, 0:rows, :], ya_send)
    drained(zsend.at[pl.ds(1, 2 * n - 1)], z_send)
    drained(sown, own_send)
    drained(zown_send, zo_send)
    landed(st2.at[0 : V - 1], b_recv)
    early = joined([st2[q] for q in range(V)])
    landed(fin.at[0 : V * WIDTH - 1], c_recv)
    parts = [jnp.concatenate(early, axis=0)]
    for q in range(END * WIDTH):
        parts.append(
            jnp.concatenate(
                [fin[(pairs - 1 - k) * END * WIDTH + q] for k in range(pairs)], axis=1
            )
        )
    largest, tot, wei, pic = joined(parts)
    log_total = jnp.log(tot)
    wide = pairs * LANES
    place = lax.broadcasted_iota(jnp.int32, (8, wide), 0)
    used = lax.rem(lax.broadcasted_iota(jnp.int32, (1, wide), 1), LANES) < pair
    spread = jnp.zeros((8, wide), jnp.float32)
    for k, rest in enumerate(
        (pic - largest - log_total, largest + log_total - wei / tot)
    ):
        rest = jnp.where(used, rest, 0.0)
        for part in range(3):
            upper = rest.astype(jnp.bfloat16).astype(jnp.float32)
            spread = jnp.where(place == 2 * part + k, upper, spread)
            rest = rest - upper
    dealt = jnp.dot(
        spread.astype(jnp.bfloat16),
        pick[...].astype(jnp.bfloat16),
        preferred_element_type=jnp.float32,
    )
    sums = dealt[0:2] + dealt[2:4] + dealt[4:6]
    out_ref[0:1, :] = sums[0:1]
    out_ref[4:6, :] = sums / fixed[0:1, :]
    out_ref[6:7, :] = fixed[1:2, :]
    highest = jnp.max(jnp.where(asked_rows[...] > 0.5, largest, LOW), axis=1, keepdims=True)
    there = lax.broadcasted_iota(jnp.int32, (reqs, LANES), 1)
    here = lax.broadcasted_iota(jnp.int32, (reqs, LANES), 0)
    out_ref[7:8, :] = jnp.sum(
        jnp.where(there == here + REQ_LANE, highest, 0.0), axis=0, keepdims=True
    )
    drained(st1.at[0 : WIDTH - 1], a_send)
    drained(st2.at[0 : V - 1], b_send)
    drained(fin.at[0 : V * WIDTH - 1], c_send)


def finish(rows, reqs, res_ref, tok_ref, stat_ref):
    tok_ref[...] = res_ref[0:1, 0:rows]
    stat_ref[...] = res_ref[4:8, REQ_LANE : REQ_LANE + reqs]


def body(hidden, norm_gain, head_weight, lengths, deal, targets):
    rows, feats = hidden.shape
    V = lax.axis_size("vocab")
    tokens = rows * V
    slab = head_weight.shape[1]
    quarter = slab // WIDTH
    cn = next(c for c in (512, 256, 128) if quarter % c == 0)
    n = quarter // cn
    mb = next(c for c in (384, 256, 192, 128, 64, 48, 16) if tokens % c == 0)
    reqs = lengths.shape[0]
    bw = tokens // WIDTH

    gain = norm_gain.reshape(-1, LANES)
    bwp = -(-bw // LANES) * LANES
    late = tokens - rows
    mb_late = next(c for c in (336, 192, 144, 96, 48, 16) if late % c == 0)

    cfg = (V, rows, tokens, feats, slab, quarter, cn, n, mb, mb_late, reqs)
    f32, bf16 = jnp.float32, jnp.bfloat16
    dma = pltpu.SemaphoreType.DMA
    vmem = pl.BlockSpec(memory_space=pltpu.VMEM)
    hbm = pl.BlockSpec(memory_space=pltpu.HBM)
    res = pl.pallas_call(
        functools.partial(kernel, cfg),
        out_shape=jax.ShapeDtypeStruct((8, LANES), f32),
        in_specs=[hbm] * 6,
        out_specs=vmem,
        scratch_shapes=[
            pltpu.SMEM((reqs,), jnp.int32),
            pltpu.VMEM((1, bw), jnp.int32),
            pltpu.VMEM((1, bw), jnp.int32),
            pltpu.VMEM((D // LANES, LANES), bf16),
            pltpu.VMEM((rows, feats), bf16),
            pltpu.VMEM((D // LANES, LANES), f32),
            pltpu.VMEM((WIDTH, 2, bwp), jnp.int32),
            pltpu.VMEM((tokens, LANES), jnp.int32),
            pltpu.VMEM((rows, feats), bf16),
            pltpu.VMEM((tokens, 2 * feats), bf16),
            pltpu.VMEM((2 * rows, 2 * feats), bf16),
            pltpu.VMEM((rows, LANES), f32),
            pltpu.VMEM((tokens, LANES), f32),
            pltpu.VMEM((WIDTH, 1, LANES), f32),
            pltpu.VMEM((V, 1, LANES), f32),
            pltpu.VMEM((tokens, 2 * feats), bf16),
            pltpu.VMEM((2 * n, 2 * feats, cn), bf16),
            pltpu.VMEM((n, tokens, cn), jnp.int16),
            pltpu.VMEM((n, tokens, cn), jnp.int16),
            pltpu.VMEM((LAST + 1, tokens, cn), f32),
            pltpu.VMEM((tokens, cn), f32),
            pltpu.VMEM((2 * n, 1, LANES), f32),
            pltpu.VMEM((2 * n, 1, LANES), f32),
            pltpu.VMEM((feats, cn), bf16),
            pltpu.VMEM((2, rows, cn), jnp.int16),
            pltpu.VMEM((2, rows, cn), jnp.int16),
            pltpu.VMEM((2, 1, LANES), f32),
            pltpu.VMEM((2, 1, LANES), f32),
            pltpu.VMEM((2, rows, LANES), f32),
            pltpu.VMEM((tokens, LANES), f32),
            pltpu.VMEM((tokens, LANES), f32),
            pltpu.VMEM((tokens, LANES), f32),
            pltpu.VMEM((tokens, LANES), f32),
            pltpu.VMEM((WIDTH, 4, V // END * LANES), f32),
            pltpu.VMEM((V, 4, V // END * LANES), f32),
            pltpu.VMEM((V * WIDTH, 4, LANES), f32),
            pltpu.VMEM((V // END * LANES, LANES), f32),
            pltpu.VMEM((reqs, V // END * LANES), f32),
            pltpu.VMEM((8, LANES), f32),
            dma((16,)),
            dma,
            dma,
            dma,
            dma((2,)),
            dma((V,)),
            dma,
            dma,
            dma((4,)),
            dma((n,)),
            dma((n,)),
            dma((n,)),
            dma((2,)),
            dma,
            dma,
            dma,
            dma,
            dma,
            dma((LAST,)),
        ],
        compiler_params=pltpu.CompilerParams(
            collective_id=0, has_side_effects=True, vmem_limit_bytes=58 << 20
        ),
    )(targets[None], deal[None], lengths, gain, hidden, head_weight)
    tok, stat = pl.pallas_call(
        functools.partial(finish, rows, reqs),
        out_shape=(
            jax.ShapeDtypeStruct((1, rows), f32),
            jax.ShapeDtypeStruct((4, reqs), f32),
        ),
        in_specs=[vmem],
        out_specs=(vmem, vmem),
    )(res)
    return tok[0], stat


def solution(mesh):
    return jax.shard_map(
        body,
        mesh=mesh,
        in_specs=(P("vocab", "width"), P(), P("width", "vocab"), P(), P("width"), P("width")),
        out_specs=(P("vocab"), P()),
        check_vma=False,
    )
```

```python
import functools

import jax
import jax.numpy as jnp
from jax import lax
from jax.experimental import pallas as pl
from jax.experimental.pallas import tpu as pltpu
from jax.sharding import PartitionSpec as P

D = 2048
epsilon = 1e-06
LOW = -1e30
TINY = 1e-30
STEPS = 32767.0
DEPTH = 3
LAST = 3
AHEAD = 1
END = 2
LANES = 128
REQ_LANE = 64
WIDTH = 4


def kernel(
    cfg,
    aim_hbm,
    deal_hbm,
    lens_hbm,
    gain_hbm,
    hid_hbm,
    w_ref,
    out_ref,
    lens_ref,
    aim_ref,
    deal_ref,
    gain_ref,
    hid_ref,
    gains,
    ints_all,
    ints_cols,
    mate_hid,
    raw,
    split_rows,
    chip_scale,
    ratio,
    sq_all,
    msq_all,
    nrm,
    wbuf,
    sbuf,
    rbuf,
    xbuf,
    ybuf,
    zsend,
    zrecv,
    wmate,
    sown,
    rown,
    zown_send,
    zown,
    own_ratio,
    m_acc,
    t_acc,
    g_acc,
    p_acc,
    st1,
    st2,
    fin,
    pick,
    asked_rows,
    fixed,
    once_send,
    x_recv,
    s_recv,
    i_recv,
    q_recv,
    h_recv,
    f_recv,
    r_recv,
    wl_sem,
    w_recv,
    y_recv,
    z_recv,
    own_recv,
    ya_recv,
    za_recv,
    a_recv,
    b_recv,
    c_recv,
    last_recv,
):
    V, rows, tokens, feats, slab, quarter, cn, n, mb, mb_late, reqs = cfg
    v = lax.axis_index("vocab")
    w = lax.axis_index("width")
    lo = lax.rem(w, 2)
    hi = w // 2
    mate = w + 1 - 2 * lo
    far = w + 2 - 4 * hi
    bw = tokens // WIDTH
    x_send, i_send, q_send, h_send, f_send, r_send = [once_send.at[k] for k in range(6)]
    w_send, y_send, z_send, ya_send, a_send, b_send, s_send, own_send, zo_send, c_send = [
        once_send.at[k] for k in range(6, 16)
    ]
    plain = n - LAST
    depth = min(DEPTH, plain)
    pair = END * rows
    pairs = V // END
    last_pair = pairs - 1 - v // END

    def rcopy(src, dst, ss, rs, where):
        return pltpu.make_async_remote_copy(
            src_ref=src,
            dst_ref=dst,
            send_sem=ss,
            recv_sem=rs,
            device_id=where,
            device_id_type=pl.DeviceIdType.MESH,
        )

    def drained(ref, sem):
        rcopy(ref, ref, sem, x_recv, (v, mate)).wait_send()

    def landed(ref, sem):
        rcopy(ref, ref, x_send, sem, (v, mate)).wait_recv()

    bits = [1 << b for b in range(V.bit_length() - 1)]
    ones = [lax.rem(v // bit, 2) * bit for bit in bits]

    def flipped(d):
        other = 0
        for bit, one in zip(bits, ones):
            if isinstance(d, int):
                other = other + (bit - one if d & bit else one)
            else:
                other = other + lax.rem(one // bit + d // bit, 2) * bit
        return other

    def each(first, last):
        def run(step):
            if last - first > 2 * LANES // WIDTH:
                pl.loop(first, last)(step)
            else:
                for k in range(first, last):
                    step(k)

        return run

    def vpeer(d):
        return flipped(d)

    def vsource(d):
        return flipped(d)

    def wpeer(d):
        return lax.rem(w + d, WIDTH)

    def wsource(d):
        return lax.rem(w + WIDTH - d, WIDTH)

    def wcols(k, is_keep, dev):
        dev_far = dev + 2 - 4 * (dev // 2)
        q = dev if is_keep else dev_far
        base = k - n if is_keep else k
        return pl.ds(pl.multiple_of(q * quarter + base * cn, LANES), cn)

    own_half = pl.ds(pl.multiple_of(lo * feats, LANES), feats)
    mate_half = pl.ds(pl.multiple_of((1 - lo) * feats, LANES), feats)

    def wlocal(k, is_keep, sem):
        return pltpu.make_async_copy(
            w_ref.at[:, wcols(k, is_keep, w)], wbuf.at[k, own_half, :], wl_sem.at[sem]
        )

    def wloaded(part, sem):
        pltpu.make_async_copy(part, part, wl_sem.at[sem]).wait()

    def wremote(k, is_keep):
        return rcopy(
            w_ref.at[:, wcols(k, is_keep, mate)],
            wbuf.at[k, own_half, :],
            w_send,
            w_recv.at[lax.rem(k, n)],
            (v, mate),
        )

    def wwait(k, is_keep):
        rcopy(
            w_ref.at[:, wcols(k, is_keep, mate)],
            wbuf.at[k, mate_half, :],
            w_send,
            w_recv.at[lax.rem(k, n)],
            (v, mate),
        ).wait_recv()

    barrier = pltpu.get_barrier_semaphore()

    @each(1, WIDTH)
    def _(d):
        pl.semaphore_signal(
            barrier, inc=1, device_id=(v, wpeer(d)), device_id_type=pl.DeviceIdType.MESH
        )

    @each(1, V)
    def _(d):
        pl.semaphore_signal(
            barrier, inc=1, device_id=(vpeer(d), w), device_id_type=pl.DeviceIdType.MESH
        )

    loads = [
        pltpu.make_async_copy(source, there, once_send.at[k])
        for k, (source, there) in enumerate(
            (
                (hid_hbm, hid_ref),
                (gain_hbm, gain_ref),
                (aim_hbm, aim_ref),
                (deal_hbm, deal_ref),
                (lens_hbm, lens_ref),
            )
        )
    ]
    for load in loads:
        load.start()

    mate_first = pltpu.make_async_copy(w_ref.at[:, wcols(0, False, mate)], wmate, wl_sem.at[3])
    wlocal(0, False, 0).start()
    mate_first.start()

    @pl.loop(1, n)
    def _(k):
        wlocal(k, False, 1).start()

    late = tokens - rows
    groups = feats // LANES
    ratio[pl.ds(rows, late), :] = jnp.ones((late, LANES), jnp.float32)
    m_acc[...] = jnp.full((tokens, LANES), LOW, jnp.float32)
    t_acc[...] = jnp.zeros((tokens, LANES), jnp.float32)
    g_acc[...] = jnp.zeros((tokens, LANES), jnp.float32)
    p_acc[...] = jnp.zeros((tokens, LANES), jnp.float32)

    def slot(d):
        return pl.ds(pl.multiple_of(d * rows, 16), rows)

    def hcopy(d):
        return rcopy(hid_ref, raw.at[slot(d), own_half], h_send, h_recv.at[d], (vpeer(d), w))

    def squares(x):
        return jnp.sum(x * x, axis=1, keepdims=True)

    def to_row(column, wide):
        height = column.shape[0]
        there = lax.broadcasted_iota(jnp.int32, (height, wide), 1)
        here = lax.broadcasted_iota(jnp.int32, (height, wide), 0)
        return jnp.sum(jnp.where(there == here, column, 0.0), axis=0, keepdims=True)

    def to_column(row, height):
        wide = row.shape[1]
        there = lax.broadcasted_iota(jnp.int32, (height, wide), 1)
        here = lax.broadcasted_iota(jnp.int32, (height, wide), 0)
        return jnp.sum(jnp.where(there == here, row, 0.0), axis=1, keepdims=True)

    for load in loads:
        load.wait()
    gains[...] = gain_ref[...].astype(jnp.float32)
    x = hid_ref[...].astype(jnp.float32)
    sq = squares(x)
    sq_all[w] = to_row(sq, LANES)
    for g in range(groups):
        column = pl.ds(pl.multiple_of(lo * feats + g * LANES, LANES), LANES)
        scaled = x[:, g * LANES : (g + 1) * LANES] * gains[pl.ds(w * groups + g, 1), :]
        upper = scaled.astype(jnp.bfloat16)
        split_rows[0:rows, column] = upper
        split_rows[rows : 2 * rows, column] = (scaled - upper.astype(jnp.float32)).astype(
            jnp.bfloat16
        )
    ints_all[w] = jnp.zeros(ints_all.shape[1:], jnp.int32)
    ints_all[w, 0:1, 0:bw] = aim_ref[...]
    ints_all[w, 1:2, 0:bw] = deal_ref[...]
    def lanes_peak(z):
        peak = jnp.max(jnp.abs(z), axis=0, keepdims=True)
        parts = [peak[:, g * LANES : (g + 1) * LANES] for g in range(cn // LANES)]
        return functools.reduce(jnp.maximum, parts)

    def quantized(z, rate):
        for g in range(cn // LANES):
            part = slice(g * LANES, (g + 1) * LANES)
            yield part, jnp.round(z[:, part] * rate).astype(jnp.int32).astype(jnp.int16)

    def folded(both, scale):
        return (both[0:rows] + both[rows : 2 * rows]) * scale

    core_scale = lax.rsqrt(sq * (1.0 / feats) + epsilon)
    wlocal(0, False, 0).wait()
    mate_first.wait()
    for k, weights in enumerate((wbuf[0, own_half, :], wmate[...])):
        z = folded(
            jnp.dot(split_rows[:, own_half], weights, preferred_element_type=jnp.float32),
            core_scale,
        )
        peak = jnp.maximum(TINY, lanes_peak(z))
        zown_send[k] = peak * (1.0 / STEPS)
        for part, value in quantized(z, STEPS / peak):
            sown[k, :, part] = value
    pl.semaphore_wait(barrier, WIDTH - 1 + V - 1)

    def xcopy():
        return rcopy(hid_ref, mate_hid, x_send, x_recv, (v, mate))

    def icopy(d, dev):
        return rcopy(ints_all.at[w], ints_all.at[dev], i_send, i_recv, (v, wpeer(d)))

    across = far + 1 - 2 * lo

    def scopy(half):
        return rcopy(
            split_rows.at[:, half], split_rows.at[:, half], s_send, s_recv, (v, mate)
        )

    def qstart(there, sem):
        rcopy(sq_all.at[w], sq_all.at[w], q_send, q_recv.at[sem], (v, there)).start()

    def owncopy(k, there):
        return rcopy(sown.at[k], rown.at[lo], own_send, own_recv.at[0], (v, there))

    def zocopy(k, there):
        return rcopy(zown_send.at[k], zown.at[lo], zo_send, own_recv.at[1], (v, there))

    for k, there in enumerate((far, across)):
        owncopy(k, there).start()
        zocopy(k, there).start()
    scopy(own_half).start()
    qstart(mate, 0)
    wremote(1, False).start()
    qstart(far, 1)
    qstart(across, 1)

    @pl.loop(2, DEPTH)
    def _(k):
        wremote(k, False).start()

    xcopy().start()

    @each(1, V)
    def _(d):
        hcopy(V - d).start()

    @pl.loop(DEPTH, n)
    def _(k):
        wremote(k, False).start()

    wremote(0, False).start()

    @pl.loop(1, WIDTH)
    def _(d):
        icopy(d, w).start()

    landed(sq_all.at[mate], q_recv.at[0])
    chip_sq = sq + to_column(sq_all[mate], rows)
    chip_scale[...] = jnp.broadcast_to(
        lax.rsqrt(chip_sq * (1.0 / (2 * feats)) + epsilon), (rows, LANES)
    )
    scopy(mate_half).wait_recv()

    def vspan(dev):
        return pl.ds(pl.multiple_of(dev * rows, 16), rows)

    def normalize():
        landed(sq_all.at[0:2], q_recv.at[1])
        xcopy().wait_recv()
        total_sq = sq_all[0] + sq_all[1] + sq_all[2] + sq_all[3]
        mean_row = total_sq * (1.0 / D)
        msq_all[v] = mean_row
        mean_sq = to_column(mean_row, rows)
        scale = lax.rsqrt(mean_sq + epsilon)
        far_sq = to_column(sq_all[far] + sq_all[across], rows)
        far_scale = lax.rsqrt(far_sq * (1.0 / (2 * feats)) + epsilon)
        ratio[0:rows, :] = jnp.broadcast_to(scale / far_scale, (rows, LANES))
        for core, dev in ((lo, far), (1 - lo, across)):
            dev_sq = to_column(sq_all[dev], rows)
            dev_scale = lax.rsqrt(dev_sq * (1.0 / feats) + epsilon)
            own_ratio[core] = jnp.broadcast_to(scale / dev_scale, (rows, LANES))
        for half, dev, source in ((lo, w, hid_ref), (1 - lo, mate, mate_hid)):
            for g in range(groups):
                column = pl.ds(pl.multiple_of(half * feats + g * LANES, LANES), LANES)
                value = source[:, g * LANES : (g + 1) * LANES].astype(jnp.float32)
                nrm[0:rows, column] = (
                    value * scale * gains[pl.ds(dev * groups + g, 1), :]
                ).astype(jnp.bfloat16)

    def fcopy(d, half):
        part = raw.at[slot(d), half]
        return rcopy(part, part, f_send, f_recv, (v, mate))

    def rmscopy(d, dev):
        return rcopy(msq_all.at[v], msq_all.at[dev], r_send, r_recv, (vpeer(d), w))

    def ycopy(i):
        part = pl.ds(rows, late)
        return rcopy(
            sbuf.at[i, part, :], rbuf.at[i, part, :], y_send, y_recv.at[i], (v, far)
        )

    def yacopy(i):
        part = pl.ds(0, rows)
        return rcopy(
            sbuf.at[i, part, :], rbuf.at[i, part, :], ya_send, ya_recv, (v, far)
        )

    def zcopy(k):
        return rcopy(zsend.at[k], zrecv.at[k], z_send, z_recv.at[k - n], (v, far))

    def zacopy(k):
        return rcopy(zsend.at[k], zrecv.at[k], z_send, za_recv, (v, far))

    def yblock(c, d, sem):
        return rcopy(sbuf.at[c, slot(d), :], rbuf.at[c, slot(d), :], y_send, sem, (v, far))

    def start_block(d):
        @pl.loop(plain, n)
        def _(c):
            yblock(c, d, h_recv.at[d]).start()

    def wait_block(d):
        landed(rbuf.at[pl.ds(plain, LAST), slot(d), :], h_recv.at[d])

    def ystart(i):
        zcopy(n + i).start()
        ycopy(i).start()

    def yarrive(i):
        zcopy(n + i).wait_recv()

    def quantize(i, span, rate, z):
        for part, value in quantized(z, rate):
            sbuf[i, span, part] = value

    def first_dot(i):
        wwait(i, False)
        z = folded(
            jnp.dot(split_rows[...], wbuf[i], preferred_element_type=jnp.float32),
            chip_scale[:, 0:1],
        )
        peak = jnp.maximum(TINY, lanes_peak(z))
        zsend[i] = peak * (1.0 / STEPS)
        quantize(i, pl.ds(0, rows), STEPS / peak, z)
        zacopy(i).start()
        yacopy(i).start()

    def add_own():
        for core in range(2):
            scale = own_ratio[core] * zown[core]
            for g in range(cn // LANES):
                part = slice(g * LANES, (g + 1) * LANES)
                xbuf[0, 0:rows, part] += rown[core, :, part].astype(jnp.int32).astype(jnp.float32) * scale

    def send_dot(i):
        def multiply(r, peak):
            span = pl.ds(pl.multiple_of(rows + r * mb_late, 16), mb_late)
            z = jnp.dot(nrm[span, :], wbuf[i], preferred_element_type=jnp.float32)
            ybuf[span, :] = z
            return jnp.maximum(peak, lanes_peak(z))

        peak = lax.fori_loop(
            0, late // mb_late, multiply, jnp.full((1, LANES), TINY, jnp.float32)
        )
        zsend[n + i] = peak * (1.0 / STEPS)
        rate = STEPS / peak

        @pl.loop(1, V)
        def _(r):
            quantize(i, slot(r), rate, ybuf[slot(r), :])

    def keep_dot(i, place):
        wwait(n + i, True)

        @pl.loop(0, tokens // mb)
        def _(r):
            span = pl.ds(pl.multiple_of(r * mb, 16), mb)
            xbuf[place, span, :] = jnp.dot(
                nrm[span, :], wbuf[n + i], preferred_element_type=jnp.float32
            )

        @pl.when(i == 0)
        def _():
            add_own()

    rb = rows
    first_column = v * slab + w * quarter

    def stats(i):
        @pl.loop(0, V)
        def _(r):
            block_stats(i, r, 0)

    def block_stats(i, r, kept):
        held = slot(r)
        span = vspan(vsource(r))
        late_z = n * ((r + V - 1) // V) + i
        target = ints_cols[span, 0:1]
        factor = zrecv[late_z] * ratio[held, :]
        lane = lax.broadcasted_iota(jnp.int32, (rb, LANES), 1)
        aim = jnp.broadcast_to(target, (rb, LANES)) - lane - (first_column + i * cn)
        xs = [
            xbuf[kept, held, g * LANES : (g + 1) * LANES]
            + rbuf[i, held, g * LANES : (g + 1) * LANES].astype(jnp.int32).astype(jnp.float32)
            * factor
            for g in range(cn // LANES)
        ]
        m_old = m_acc[span, :]
        m_new = functools.reduce(jnp.maximum, xs, m_old)
        decay = jnp.exp(m_old - m_new)
        t = t_acc[span, :] * decay
        g_ = g_acc[span, :] * decay
        p = p_acc[span, :]
        for g, z in enumerate(xs):
            e = jnp.exp(z - m_new)
            t = t + e
            g_ = g_ + e * z
            p = p + jnp.where(aim == g * LANES, z, 0.0)
        m_acc[span, :] = m_new
        t_acc[span, :] = t
        g_acc[span, :] = g_
        p_acc[span, :] = p

    def relay(d):
        hcopy(d).wait_recv()
        fcopy(d, own_half).start()

    head = min(3, n)
    wloaded(wbuf.at[1:n, own_half, :], 1)

    @pl.loop(1, head)
    def _(i):
        first_dot(i)

    normalize()

    @each(1, V)
    def _(d):
        rmscopy(d, v).start()

    turns = min(n - head, V - 2)

    @pl.loop(0, turns)
    def _(i):
        first_dot(head + i)
        relay(V - 1 - i)

    @pl.loop(head + turns, n)
    def _(i):
        first_dot(i)

    wwait(0, False)

    @pl.loop(1 + turns, V)
    def _(d):
        relay(V - d)

    landed(msq_all.at[0 : V - 1], r_recv)
    landed(raw.at[pl.ds(rows, late), mate_half], f_recv)

    @pl.loop(1, V)
    def _(d):
        scale = lax.rsqrt(to_column(msq_all[vsource(d)], rows) + epsilon)
        for g in range(2 * groups):
            column = slice(g * LANES, (g + 1) * LANES)
            gain_row = gains[pl.ds((w - lo) * groups + g, 1), :]
            nrm[slot(d), column] = (
                raw[slot(d), column].astype(jnp.float32) * scale * gain_row
            ).astype(jnp.bfloat16)

    @pl.loop(0, depth)
    def _(i):
        send_dot(i)
        ystart(i)

    @pl.loop(0, n)
    def _(k):
        wremote(n + k, True).start()
        wlocal(n + k, True, 2).start()

    def padded(block):
        return jnp.concatenate([block, jnp.zeros((LANES - pair, LANES), jnp.float32)], axis=0)

    landed(ints_all.at[0 : WIDTH - 1], i_recv)

    for q in range(WIDTH):
        columns = [
            jnp.broadcast_to(to_column(ints_all[q, k : k + 1, :].astype(jnp.float32), bw), (bw, LANES))
            for k in range(2)
        ]
        pick_lane = lax.broadcasted_iota(jnp.int32, (bw, LANES), 1)
        ints_cols[q * bw : (q + 1) * bw, :] = jnp.where(
            pick_lane == 0, columns[0], columns[1]
        ).astype(jnp.int32)

    r_row = lax.broadcasted_iota(jnp.int32, (1, LANES), 1)
    ends = jnp.zeros((1, LANES), jnp.int32)
    counts = jnp.ones((1, LANES), jnp.int32)
    for r in range(reqs):
        ends = ends + jnp.where(r_row >= REQ_LANE + r, lens_ref[r], 0)
        counts = jnp.where(r_row == REQ_LANE + r, lens_ref[r], counts)
    asked = (r_row >= REQ_LANE) & (r_row < REQ_LANE + reqs)
    starts = jnp.where(asked, ends - counts, tokens).astype(jnp.float32)
    ends = ends.astype(jnp.float32)
    counts = counts.astype(jnp.float32)
    place = ints_cols[:, 1:2].astype(jnp.float32)
    spot = jnp.where(r_row < rows, v * rows + r_row, tokens).astype(jnp.float32)
    member = (place >= starts) & (place < ends)
    chosen = jnp.where(member | (place == spot), 1.0, 0.0)
    for k in range(pairs):
        part = padded(chosen[k * pair : (k + 1) * pair])
        span = slice(k * LANES, (k + 1) * LANES)
        pick[span, :] = part
        asked_rows[:, span] = jnp.transpose(part)[REQ_LANE : REQ_LANE + reqs]
    rms = jnp.concatenate(
        [to_column(jnp.sqrt(msq_all[q] + epsilon), rows) for q in range(V)], axis=0
    )
    fixed[0:1, :] = counts
    fixed[1:2, :] = jnp.sum(jnp.where(member, rms, 0.0), axis=0, keepdims=True) / counts

    wloaded(wbuf.at[n : 2 * n, own_half, :], 2)
    landed(rbuf.at[1:n, 0:rows, :], ya_recv)
    landed(zrecv.at[1:n], za_recv)
    landed(rown, own_recv.at[0])
    landed(zown, own_recv.at[1])
    rbuf[0, 0:rows, :] = jnp.zeros((rows, cn), jnp.int16)
    zrecv[0] = jnp.zeros((1, LANES), jnp.float32)

    def finished(i):
        yarrive(i)
        ycopy(i).wait_recv()

    @pl.loop(0, plain - depth)
    def _(i):
        keep_dot(i, 0)
        send_dot(i + depth)
        finished(i)
        ystart(i + depth)
        stats(i)

    @pl.loop(plain, n)
    def _(c):
        send_dot(c)
        zcopy(n + c).start()

    @pl.loop(1, 1 + DEPTH)
    def _(d):
        start_block(d)

    @pl.loop(plain - depth, plain)
    def _(i):
        keep_dot(i, 0)
        finished(i)
        stats(i)

    def block_total(d):
        @pl.loop(plain, n)
        def _(c):
            block_stats(c, d, 1 + c - plain)

    @pl.loop(plain, n)
    def _(c):
        keep_dot(c, 1 + c - plain)
        yarrive(c)

    block_total(0)

    @pl.loop(1, V - 1 - END)
    def _(d):
        wait_block(d)

        @pl.when(d + DEPTH < V - 1)
        def _():
            start_block(d + DEPTH)

        block_total(d)

    def last_piece(k):
        return yblock(plain + k, V - 1, last_recv.at[k])

    wait_block(V - 1 - END)
    for k in range(AHEAD):
        last_piece(k).start()
    block_total(V - 1 - END)

    def columns_of(span, height):
        m = m_acc[span, :]
        top = jnp.max(m, axis=1, keepdims=True)
        share = jnp.exp(m - top)
        tot = jnp.sum(t_acc[span, :] * share, axis=1, keepdims=True)
        wei = jnp.sum(g_acc[span, :] * share, axis=1, keepdims=True)
        pic = jnp.sum(p_acc[span, :], axis=1, keepdims=True)
        lane = lax.broadcasted_iota(jnp.int32, (height, LANES), 1)
        return jnp.where(
            lane == 0, top, jnp.where(lane == 1, tot, jnp.where(lane == 2, wei, pic))
        )

    lane = lax.broadcasted_iota(jnp.int32, (tokens, LANES), 1)
    line = lax.broadcasted_iota(jnp.int32, (tokens, LANES), 0)
    open_row = (line >= last_pair * pair) & (line < (last_pair + 1) * pair)
    table = jnp.where(
        open_row, jnp.where(lane == 0, LOW, 0.0), columns_of(slice(0, tokens), tokens)
    )
    for k in range(pairs):
        part = padded(table[k * pair : (k + 1) * pair])
        st1[w, :, k * LANES : (k + 1) * LANES] = jnp.transpose(part)[0:4]

    def acopy(d, dev):
        return rcopy(st1.at[w], st1.at[dev], a_send, a_recv, (v, wpeer(d)))

    def bcopy(d, dev):
        return rcopy(st2.at[v], st2.at[dev], b_send, b_recv, (vpeer(d), w))

    def joined(parts):
        top = functools.reduce(jnp.maximum, [s[0:1, :] for s in parts])
        tot = jnp.zeros_like(top)
        wei = jnp.zeros_like(top)
        pic = jnp.zeros_like(top)
        for s in parts:
            share = jnp.exp(s[0:1, :] - top)
            tot = tot + s[1:2, :] * share
            wei = wei + s[2:3, :] * share
            pic = pic + s[3:4, :]
        return top, tot, wei, pic

    @each(1, WIDTH)
    def _(d):
        acopy(d, w).start()

    for k in range(AHEAD, LAST):
        last_piece(k).start()
    wait_block(V - END)
    block_total(V - END)

    def last_stats(k):
        last_piece(k).wait_recv()
        block_stats(plain + k, V - 1, 1 + k)

    for k in range(AHEAD):
        last_stats(k)

    landed(st1.at[0 : WIDTH - 1], a_recv)

    sub = lax.broadcasted_iota(jnp.int32, (4, pairs * LANES), 0)
    top, tot, wei, pic = joined([st1[q] for q in range(WIDTH)])
    st2[v] = jnp.where(sub == 0, top, jnp.where(sub == 1, tot, jnp.where(sub == 2, wei, pic)))

    @each(1, V)
    def _(d):
        bcopy(d, v).start()

    for k in range(AHEAD, LAST):
        last_stats(k)
    me = v * WIDTH + w
    span = pl.ds(pl.multiple_of(last_pair * pair, 16), pair)
    fin[me] = jnp.transpose(padded(columns_of(span, pair)))[0:4]

    def ccopy(k):
        return rcopy(
            fin.at[me], fin.at[me], c_send, c_recv, (flipped(k // WIDTH), lax.rem(w + k, WIDTH))
        )

    @each(1, V * WIDTH)
    def _(k):
        ccopy(V * WIDTH - k).start()

    xcopy().wait_send()
    drained(sq_all.at[0 : WIDTH - 1], q_send)
    scopy(own_half).wait_send()
    drained(ints_all.at[0 : WIDTH - 1], i_send)
    drained(msq_all.at[0 : V - 1], r_send)
    drained(raw.at[pl.ds(rows, late), own_half], h_send)
    drained(raw.at[pl.ds(rows, late), own_half], f_send)
    drained(wbuf.at[:, own_half, :], w_send)
    drained(sbuf.at[:, pl.ds(rows, late), :], y_send)
    drained(sbuf.at[1:n, 0:rows, :], ya_send)
    drained(zsend.at[pl.ds(1, 2 * n - 1)], z_send)
    drained(sown, own_send)
    drained(zown_send, zo_send)
    landed(st2.at[0 : V - 1], b_recv)
    early = joined([st2[q] for q in range(V)])
    landed(fin.at[0 : V * WIDTH - 1], c_recv)
    parts = [jnp.concatenate(early, axis=0)]
    for q in range(END * WIDTH):
        parts.append(
            jnp.concatenate(
                [fin[(pairs - 1 - k) * END * WIDTH + q] for k in range(pairs)], axis=1
            )
        )
    largest, tot, wei, pic = joined(parts)
    log_total = jnp.log(tot)
    wide = pairs * LANES
    place = lax.broadcasted_iota(jnp.int32, (8, wide), 0)
    used = lax.rem(lax.broadcasted_iota(jnp.int32, (1, wide), 1), LANES) < pair
    spread = jnp.zeros((8, wide), jnp.float32)
    for k, rest in enumerate(
        (pic - largest - log_total, largest + log_total - wei / tot)
    ):
        rest = jnp.where(used, rest, 0.0)
        for part in range(3):
            upper = rest.astype(jnp.bfloat16).astype(jnp.float32)
            spread = jnp.where(place == 2 * part + k, upper, spread)
            rest = rest - upper
    dealt = jnp.dot(
        spread.astype(jnp.bfloat16),
        pick[...].astype(jnp.bfloat16),
        preferred_element_type=jnp.float32,
    )
    sums = dealt[0:2] + dealt[2:4] + dealt[4:6]
    out_ref[0:1, :] = sums[0:1]
    out_ref[4:6, :] = sums / fixed[0:1, :]
    out_ref[6:7, :] = fixed[1:2, :]
    highest = jnp.max(jnp.where(asked_rows[...] > 0.5, largest, LOW), axis=1, keepdims=True)
    there = lax.broadcasted_iota(jnp.int32, (reqs, LANES), 1)
    here = lax.broadcasted_iota(jnp.int32, (reqs, LANES), 0)
    out_ref[7:8, :] = jnp.sum(
        jnp.where(there == here + REQ_LANE, highest, 0.0), axis=0, keepdims=True
    )
    drained(st1.at[0 : WIDTH - 1], a_send)
    drained(st2.at[0 : V - 1], b_send)
    drained(fin.at[0 : V * WIDTH - 1], c_send)


def finish(rows, reqs, res_ref, tok_ref, stat_ref):
    tok_ref[...] = res_ref[0:1, 0:rows]
    stat_ref[...] = res_ref[4:8, REQ_LANE : REQ_LANE + reqs]


def body(hidden, norm_gain, head_weight, lengths, deal, targets):
    rows, feats = hidden.shape
    V = lax.axis_size("vocab")
    tokens = rows * V
    slab = head_weight.shape[1]
    quarter = slab // WIDTH
    cn = next(c for c in (512, 256, 128) if quarter % c == 0)
    n = quarter // cn
    mb = next(c for c in (384, 256, 192, 128, 64, 48, 16) if tokens % c == 0)
    reqs = lengths.shape[0]
    bw = tokens // WIDTH

    gain = norm_gain.reshape(-1, LANES)
    bwp = -(-bw // LANES) * LANES
    late = tokens - rows
    mb_late = next(c for c in (336, 192, 144, 96, 48, 16) if late % c == 0)

    cfg = (V, rows, tokens, feats, slab, quarter, cn, n, mb, mb_late, reqs)
    f32, bf16 = jnp.float32, jnp.bfloat16
    dma = pltpu.SemaphoreType.DMA
    vmem = pl.BlockSpec(memory_space=pltpu.VMEM)
    hbm = pl.BlockSpec(memory_space=pltpu.HBM)
    res = pl.pallas_call(
        functools.partial(kernel, cfg),
        out_shape=jax.ShapeDtypeStruct((8, LANES), f32),
        in_specs=[hbm] * 6,
        out_specs=vmem,
        scratch_shapes=[
            pltpu.SMEM((reqs,), jnp.int32),
            pltpu.VMEM((1, bw), jnp.int32),
            pltpu.VMEM((1, bw), jnp.int32),
            pltpu.VMEM((D // LANES, LANES), bf16),
            pltpu.VMEM((rows, feats), bf16),
            pltpu.VMEM((D // LANES, LANES), f32),
            pltpu.VMEM((WIDTH, 2, bwp), jnp.int32),
            pltpu.VMEM((tokens, LANES), jnp.int32),
            pltpu.VMEM((rows, feats), bf16),
            pltpu.VMEM((tokens, 2 * feats), bf16),
            pltpu.VMEM((2 * rows, 2 * feats), bf16),
            pltpu.VMEM((rows, LANES), f32),
            pltpu.VMEM((tokens, LANES), f32),
            pltpu.VMEM((WIDTH, 1, LANES), f32),
            pltpu.VMEM((V, 1, LANES), f32),
            pltpu.VMEM((tokens, 2 * feats), bf16),
            pltpu.VMEM((2 * n, 2 * feats, cn), bf16),
            pltpu.VMEM((n, tokens, cn), jnp.int16),
            pltpu.VMEM((n, tokens, cn), jnp.int16),
            pltpu.VMEM((LAST + 1, tokens, cn), f32),
            pltpu.VMEM((tokens, cn), f32),
            pltpu.VMEM((2 * n, 1, LANES), f32),
            pltpu.VMEM((2 * n, 1, LANES), f32),
            pltpu.VMEM((feats, cn), bf16),
            pltpu.VMEM((2, rows, cn), jnp.int16),
            pltpu.VMEM((2, rows, cn), jnp.int16),
            pltpu.VMEM((2, 1, LANES), f32),
            pltpu.VMEM((2, 1, LANES), f32),
            pltpu.VMEM((2, rows, LANES), f32),
            pltpu.VMEM((tokens, LANES), f32),
            pltpu.VMEM((tokens, LANES), f32),
            pltpu.VMEM((tokens, LANES), f32),
            pltpu.VMEM((tokens, LANES), f32),
            pltpu.VMEM((WIDTH, 4, V // END * LANES), f32),
            pltpu.VMEM((V, 4, V // END * LANES), f32),
            pltpu.VMEM((V * WIDTH, 4, LANES), f32),
            pltpu.VMEM((V // END * LANES, LANES), f32),
            pltpu.VMEM((reqs, V // END * LANES), f32),
            pltpu.VMEM((8, LANES), f32),
            dma((16,)),
            dma,
            dma,
            dma,
            dma((2,)),
            dma((V,)),
            dma,
            dma,
            dma((4,)),
            dma((n,)),
            dma((n,)),
            dma((n,)),
            dma((2,)),
            dma,
            dma,
            dma,
            dma,
            dma,
            dma((LAST,)),
        ],
        compiler_params=pltpu.CompilerParams(
            collective_id=0, has_side_effects=True, vmem_limit_bytes=58 << 20
        ),
    )(targets[None], deal[None], lengths, gain, hidden, head_weight)
    tok, stat = pl.pallas_call(
        functools.partial(finish, rows, reqs),
        out_shape=(
            jax.ShapeDtypeStruct((1, rows), f32),
            jax.ShapeDtypeStruct((4, reqs), f32),
        ),
        in_specs=[vmem],
        out_specs=(vmem, vmem),
    )(res)
    return tok[0], stat


def solution(mesh):
    return jax.shard_map(
        body,
        mesh=mesh,
        in_specs=(P("vocab", "width"), P(), P("width", "vocab"), P(), P("width"), P("width")),
        out_specs=(P("vocab"), P()),
        check_vma=False,
    )
```

```python
import functools

import jax
import jax.numpy as jnp
from jax import lax
from jax.experimental import pallas as pl
from jax.experimental.pallas import tpu as pltpu
from jax.sharding import PartitionSpec as P

D = 2048
epsilon = 1e-06
LOW = -1e30
TINY = 1e-30
STEPS = 32767.0
DEPTH = 3
LAST = 3
AHEAD = 1
END = 2
LANES = 128
REQ_LANE = 64
WIDTH = 4


def kernel(
    cfg,
    aim_hbm,
    deal_hbm,
    lens_hbm,
    gain_hbm,
    hid_hbm,
    w_ref,
    out_ref,
    lens_ref,
    aim_ref,
    deal_ref,
    gain_ref,
    hid_ref,
    gains,
    ints_all,
    ints_cols,
    mate_hid,
    raw,
    split_rows,
    chip_scale,
    ratio,
    sq_all,
    msq_all,
    nrm,
    wbuf,
    sbuf,
    rbuf,
    xbuf,
    ybuf,
    zsend,
    zrecv,
    wmate,
    sown,
    rown,
    zown_send,
    zown,
    own_ratio,
    m_acc,
    t_acc,
    g_acc,
    p_acc,
    st1,
    st2,
    fin,
    pick,
    asked_rows,
    fixed,
    once_send,
    x_recv,
    s_recv,
    i_recv,
    q_recv,
    h_recv,
    f_recv,
    r_recv,
    wl_sem,
    w_recv,
    y_recv,
    z_recv,
    own_recv,
    ya_recv,
    za_recv,
    a_recv,
    b_recv,
    c_recv,
    last_recv,
):
    V, rows, tokens, feats, slab, quarter, cn, n, mb, mb_late, reqs = cfg
    v = lax.axis_index("vocab")
    w = lax.axis_index("width")
    lo = lax.rem(w, 2)
    hi = w // 2
    mate = w + 1 - 2 * lo
    far = w + 2 - 4 * hi
    bw = tokens // WIDTH
    x_send, i_send, q_send, h_send, f_send, r_send = [once_send.at[k] for k in range(6)]
    w_send, y_send, z_send, ya_send, a_send, b_send, s_send, own_send, zo_send, c_send = [
        once_send.at[k] for k in range(6, 16)
    ]
    plain = n - LAST
    depth = min(DEPTH, plain)
    pair = END * rows
    pairs = V // END
    last_pair = pairs - 1 - v // END

    def rcopy(src, dst, ss, rs, where):
        return pltpu.make_async_remote_copy(
            src_ref=src,
            dst_ref=dst,
            send_sem=ss,
            recv_sem=rs,
            device_id=where,
            device_id_type=pl.DeviceIdType.MESH,
        )

    def drained(ref, sem):
        rcopy(ref, ref, sem, x_recv, (v, mate)).wait_send()

    def landed(ref, sem):
        rcopy(ref, ref, x_send, sem, (v, mate)).wait_recv()

    bits = [1 << b for b in range(V.bit_length() - 1)]
    ones = [lax.rem(v // bit, 2) * bit for bit in bits]

    def flipped(d):
        other = 0
        for bit, one in zip(bits, ones):
            if isinstance(d, int):
                other = other + (bit - one if d & bit else one)
            else:
                other = other + lax.rem(one // bit + d // bit, 2) * bit
        return other

    def each(first, last):
        def run(step):
            if last - first > 2 * LANES // WIDTH:
                pl.loop(first, last)(step)
            else:
                for k in range(first, last):
                    step(k)

        return run

    def vpeer(d):
        return flipped(d)

    def vsource(d):
        return flipped(d)

    def wpeer(d):
        return lax.rem(w + d, WIDTH)

    def wsource(d):
        return lax.rem(w + WIDTH - d, WIDTH)

    def wcols(k, is_keep, dev):
        dev_far = dev + 2 - 4 * (dev // 2)
        q = dev if is_keep else dev_far
        base = k - n if is_keep else k
        return pl.ds(pl.multiple_of(q * quarter + base * cn, LANES), cn)

    own_half = pl.ds(pl.multiple_of(lo * feats, LANES), feats)
    mate_half = pl.ds(pl.multiple_of((1 - lo) * feats, LANES), feats)

    def wlocal(k, is_keep, sem):
        return pltpu.make_async_copy(
            w_ref.at[:, wcols(k, is_keep, w)], wbuf.at[k, own_half, :], wl_sem.at[sem]
        )

    def wloaded(part, sem):
        pltpu.make_async_copy(part, part, wl_sem.at[sem]).wait()

    def wremote(k, is_keep):
        return rcopy(
            w_ref.at[:, wcols(k, is_keep, mate)],
            wbuf.at[k, own_half, :],
            w_send,
            w_recv.at[lax.rem(k, n)],
            (v, mate),
        )

    def wwait(k, is_keep):
        rcopy(
            w_ref.at[:, wcols(k, is_keep, mate)],
            wbuf.at[k, mate_half, :],
            w_send,
            w_recv.at[lax.rem(k, n)],
            (v, mate),
        ).wait_recv()

    barrier = pltpu.get_barrier_semaphore()

    @each(1, WIDTH)
    def _(d):
        pl.semaphore_signal(
            barrier, inc=1, device_id=(v, wpeer(d)), device_id_type=pl.DeviceIdType.MESH
        )

    @each(1, V)
    def _(d):
        pl.semaphore_signal(
            barrier, inc=1, device_id=(vpeer(d), w), device_id_type=pl.DeviceIdType.MESH
        )

    loads = [
        pltpu.make_async_copy(source, there, once_send.at[k])
        for k, (source, there) in enumerate(
            (
                (hid_hbm, hid_ref),
                (gain_hbm, gain_ref),
                (aim_hbm, aim_ref),
                (deal_hbm, deal_ref),
                (lens_hbm, lens_ref),
            )
        )
    ]
    for load in loads:
        load.start()

    mate_first = pltpu.make_async_copy(w_ref.at[:, wcols(0, False, mate)], wmate, wl_sem.at[3])
    wlocal(0, False, 0).start()
    mate_first.start()

    @pl.loop(1, n)
    def _(k):
        wlocal(k, False, 1).start()

    late = tokens - rows
    groups = feats // LANES
    ratio[pl.ds(rows, late), :] = jnp.ones((late, LANES), jnp.float32)
    m_acc[...] = jnp.full((tokens, LANES), LOW, jnp.float32)
    t_acc[...] = jnp.zeros((tokens, LANES), jnp.float32)
    g_acc[...] = jnp.zeros((tokens, LANES), jnp.float32)
    p_acc[...] = jnp.zeros((tokens, LANES), jnp.float32)

    def slot(d):
        return pl.ds(pl.multiple_of(d * rows, 16), rows)

    def hcopy(d):
        return rcopy(hid_ref, raw.at[slot(d), own_half], h_send, h_recv.at[d], (vpeer(d), w))

    def squares(x):
        return jnp.sum(x * x, axis=1, keepdims=True)

    def to_row(column, wide):
        height = column.shape[0]
        there = lax.broadcasted_iota(jnp.int32, (height, wide), 1)
        here = lax.broadcasted_iota(jnp.int32, (height, wide), 0)
        return jnp.sum(jnp.where(there == here, column, 0.0), axis=0, keepdims=True)

    def to_column(row, height):
        wide = row.shape[1]
        there = lax.broadcasted_iota(jnp.int32, (height, wide), 1)
        here = lax.broadcasted_iota(jnp.int32, (height, wide), 0)
        return jnp.sum(jnp.where(there == here, row, 0.0), axis=1, keepdims=True)

    for load in loads:
        load.wait()
    gains[...] = gain_ref[...].astype(jnp.float32)
    x = hid_ref[...].astype(jnp.float32)
    sq = squares(x)
    sq_all[w] = to_row(sq, LANES)
    for g in range(groups):
        column = pl.ds(pl.multiple_of(lo * feats + g * LANES, LANES), LANES)
        scaled = x[:, g * LANES : (g + 1) * LANES] * gains[pl.ds(w * groups + g, 1), :]
        upper = scaled.astype(jnp.bfloat16)
        split_rows[0:rows, column] = upper
        split_rows[rows : 2 * rows, column] = (scaled - upper.astype(jnp.float32)).astype(
            jnp.bfloat16
        )
    ints_all[w] = jnp.zeros(ints_all.shape[1:], jnp.int32)
    ints_all[w, 0:1, 0:bw] = aim_ref[...]
    ints_all[w, 1:2, 0:bw] = deal_ref[...]
    def lanes_peak(z):
        peak = jnp.max(jnp.abs(z), axis=0, keepdims=True)
        parts = [peak[:, g * LANES : (g + 1) * LANES] for g in range(cn // LANES)]
        return functools.reduce(jnp.maximum, parts)

    def quantized(z, rate):
        for g in range(cn // LANES):
            part = slice(g * LANES, (g + 1) * LANES)
            yield part, jnp.round(z[:, part] * rate).astype(jnp.int32).astype(jnp.int16)

    def folded(both, scale):
        return (both[0:rows] + both[rows : 2 * rows]) * scale

    core_scale = lax.rsqrt(sq * (1.0 / feats) + epsilon)
    wlocal(0, False, 0).wait()
    mate_first.wait()
    for k, weights in enumerate((wbuf[0, own_half, :], wmate[...])):
        z = folded(
            jnp.dot(split_rows[:, own_half], weights, preferred_element_type=jnp.float32),
            core_scale,
        )
        peak = jnp.maximum(TINY, lanes_peak(z))
        zown_send[k] = peak * (1.0 / STEPS)
        for part, value in quantized(z, STEPS / peak):
            sown[k, :, part] = value
    pl.semaphore_wait(barrier, WIDTH - 1 + V - 1)

    def xcopy():
        return rcopy(hid_ref, mate_hid, x_send, x_recv, (v, mate))

    def icopy(d, dev):
        return rcopy(ints_all.at[w], ints_all.at[dev], i_send, i_recv, (v, wpeer(d)))

    across = far + 1 - 2 * lo

    def scopy(half):
        return rcopy(
            split_rows.at[:, half], split_rows.at[:, half], s_send, s_recv, (v, mate)
        )

    def qstart(there, sem):
        rcopy(sq_all.at[w], sq_all.at[w], q_send, q_recv.at[sem], (v, there)).start()

    def owncopy(k, there):
        return rcopy(sown.at[k], rown.at[lo], own_send, own_recv.at[0], (v, there))

    def zocopy(k, there):
        return rcopy(zown_send.at[k], zown.at[lo], zo_send, own_recv.at[1], (v, there))

    for k, there in enumerate((far, across)):
        owncopy(k, there).start()
        zocopy(k, there).start()
    scopy(own_half).start()
    qstart(mate, 0)
    wremote(1, False).start()
    qstart(far, 1)
    qstart(across, 1)

    @pl.loop(2, DEPTH)
    def _(k):
        wremote(k, False).start()

    xcopy().start()

    @each(1, V)
    def _(d):
        hcopy(V - d).start()

    @pl.loop(DEPTH, n)
    def _(k):
        wremote(k, False).start()

    wremote(0, False).start()

    @pl.loop(1, WIDTH)
    def _(d):
        icopy(d, w).start()

    landed(sq_all.at[mate], q_recv.at[0])
    chip_sq = sq + to_column(sq_all[mate], rows)
    chip_scale[...] = jnp.broadcast_to(
        lax.rsqrt(chip_sq * (1.0 / (2 * feats)) + epsilon), (rows, LANES)
    )
    scopy(mate_half).wait_recv()

    def vspan(dev):
        return pl.ds(pl.multiple_of(dev * rows, 16), rows)

    def normalize():
        landed(sq_all.at[0:2], q_recv.at[1])
        xcopy().wait_recv()
        total_sq = sq_all[0] + sq_all[1] + sq_all[2] + sq_all[3]
        mean_row = total_sq * (1.0 / D)
        msq_all[v] = mean_row
        mean_sq = to_column(mean_row, rows)
        scale = lax.rsqrt(mean_sq + epsilon)
        far_sq = to_column(sq_all[far] + sq_all[across], rows)
        far_scale = lax.rsqrt(far_sq * (1.0 / (2 * feats)) + epsilon)
        ratio[0:rows, :] = jnp.broadcast_to(scale / far_scale, (rows, LANES))
        for core, dev in ((lo, far), (1 - lo, across)):
            dev_sq = to_column(sq_all[dev], rows)
            dev_scale = lax.rsqrt(dev_sq * (1.0 / feats) + epsilon)
            own_ratio[core] = jnp.broadcast_to(scale / dev_scale, (rows, LANES))
        for half, dev, source in ((lo, w, hid_ref), (1 - lo, mate, mate_hid)):
            for g in range(groups):
                column = pl.ds(pl.multiple_of(half * feats + g * LANES, LANES), LANES)
                value = source[:, g * LANES : (g + 1) * LANES].astype(jnp.float32)
                nrm[0:rows, column] = (
                    value * scale * gains[pl.ds(dev * groups + g, 1), :]
                ).astype(jnp.bfloat16)

    def fcopy(d, half):
        part = raw.at[slot(d), half]
        return rcopy(part, part, f_send, f_recv, (v, mate))

    def rmscopy(d, dev):
        return rcopy(msq_all.at[v], msq_all.at[dev], r_send, r_recv, (vpeer(d), w))

    def ycopy(i):
        part = pl.ds(rows, late)
        return rcopy(
            sbuf.at[i, part, :], rbuf.at[i, part, :], y_send, y_recv.at[i], (v, far)
        )

    def yacopy(i):
        part = pl.ds(0, rows)
        return rcopy(
            sbuf.at[i, part, :], rbuf.at[i, part, :], ya_send, ya_recv, (v, far)
        )

    def zcopy(k):
        return rcopy(zsend.at[k], zrecv.at[k], z_send, z_recv.at[k - n], (v, far))

    def zacopy(k):
        return rcopy(zsend.at[k], zrecv.at[k], z_send, za_recv, (v, far))

    def yblock(c, d, sem):
        return rcopy(sbuf.at[c, slot(d), :], rbuf.at[c, slot(d), :], y_send, sem, (v, far))

    def start_block(d):
        @pl.loop(plain, n)
        def _(c):
            yblock(c, d, h_recv.at[d]).start()

    def wait_block(d):
        landed(rbuf.at[pl.ds(plain, LAST), slot(d), :], h_recv.at[d])

    def ystart(i):
        zcopy(n + i).start()
        ycopy(i).start()

    def yarrive(i):
        zcopy(n + i).wait_recv()

    def quantize(i, span, rate, z):
        for part, value in quantized(z, rate):
            sbuf[i, span, part] = value

    def first_dot(i):
        wwait(i, False)
        z = folded(
            jnp.dot(split_rows[...], wbuf[i], preferred_element_type=jnp.float32),
            chip_scale[:, 0:1],
        )
        peak = jnp.maximum(TINY, lanes_peak(z))
        zsend[i] = peak * (1.0 / STEPS)
        quantize(i, pl.ds(0, rows), STEPS / peak, z)
        zacopy(i).start()
        yacopy(i).start()

    def add_own():
        for core in range(2):
            scale = own_ratio[core] * zown[core]
            for g in range(cn // LANES):
                part = slice(g * LANES, (g + 1) * LANES)
                xbuf[0, 0:rows, part] += rown[core, :, part].astype(jnp.int32).astype(jnp.float32) * scale

    def send_dot(i):
        def multiply(r, peak):
            span = pl.ds(pl.multiple_of(rows + r * mb_late, 16), mb_late)
            z = jnp.dot(nrm[span, :], wbuf[i], preferred_element_type=jnp.float32)
            ybuf[span, :] = z
            return jnp.maximum(peak, lanes_peak(z))

        peak = lax.fori_loop(
            0, late // mb_late, multiply, jnp.full((1, LANES), TINY, jnp.float32)
        )
        zsend[n + i] = peak * (1.0 / STEPS)
        rate = STEPS / peak

        @pl.loop(1, V)
        def _(r):
            quantize(i, slot(r), rate, ybuf[slot(r), :])

    def keep_dot(i, place):
        wwait(n + i, True)

        @pl.loop(0, tokens // mb)
        def _(r):
            span = pl.ds(pl.multiple_of(r * mb, 16), mb)
            xbuf[place, span, :] = jnp.dot(
                nrm[span, :], wbuf[n + i], preferred_element_type=jnp.float32
            )

        @pl.when(i == 0)
        def _():
            add_own()

    rb = rows
    first_column = v * slab + w * quarter

    def stats(i):
        @pl.loop(0, V)
        def _(r):
            block_stats(i, r, 0)

    def block_stats(i, r, kept):
        held = slot(r)
        span = vspan(vsource(r))
        late_z = n * ((r + V - 1) // V) + i
        target = ints_cols[span, 0:1]
        factor = zrecv[late_z] * ratio[held, :]
        lane = lax.broadcasted_iota(jnp.int32, (rb, LANES), 1)
        aim = jnp.broadcast_to(target, (rb, LANES)) - lane - (first_column + i * cn)
        xs = [
            xbuf[kept, held, g * LANES : (g + 1) * LANES]
            + rbuf[i, held, g * LANES : (g + 1) * LANES].astype(jnp.int32).astype(jnp.float32)
            * factor
            for g in range(cn // LANES)
        ]
        m_old = m_acc[span, :]
        m_new = functools.reduce(jnp.maximum, xs, m_old)
        decay = jnp.exp(m_old - m_new)
        t = t_acc[span, :] * decay
        g_ = g_acc[span, :] * decay
        p = p_acc[span, :]
        for g, z in enumerate(xs):
            e = jnp.exp(z - m_new)
            t = t + e
            g_ = g_ + e * z
            p = p + jnp.where(aim == g * LANES, z, 0.0)
        m_acc[span, :] = m_new
        t_acc[span, :] = t
        g_acc[span, :] = g_
        p_acc[span, :] = p

    def relay(d):
        hcopy(d).wait_recv()
        fcopy(d, own_half).start()

    head = min(3, n)
    wloaded(wbuf.at[1:n, own_half, :], 1)

    @pl.loop(1, head)
    def _(i):
        first_dot(i)

    normalize()

    @each(1, V)
    def _(d):
        rmscopy(d, v).start()

    turns = min(n - head, V - 2)

    @pl.loop(0, turns)
    def _(i):
        first_dot(head + i)
        relay(V - 1 - i)

    @pl.loop(head + turns, n)
    def _(i):
        first_dot(i)

    wwait(0, False)

    @pl.loop(1 + turns, V)
    def _(d):
        relay(V - d)

    landed(msq_all.at[0 : V - 1], r_recv)
    landed(raw.at[pl.ds(rows, late), mate_half], f_recv)

    @pl.loop(1, V)
    def _(d):
        scale = lax.rsqrt(to_column(msq_all[vsource(d)], rows) + epsilon)
        for g in range(2 * groups):
            column = slice(g * LANES, (g + 1) * LANES)
            gain_row = gains[pl.ds((w - lo) * groups + g, 1), :]
            nrm[slot(d), column] = (
                raw[slot(d), column].astype(jnp.float32) * scale * gain_row
            ).astype(jnp.bfloat16)

    @pl.loop(0, depth)
    def _(i):
        send_dot(i)
        ystart(i)

    @pl.loop(0, n)
    def _(k):
        wremote(n + k, True).start()
        wlocal(n + k, True, 2).start()

    def padded(block):
        return jnp.concatenate([block, jnp.zeros((LANES - pair, LANES), jnp.float32)], axis=0)

    landed(ints_all.at[0 : WIDTH - 1], i_recv)

    for q in range(WIDTH):
        columns = [
            jnp.broadcast_to(to_column(ints_all[q, k : k + 1, :].astype(jnp.float32), bw), (bw, LANES))
            for k in range(2)
        ]
        pick_lane = lax.broadcasted_iota(jnp.int32, (bw, LANES), 1)
        ints_cols[q * bw : (q + 1) * bw, :] = jnp.where(
            pick_lane == 0, columns[0], columns[1]
        ).astype(jnp.int32)

    r_row = lax.broadcasted_iota(jnp.int32, (1, LANES), 1)
    ends = jnp.zeros((1, LANES), jnp.int32)
    counts = jnp.ones((1, LANES), jnp.int32)
    for r in range(reqs):
        ends = ends + jnp.where(r_row >= REQ_LANE + r, lens_ref[r], 0)
        counts = jnp.where(r_row == REQ_LANE + r, lens_ref[r], counts)
    asked = (r_row >= REQ_LANE) & (r_row < REQ_LANE + reqs)
    starts = jnp.where(asked, ends - counts, tokens).astype(jnp.float32)
    ends = ends.astype(jnp.float32)
    counts = counts.astype(jnp.float32)
    place = ints_cols[:, 1:2].astype(jnp.float32)
    spot = jnp.where(r_row < rows, v * rows + r_row, tokens).astype(jnp.float32)
    member = (place >= starts) & (place < ends)
    chosen = jnp.where(member | (place == spot), 1.0, 0.0)
    for k in range(pairs):
        part = padded(chosen[k * pair : (k + 1) * pair])
        span = slice(k * LANES, (k + 1) * LANES)
        pick[span, :] = part
        asked_rows[:, span] = jnp.transpose(part)[REQ_LANE : REQ_LANE + reqs]
    rms = jnp.concatenate(
        [to_column(jnp.sqrt(msq_all[q] + epsilon), rows) for q in range(V)], axis=0
    )
    fixed[0:1, :] = counts
    fixed[1:2, :] = jnp.sum(jnp.where(member, rms, 0.0), axis=0, keepdims=True) / counts

    wloaded(wbuf.at[n : 2 * n, own_half, :], 2)
    landed(rbuf.at[1:n, 0:rows, :], ya_recv)
    landed(zrecv.at[1:n], za_recv)
    landed(rown, own_recv.at[0])
    landed(zown, own_recv.at[1])
    rbuf[0, 0:rows, :] = jnp.zeros((rows, cn), jnp.int16)
    zrecv[0] = jnp.zeros((1, LANES), jnp.float32)

    def finished(i):
        yarrive(i)
        ycopy(i).wait_recv()

    @pl.loop(0, plain - depth)
    def _(i):
        keep_dot(i, 0)
        send_dot(i + depth)
        finished(i)
        ystart(i + depth)
        stats(i)

    @pl.loop(plain, n)
    def _(c):
        send_dot(c)
        zcopy(n + c).start()

    @pl.loop(1, 1 + DEPTH)
    def _(d):
        start_block(d)

    @pl.loop(plain - depth, plain)
    def _(i):
        keep_dot(i, 0)
        finished(i)
        stats(i)

    def block_total(d):
        @pl.loop(plain, n)
        def _(c):
            block_stats(c, d, 1 + c - plain)

    @pl.loop(plain, n)
    def _(c):
        keep_dot(c, 1 + c - plain)
        yarrive(c)

    block_total(0)

    @pl.loop(1, V - 1 - END)
    def _(d):
        wait_block(d)

        @pl.when(d + DEPTH < V - 1)
        def _():
            start_block(d + DEPTH)

        block_total(d)

    def last_piece(k):
        return yblock(plain + k, V - 1, last_recv.at[k])

    wait_block(V - 1 - END)
    for k in range(AHEAD):
        last_piece(k).start()
    block_total(V - 1 - END)

    def columns_of(span, height):
        m = m_acc[span, :]
        top = jnp.max(m, axis=1, keepdims=True)
        share = jnp.exp(m - top)
        tot = jnp.sum(t_acc[span, :] * share, axis=1, keepdims=True)
        wei = jnp.sum(g_acc[span, :] * share, axis=1, keepdims=True)
        pic = jnp.sum(p_acc[span, :], axis=1, keepdims=True)
        lane = lax.broadcasted_iota(jnp.int32, (height, LANES), 1)
        return jnp.where(
            lane == 0, top, jnp.where(lane == 1, tot, jnp.where(lane == 2, wei, pic))
        )

    lane = lax.broadcasted_iota(jnp.int32, (tokens, LANES), 1)
    line = lax.broadcasted_iota(jnp.int32, (tokens, LANES), 0)
    open_row = (line >= last_pair * pair) & (line < (last_pair + 1) * pair)
    table = jnp.where(
        open_row, jnp.where(lane == 0, LOW, 0.0), columns_of(slice(0, tokens), tokens)
    )
    for k in range(pairs):
        part = padded(table[k * pair : (k + 1) * pair])
        st1[w, :, k * LANES : (k + 1) * LANES] = jnp.transpose(part)[0:4]

    def acopy(d, dev):
        return rcopy(st1.at[w], st1.at[dev], a_send, a_recv, (v, wpeer(d)))

    def bcopy(d, dev):
        return rcopy(st2.at[v], st2.at[dev], b_send, b_recv, (vpeer(d), w))

    def joined(parts):
        top = functools.reduce(jnp.maximum, [s[0:1, :] for s in parts])
        tot = jnp.zeros_like(top)
        wei = jnp.zeros_like(top)
        pic = jnp.zeros_like(top)
        for s in parts:
            share = jnp.exp(s[0:1, :] - top)
            tot = tot + s[1:2, :] * share
            wei = wei + s[2:3, :] * share
            pic = pic + s[3:4, :]
        return top, tot, wei, pic

    @each(1, WIDTH)
    def _(d):
        acopy(d, w).start()

    for k in range(AHEAD, LAST):
        last_piece(k).start()
    wait_block(V - END)
    block_total(V - END)

    def last_stats(k):
        last_piece(k).wait_recv()
        block_stats(plain + k, V - 1, 1 + k)

    for k in range(AHEAD):
        last_stats(k)

    landed(st1.at[0 : WIDTH - 1], a_recv)

    sub = lax.broadcasted_iota(jnp.int32, (4, pairs * LANES), 0)
    top, tot, wei, pic = joined([st1[q] for q in range(WIDTH)])
    st2[v] = jnp.where(sub == 0, top, jnp.where(sub == 1, tot, jnp.where(sub == 2, wei, pic)))

    @each(1, V)
    def _(d):
        bcopy(d, v).start()

    for k in range(AHEAD, LAST):
        last_stats(k)
    me = v * WIDTH + w
    span = pl.ds(pl.multiple_of(last_pair * pair, 16), pair)
    fin[me] = jnp.transpose(padded(columns_of(span, pair)))[0:4]

    def ccopy(k):
        return rcopy(
            fin.at[me], fin.at[me], c_send, c_recv, (flipped(k // WIDTH), lax.rem(w + k, WIDTH))
        )

    @each(1, V * WIDTH)
    def _(k):
        ccopy(V * WIDTH - k).start()

    xcopy().wait_send()
    drained(sq_all.at[0 : WIDTH - 1], q_send)
    scopy(own_half).wait_send()
    drained(ints_all.at[0 : WIDTH - 1], i_send)
    drained(msq_all.at[0 : V - 1], r_send)
    drained(raw.at[pl.ds(rows, late), own_half], h_send)
    drained(raw.at[pl.ds(rows, late), own_half], f_send)
    drained(wbuf.at[:, own_half, :], w_send)
    drained(sbuf.at[:, pl.ds(rows, late), :], y_send)
    drained(sbuf.at[1:n, 0:rows, :], ya_send)
    drained(zsend.at[pl.ds(1, 2 * n - 1)], z_send)
    drained(sown, own_send)
    drained(zown_send, zo_send)
    landed(st2.at[0 : V - 1], b_recv)
    early = joined([st2[q] for q in range(V)])
    landed(fin.at[0 : V * WIDTH - 1], c_recv)
    parts = [jnp.concatenate(early, axis=0)]
    for q in range(END * WIDTH):
        parts.append(
            jnp.concatenate(
                [fin[(pairs - 1 - k) * END * WIDTH + q] for k in range(pairs)], axis=1
            )
        )
    largest, tot, wei, pic = joined(parts)
    log_total = jnp.log(tot)
    wide = pairs * LANES
    place = lax.broadcasted_iota(jnp.int32, (8, wide), 0)
    used = lax.rem(lax.broadcasted_iota(jnp.int32, (1, wide), 1), LANES) < pair
    spread = jnp.zeros((8, wide), jnp.float32)
    for k, rest in enumerate(
        (pic - largest - log_total, largest + log_total - wei / tot)
    ):
        rest = jnp.where(used, rest, 0.0)
        for part in range(3):
            upper = rest.astype(jnp.bfloat16).astype(jnp.float32)
            spread = jnp.where(place == 2 * part + k, upper, spread)
            rest = rest - upper
    dealt = jnp.dot(
        spread.astype(jnp.bfloat16),
        pick[...].astype(jnp.bfloat16),
        preferred_element_type=jnp.float32,
    )
    sums = dealt[0:2] + dealt[2:4] + dealt[4:6]
    out_ref[0:1, :] = sums[0:1]
    out_ref[4:6, :] = sums / fixed[0:1, :]
    out_ref[6:7, :] = fixed[1:2, :]
    highest = jnp.max(jnp.where(asked_rows[...] > 0.5, largest, LOW), axis=1, keepdims=True)
    there = lax.broadcasted_iota(jnp.int32, (reqs, LANES), 1)
    here = lax.broadcasted_iota(jnp.int32, (reqs, LANES), 0)
    out_ref[7:8, :] = jnp.sum(
        jnp.where(there == here + REQ_LANE, highest, 0.0), axis=0, keepdims=True
    )
    drained(st1.at[0 : WIDTH - 1], a_send)
    drained(st2.at[0 : V - 1], b_send)
    drained(fin.at[0 : V * WIDTH - 1], c_send)


def finish(rows, reqs, res_ref, tok_ref, stat_ref):
    tok_ref[...] = res_ref[0:1, 0:rows]
    stat_ref[...] = res_ref[4:8, REQ_LANE : REQ_LANE + reqs]


def body(hidden, norm_gain, head_weight, lengths, deal, targets):
    rows, feats = hidden.shape
    V = lax.axis_size("vocab")
    tokens = rows * V
    slab = head_weight.shape[1]
    quarter = slab // WIDTH
    cn = next(c for c in (512, 256, 128) if quarter % c == 0)
    n = quarter // cn
    mb = next(c for c in (384, 256, 192, 128, 64, 48, 16) if tokens % c == 0)
    reqs = lengths.shape[0]
    bw = tokens // WIDTH

    gain = norm_gain.reshape(-1, LANES)
    bwp = -(-bw // LANES) * LANES
    late = tokens - rows
    mb_late = next(c for c in (336, 192, 144, 96, 48, 16) if late % c == 0)

    cfg = (V, rows, tokens, feats, slab, quarter, cn, n, mb, mb_late, reqs)
    f32, bf16 = jnp.float32, jnp.bfloat16
    dma = pltpu.SemaphoreType.DMA
    vmem = pl.BlockSpec(memory_space=pltpu.VMEM)
    hbm = pl.BlockSpec(memory_space=pltpu.HBM)
    res = pl.pallas_call(
        functools.partial(kernel, cfg),
        out_shape=jax.ShapeDtypeStruct((8, LANES), f32),
        in_specs=[hbm] * 6,
        out_specs=vmem,
        scratch_shapes=[
            pltpu.SMEM((reqs,), jnp.int32),
            pltpu.VMEM((1, bw), jnp.int32),
            pltpu.VMEM((1, bw), jnp.int32),
            pltpu.VMEM((D // LANES, LANES), bf16),
            pltpu.VMEM((rows, feats), bf16),
            pltpu.VMEM((D // LANES, LANES), f32),
            pltpu.VMEM((WIDTH, 2, bwp), jnp.int32),
            pltpu.VMEM((tokens, LANES), jnp.int32),
            pltpu.VMEM((rows, feats), bf16),
            pltpu.VMEM((tokens, 2 * feats), bf16),
            pltpu.VMEM((2 * rows, 2 * feats), bf16),
            pltpu.VMEM((rows, LANES), f32),
            pltpu.VMEM((tokens, LANES), f32),
            pltpu.VMEM((WIDTH, 1, LANES), f32),
            pltpu.VMEM((V, 1, LANES), f32),
            pltpu.VMEM((tokens, 2 * feats), bf16),
            pltpu.VMEM((2 * n, 2 * feats, cn), bf16),
            pltpu.VMEM((n, tokens, cn), jnp.int16),
            pltpu.VMEM((n, tokens, cn), jnp.int16),
            pltpu.VMEM((LAST + 1, tokens, cn), f32),
            pltpu.VMEM((tokens, cn), f32),
            pltpu.VMEM((2 * n, 1, LANES), f32),
            pltpu.VMEM((2 * n, 1, LANES), f32),
            pltpu.VMEM((feats, cn), bf16),
            pltpu.VMEM((2, rows, cn), jnp.int16),
            pltpu.VMEM((2, rows, cn), jnp.int16),
            pltpu.VMEM((2, 1, LANES), f32),
            pltpu.VMEM((2, 1, LANES), f32),
            pltpu.VMEM((2, rows, LANES), f32),
            pltpu.VMEM((tokens, LANES), f32),
            pltpu.VMEM((tokens, LANES), f32),
            pltpu.VMEM((tokens, LANES), f32),
            pltpu.VMEM((tokens, LANES), f32),
            pltpu.VMEM((WIDTH, 4, V // END * LANES), f32),
            pltpu.VMEM((V, 4, V // END * LANES), f32),
            pltpu.VMEM((V * WIDTH, 4, LANES), f32),
            pltpu.VMEM((V // END * LANES, LANES), f32),
            pltpu.VMEM((reqs, V // END * LANES), f32),
            pltpu.VMEM((8, LANES), f32),
            dma((16,)),
            dma,
            dma,
            dma,
            dma((2,)),
            dma((V,)),
            dma,
            dma,
            dma((4,)),
            dma((n,)),
            dma((n,)),
            dma((n,)),
            dma((2,)),
            dma,
            dma,
            dma,
            dma,
            dma,
            dma((LAST,)),
        ],
        compiler_params=pltpu.CompilerParams(
            collective_id=0, has_side_effects=True, vmem_limit_bytes=(50 if V <= 8 else 58) << 20
        ),
    )(*[
        pltpu.with_memory_space_constraint(x, pltpu.HBM)
        for x in (targets[None], deal[None], lengths, gain, hidden, head_weight)
    ])
    tok, stat = pl.pallas_call(
        functools.partial(finish, rows, reqs),
        out_shape=(
            jax.ShapeDtypeStruct((1, rows), f32),
            jax.ShapeDtypeStruct((4, reqs), f32),
        ),
        in_specs=[vmem],
        out_specs=(vmem, vmem),
        compiler_params=pltpu.CompilerParams(vmem_limit_bytes=4 << 20),
    )(res)
    return tok[0], stat


def solution(mesh):
    return jax.shard_map(
        body,
        mesh=mesh,
        in_specs=(P("vocab", "width"), P(), P("width", "vocab"), P(), P("width"), P("width")),
        out_specs=(P("vocab"), P()),
        check_vma=False,
    )
```

```python
import functools

import jax
import jax.numpy as jnp
from jax import lax
from jax.experimental import pallas as pl
from jax.experimental.pallas import tpu as pltpu
from jax.sharding import PartitionSpec as P

D = 2048
epsilon = 1e-06
LOW = -1e30
TINY = 1e-30
STEPS = 32767.0
DEPTH = 3
LAST = 4
AHEAD = 1
END = 2
LANES = 128
REQ_LANE = 64
WIDTH = 4


def kernel(
    cfg,
    aim_hbm,
    deal_hbm,
    lens_hbm,
    gain_hbm,
    hid_hbm,
    w_ref,
    out_ref,
    lens_ref,
    aim_ref,
    deal_ref,
    gain_ref,
    hid_ref,
    gains,
    ints_all,
    ints_cols,
    mate_hid,
    raw,
    split_rows,
    chip_scale,
    ratio,
    sq_all,
    msq_all,
    nrm,
    wbuf,
    sbuf,
    rbuf,
    xbuf,
    ybuf,
    zsend,
    zrecv,
    wmate,
    sown,
    rown,
    zown_send,
    zown,
    own_ratio,
    m_acc,
    t_acc,
    g_acc,
    p_acc,
    st1,
    st2,
    fin,
    pick,
    asked_rows,
    fixed,
    once_send,
    x_recv,
    s_recv,
    i_recv,
    q_recv,
    h_recv,
    f_recv,
    r_recv,
    wl_sem,
    w_recv,
    y_recv,
    z_recv,
    own_recv,
    ya_recv,
    za_recv,
    a_recv,
    b_recv,
    c_recv,
    last_recv,
):
    V, rows, tokens, feats, slab, quarter, cn, n, mb, mb_late, reqs = cfg
    v = lax.axis_index("vocab")
    w = lax.axis_index("width")
    lo = lax.rem(w, 2)
    hi = w // 2
    mate = w + 1 - 2 * lo
    far = w + 2 - 4 * hi
    bw = tokens // WIDTH
    x_send, i_send, q_send, h_send, f_send, r_send = [once_send.at[k] for k in range(6)]
    w_send, y_send, z_send, ya_send, a_send, b_send, s_send, own_send, zo_send, c_send = [
        once_send.at[k] for k in range(6, 16)
    ]
    plain = n - LAST
    depth = min(DEPTH, plain)
    pair = END * rows
    pairs = V // END
    last_pair = pairs - 1 - v // END

    def rcopy(src, dst, ss, rs, where):
        return pltpu.make_async_remote_copy(
            src_ref=src,
            dst_ref=dst,
            send_sem=ss,
            recv_sem=rs,
            device_id=where,
            device_id_type=pl.DeviceIdType.MESH,
        )

    def drained(ref, sem):
        rcopy(ref, ref, sem, x_recv, (v, mate)).wait_send()

    def landed(ref, sem):
        rcopy(ref, ref, x_send, sem, (v, mate)).wait_recv()

    bits = [1 << b for b in range(V.bit_length() - 1)]
    ones = [lax.rem(v // bit, 2) * bit for bit in bits]

    def flipped(d):
        other = 0
        for bit, one in zip(bits, ones):
            if isinstance(d, int):
                other = other + (bit - one if d & bit else one)
            else:
                other = other + lax.rem(one // bit + d // bit, 2) * bit
        return other

    def each(first, last):
        def run(step):
            if last - first > 2 * LANES // WIDTH:
                pl.loop(first, last)(step)
            else:
                for k in range(first, last):
                    step(k)

        return run

    def vpeer(d):
        return flipped(d)

    def vsource(d):
        return flipped(d)

    def wpeer(d):
        return lax.rem(w + d, WIDTH)

    def wsource(d):
        return lax.rem(w + WIDTH - d, WIDTH)

    def wcols(k, is_keep, dev):
        dev_far = dev + 2 - 4 * (dev // 2)
        q = dev if is_keep else dev_far
        base = k - n if is_keep else k
        return pl.ds(pl.multiple_of(q * quarter + base * cn, LANES), cn)

    own_half = pl.ds(pl.multiple_of(lo * feats, LANES), feats)
    mate_half = pl.ds(pl.multiple_of((1 - lo) * feats, LANES), feats)

    def wlocal(k, is_keep, sem):
        return pltpu.make_async_copy(
            w_ref.at[:, wcols(k, is_keep, w)], wbuf.at[k, own_half, :], wl_sem.at[sem]
        )

    def wloaded(part, sem):
        pltpu.make_async_copy(part, part, wl_sem.at[sem]).wait()

    def wremote(k, is_keep):
        return rcopy(
            w_ref.at[:, wcols(k, is_keep, mate)],
            wbuf.at[k, own_half, :],
            w_send,
            w_recv.at[lax.rem(k, n)],
            (v, mate),
        )

    def wwait(k, is_keep):
        rcopy(
            w_ref.at[:, wcols(k, is_keep, mate)],
            wbuf.at[k, mate_half, :],
            w_send,
            w_recv.at[lax.rem(k, n)],
            (v, mate),
        ).wait_recv()

    barrier = pltpu.get_barrier_semaphore()

    @each(1, WIDTH)
    def _(d):
        pl.semaphore_signal(
            barrier, inc=1, device_id=(v, wpeer(d)), device_id_type=pl.DeviceIdType.MESH
        )

    @each(1, V)
    def _(d):
        pl.semaphore_signal(
            barrier, inc=1, device_id=(vpeer(d), w), device_id_type=pl.DeviceIdType.MESH
        )

    loads = [
        pltpu.make_async_copy(source, there, once_send.at[k])
        for k, (source, there) in enumerate(
            (
                (hid_hbm, hid_ref),
                (gain_hbm, gain_ref),
                (aim_hbm, aim_ref),
                (deal_hbm, deal_ref),
                (lens_hbm, lens_ref),
            )
        )
    ]
    for load in loads:
        load.start()

    mate_first = pltpu.make_async_copy(w_ref.at[:, wcols(0, False, mate)], wmate, wl_sem.at[3])
    wlocal(0, False, 0).start()
    mate_first.start()

    late = tokens - rows
    groups = feats // LANES
    ratio[pl.ds(rows, late), :] = jnp.ones((late, LANES), jnp.float32)
    m_acc[...] = jnp.full((tokens, LANES), LOW, jnp.float32)
    t_acc[...] = jnp.zeros((tokens, LANES), jnp.float32)
    g_acc[...] = jnp.zeros((tokens, LANES), jnp.float32)
    p_acc[...] = jnp.zeros((tokens, LANES), jnp.float32)

    def slot(d):
        return pl.ds(pl.multiple_of(d * rows, 16), rows)

    def hcopy(d):
        return rcopy(hid_ref, raw.at[slot(d), own_half], h_send, h_recv.at[d], (vpeer(d), w))

    def squares(x):
        return jnp.sum(x * x, axis=1, keepdims=True)

    def to_row(column, wide):
        height = column.shape[0]
        there = lax.broadcasted_iota(jnp.int32, (height, wide), 1)
        here = lax.broadcasted_iota(jnp.int32, (height, wide), 0)
        return jnp.sum(jnp.where(there == here, column, 0.0), axis=0, keepdims=True)

    def to_column(row, height):
        wide = row.shape[1]
        there = lax.broadcasted_iota(jnp.int32, (height, wide), 1)
        here = lax.broadcasted_iota(jnp.int32, (height, wide), 0)
        return jnp.sum(jnp.where(there == here, row, 0.0), axis=1, keepdims=True)

    for load in loads:
        load.wait()
    gains[...] = gain_ref[...].astype(jnp.float32)
    x = hid_ref[...].astype(jnp.float32)
    sq = squares(x)
    sq_all[w] = to_row(sq, LANES)
    for g in range(groups):
        column = pl.ds(pl.multiple_of(lo * feats + g * LANES, LANES), LANES)
        scaled = x[:, g * LANES : (g + 1) * LANES] * gains[pl.ds(w * groups + g, 1), :]
        upper = scaled.astype(jnp.bfloat16)
        split_rows[0:rows, column] = upper
        split_rows[rows : 2 * rows, column] = (scaled - upper.astype(jnp.float32)).astype(
            jnp.bfloat16
        )
    ints_all[w] = jnp.zeros(ints_all.shape[1:], jnp.int32)
    ints_all[w, 0:1, 0:bw] = aim_ref[...]
    ints_all[w, 1:2, 0:bw] = deal_ref[...]
    def lanes_peak(z):
        peak = jnp.max(jnp.abs(z), axis=0, keepdims=True)
        parts = [peak[:, g * LANES : (g + 1) * LANES] for g in range(cn // LANES)]
        return functools.reduce(jnp.maximum, parts)

    def quantized(z, rate):
        for g in range(cn // LANES):
            part = slice(g * LANES, (g + 1) * LANES)
            yield part, jnp.round(z[:, part] * rate).astype(jnp.int32).astype(jnp.int16)

    def folded(both, scale):
        return (both[0:rows] + both[rows : 2 * rows]) * scale

    core_scale = lax.rsqrt(sq * (1.0 / feats) + epsilon)
    wlocal(0, False, 0).wait()
    mate_first.wait()

    @pl.loop(1, n)
    def _(k):
        wlocal(k, False, 1).start()

    for k, weights in enumerate((wbuf[0, own_half, :], wmate[...])):
        z = folded(
            jnp.dot(split_rows[:, own_half], weights, preferred_element_type=jnp.float32),
            core_scale,
        )
        peak = jnp.maximum(TINY, lanes_peak(z))
        zown_send[k] = peak * (1.0 / STEPS)
        for part, value in quantized(z, STEPS / peak):
            sown[k, :, part] = value
    pl.semaphore_wait(barrier, WIDTH - 1 + V - 1)

    def xcopy():
        return rcopy(hid_ref, mate_hid, x_send, x_recv, (v, mate))

    def icopy(d, dev):
        return rcopy(ints_all.at[w], ints_all.at[dev], i_send, i_recv, (v, wpeer(d)))

    across = far + 1 - 2 * lo

    def scopy(half):
        return rcopy(
            split_rows.at[:, half], split_rows.at[:, half], s_send, s_recv, (v, mate)
        )

    def qstart(there, sem):
        rcopy(sq_all.at[w], sq_all.at[w], q_send, q_recv.at[sem], (v, there)).start()

    def owncopy(k, there):
        return rcopy(sown.at[k], rown.at[lo], own_send, own_recv.at[0], (v, there))

    def zocopy(k, there):
        return rcopy(zown_send.at[k], zown.at[lo], zo_send, own_recv.at[1], (v, there))

    for k, there in enumerate((far, across)):
        owncopy(k, there).start()
        zocopy(k, there).start()
    scopy(own_half).start()
    qstart(mate, 0)
    wremote(1, False).start()
    qstart(far, 1)
    qstart(across, 1)

    @pl.loop(2, DEPTH)
    def _(k):
        wremote(k, False).start()

    xcopy().start()

    @each(1, V)
    def _(d):
        hcopy(V - d).start()

    @pl.loop(DEPTH, n)
    def _(k):
        wremote(k, False).start()

    wremote(0, False).start()

    @pl.loop(1, WIDTH)
    def _(d):
        icopy(d, w).start()

    landed(sq_all.at[mate], q_recv.at[0])
    chip_sq = sq + to_column(sq_all[mate], rows)
    chip_scale[...] = jnp.broadcast_to(
        lax.rsqrt(chip_sq * (1.0 / (2 * feats)) + epsilon), (rows, LANES)
    )
    scopy(mate_half).wait_recv()

    def vspan(dev):
        return pl.ds(pl.multiple_of(dev * rows, 16), rows)

    def normalize():
        landed(sq_all.at[0:2], q_recv.at[1])
        xcopy().wait_recv()
        total_sq = sq_all[0] + sq_all[1] + sq_all[2] + sq_all[3]
        mean_row = total_sq * (1.0 / D)
        msq_all[v] = mean_row
        mean_sq = to_column(mean_row, rows)
        scale = lax.rsqrt(mean_sq + epsilon)
        far_sq = to_column(sq_all[far] + sq_all[across], rows)
        far_scale = lax.rsqrt(far_sq * (1.0 / (2 * feats)) + epsilon)
        ratio[0:rows, :] = jnp.broadcast_to(scale / far_scale, (rows, LANES))
        for core, dev in ((lo, far), (1 - lo, across)):
            dev_sq = to_column(sq_all[dev], rows)
            dev_scale = lax.rsqrt(dev_sq * (1.0 / feats) + epsilon)
            own_ratio[core] = jnp.broadcast_to(scale / dev_scale, (rows, LANES))
        for half, dev, source in ((lo, w, hid_ref), (1 - lo, mate, mate_hid)):
            for g in range(groups):
                column = pl.ds(pl.multiple_of(half * feats + g * LANES, LANES), LANES)
                value = source[:, g * LANES : (g + 1) * LANES].astype(jnp.float32)
                nrm[0:rows, column] = (
                    value * scale * gains[pl.ds(dev * groups + g, 1), :]
                ).astype(jnp.bfloat16)

    def fcopy(d, half):
        part = raw.at[slot(d), half]
        return rcopy(part, part, f_send, f_recv, (v, mate))

    def rmscopy(d, dev):
        return rcopy(msq_all.at[v], msq_all.at[dev], r_send, r_recv, (vpeer(d), w))

    def ycopy(i):
        part = pl.ds(rows, late)
        return rcopy(
            sbuf.at[i, part, :], rbuf.at[i, part, :], y_send, y_recv.at[i], (v, far)
        )

    def yacopy(i):
        part = pl.ds(0, rows)
        return rcopy(
            sbuf.at[i, part, :], rbuf.at[i, part, :], ya_send, ya_recv, (v, far)
        )

    def zcopy(k):
        return rcopy(zsend.at[k], zrecv.at[k], z_send, z_recv.at[k - n], (v, far))

    def zacopy(k):
        return rcopy(zsend.at[k], zrecv.at[k], z_send, za_recv, (v, far))

    def yblock(c, d, sem):
        return rcopy(sbuf.at[c, slot(d), :], rbuf.at[c, slot(d), :], y_send, sem, (v, far))

    def start_block(d):
        @pl.loop(plain, n)
        def _(c):
            yblock(c, d, h_recv.at[d]).start()

    def wait_block(d):
        landed(rbuf.at[pl.ds(plain, LAST), slot(d), :], h_recv.at[d])

    def ystart(i):
        zcopy(n + i).start()
        ycopy(i).start()

    def yarrive(i):
        zcopy(n + i).wait_recv()

    def quantize(i, span, rate, z):
        for part, value in quantized(z, rate):
            sbuf[i, span, part] = value

    def first_dot(i):
        wwait(i, False)
        z = folded(
            jnp.dot(split_rows[...], wbuf[i], preferred_element_type=jnp.float32),
            chip_scale[:, 0:1],
        )
        peak = jnp.maximum(TINY, lanes_peak(z))
        zsend[i] = peak * (1.0 / STEPS)
        quantize(i, pl.ds(0, rows), STEPS / peak, z)
        zacopy(i).start()
        yacopy(i).start()

    def add_own():
        for core in range(2):
            scale = own_ratio[core] * zown[core]
            for g in range(cn // LANES):
                part = slice(g * LANES, (g + 1) * LANES)
                xbuf[0, 0:rows, part] += rown[core, :, part].astype(jnp.int32).astype(jnp.float32) * scale

    def send_dot(i):
        def multiply(r, peak):
            span = pl.ds(pl.multiple_of(rows + r * mb_late, 16), mb_late)
            z = jnp.dot(nrm[span, :], wbuf[i], preferred_element_type=jnp.float32)
            ybuf[span, :] = z
            return jnp.maximum(peak, lanes_peak(z))

        peak = lax.fori_loop(
            0, late // mb_late, multiply, jnp.full((1, LANES), TINY, jnp.float32)
        )
        zsend[n + i] = peak * (1.0 / STEPS)
        rate = STEPS / peak

        @pl.loop(1, V)
        def _(r):
            quantize(i, slot(r), rate, ybuf[slot(r), :])

    def keep_dot(i, place):
        wwait(n + i, True)

        @pl.loop(0, tokens // mb)
        def _(r):
            span = pl.ds(pl.multiple_of(r * mb, 16), mb)
            xbuf[place, span, :] = jnp.dot(
                nrm[span, :], wbuf[n + i], preferred_element_type=jnp.float32
            )

        @pl.when(i == 0)
        def _():
            add_own()

    rb = rows
    first_column = v * slab + w * quarter

    def stats(i):
        @pl.loop(0, V)
        def _(r):
            block_stats(i, r, 0)

    def block_stats(i, r, kept):
        held = slot(r)
        span = vspan(vsource(r))
        late_z = n * ((r + V - 1) // V) + i
        target = ints_cols[span, 0:1]
        factor = zrecv[late_z] * ratio[held, :]
        lane = lax.broadcasted_iota(jnp.int32, (rb, LANES), 1)
        aim = jnp.broadcast_to(target, (rb, LANES)) - lane - (first_column + i * cn)
        xs = [
            xbuf[kept, held, g * LANES : (g + 1) * LANES]
            + rbuf[i, held, g * LANES : (g + 1) * LANES].astype(jnp.int32).astype(jnp.float32)
            * factor
            for g in range(cn // LANES)
        ]
        m_old = m_acc[span, :]
        m_new = functools.reduce(jnp.maximum, xs, m_old)
        decay = jnp.exp(m_old - m_new)
        t = t_acc[span, :] * decay
        g_ = g_acc[span, :] * decay
        p = p_acc[span, :]
        for g, z in enumerate(xs):
            e = jnp.exp(z - m_new)
            t = t + e
            g_ = g_ + e * z
            p = p + jnp.where(aim == g * LANES, z, 0.0)
        m_acc[span, :] = m_new
        t_acc[span, :] = t
        g_acc[span, :] = g_
        p_acc[span, :] = p

    def relay(d):
        hcopy(d).wait_recv()
        fcopy(d, own_half).start()

    head = min(3, n)
    wloaded(wbuf.at[1:n, own_half, :], 1)

    @pl.loop(1, head)
    def _(i):
        first_dot(i)

    normalize()

    @each(1, V)
    def _(d):
        rmscopy(d, v).start()

    turns = min(n - head, V - 2)

    @pl.loop(0, turns)
    def _(i):
        first_dot(head + i)
        relay(V - 1 - i)

    @pl.loop(head + turns, n)
    def _(i):
        first_dot(i)

    wwait(0, False)

    @pl.loop(1 + turns, V)
    def _(d):
        relay(V - d)

    landed(msq_all.at[0 : V - 1], r_recv)
    landed(raw.at[pl.ds(rows, late), mate_half], f_recv)

    @pl.loop(1, V)
    def _(d):
        scale = lax.rsqrt(to_column(msq_all[vsource(d)], rows) + epsilon)
        for g in range(2 * groups):
            column = slice(g * LANES, (g + 1) * LANES)
            gain_row = gains[pl.ds((w - lo) * groups + g, 1), :]
            nrm[slot(d), column] = (
                raw[slot(d), column].astype(jnp.float32) * scale * gain_row
            ).astype(jnp.bfloat16)

    @pl.loop(0, depth)
    def _(i):
        send_dot(i)
        ystart(i)

    @pl.loop(0, n)
    def _(k):
        wremote(n + k, True).start()
        wlocal(n + k, True, 2).start()

    def padded(block):
        return jnp.concatenate([block, jnp.zeros((LANES - pair, LANES), jnp.float32)], axis=0)

    landed(ints_all.at[0 : WIDTH - 1], i_recv)

    for q in range(WIDTH):
        columns = [
            jnp.broadcast_to(to_column(ints_all[q, k : k + 1, :].astype(jnp.float32), bw), (bw, LANES))
            for k in range(2)
        ]
        pick_lane = lax.broadcasted_iota(jnp.int32, (bw, LANES), 1)
        ints_cols[q * bw : (q + 1) * bw, :] = jnp.where(
            pick_lane == 0, columns[0], columns[1]
        ).astype(jnp.int32)

    r_row = lax.broadcasted_iota(jnp.int32, (1, LANES), 1)
    ends = jnp.zeros((1, LANES), jnp.int32)
    counts = jnp.ones((1, LANES), jnp.int32)
    for r in range(reqs):
        ends = ends + jnp.where(r_row >= REQ_LANE + r, lens_ref[r], 0)
        counts = jnp.where(r_row == REQ_LANE + r, lens_ref[r], counts)
    asked = (r_row >= REQ_LANE) & (r_row < REQ_LANE + reqs)
    starts = jnp.where(asked, ends - counts, tokens).astype(jnp.float32)
    ends = ends.astype(jnp.float32)
    counts = counts.astype(jnp.float32)
    place = ints_cols[:, 1:2].astype(jnp.float32)
    spot = jnp.where(r_row < rows, v * rows + r_row, tokens).astype(jnp.float32)
    member = (place >= starts) & (place < ends)
    chosen = jnp.where(member | (place == spot), 1.0, 0.0)
    for k in range(pairs):
        part = padded(chosen[k * pair : (k + 1) * pair])
        span = slice(k * LANES, (k + 1) * LANES)
        pick[span, :] = part.astype(jnp.bfloat16)
        asked_rows[:, span] = jnp.transpose(part)[REQ_LANE : REQ_LANE + reqs]
    rms = jnp.concatenate(
        [to_column(jnp.sqrt(msq_all[q] + epsilon), rows) for q in range(V)], axis=0
    )
    fixed[0:1, :] = counts
    fixed[1:2, :] = jnp.sum(jnp.where(member, rms, 0.0), axis=0, keepdims=True) / counts

    wloaded(wbuf.at[n : 2 * n, own_half, :], 2)
    landed(rbuf.at[1:n, 0:rows, :], ya_recv)
    landed(zrecv.at[1:n], za_recv)
    landed(rown, own_recv.at[0])
    landed(zown, own_recv.at[1])
    rbuf[0, 0:rows, :] = jnp.zeros((rows, cn), jnp.int16)
    zrecv[0] = jnp.zeros((1, LANES), jnp.float32)

    def finished(i):
        yarrive(i)
        ycopy(i).wait_recv()

    @pl.loop(0, plain - depth)
    def _(i):
        keep_dot(i, 0)
        send_dot(i + depth)
        finished(i)
        ystart(i + depth)
        stats(i)

    @pl.loop(plain, n)
    def _(c):
        send_dot(c)
        zcopy(n + c).start()

    @pl.loop(1, 1 + DEPTH)
    def _(d):
        start_block(d)

    @pl.loop(plain - depth, plain)
    def _(i):
        keep_dot(i, 0)
        finished(i)
        stats(i)

    def block_total(d):
        @pl.loop(plain, n)
        def _(c):
            block_stats(c, d, 1 + c - plain)

    @pl.loop(plain, n)
    def _(c):
        keep_dot(c, 1 + c - plain)
        yarrive(c)

    block_total(0)

    @pl.loop(1, V - 1 - END)
    def _(d):
        wait_block(d)

        @pl.when(d + DEPTH < V - 1)
        def _():
            start_block(d + DEPTH)

        block_total(d)

    def last_piece(k):
        return yblock(plain + k, V - 1, last_recv.at[k])

    wait_block(V - 1 - END)
    for k in range(AHEAD):
        last_piece(k).start()
    block_total(V - 1 - END)

    def columns_of(span, height):
        m = m_acc[span, :]
        top = jnp.max(m, axis=1, keepdims=True)
        share = jnp.exp(m - top)
        tot = jnp.sum(t_acc[span, :] * share, axis=1, keepdims=True)
        wei = jnp.sum(g_acc[span, :] * share, axis=1, keepdims=True)
        pic = jnp.sum(p_acc[span, :], axis=1, keepdims=True)
        lane = lax.broadcasted_iota(jnp.int32, (height, LANES), 1)
        return jnp.where(
            lane == 0, top, jnp.where(lane == 1, tot, jnp.where(lane == 2, wei, pic))
        )

    lane = lax.broadcasted_iota(jnp.int32, (tokens, LANES), 1)
    line = lax.broadcasted_iota(jnp.int32, (tokens, LANES), 0)
    open_row = (line >= last_pair * pair) & (line < (last_pair + 1) * pair)
    table = jnp.where(
        open_row, jnp.where(lane == 0, LOW, 0.0), columns_of(slice(0, tokens), tokens)
    )
    for k in range(pairs):
        part = padded(table[k * pair : (k + 1) * pair])
        st1[w, :, k * LANES : (k + 1) * LANES] = jnp.transpose(part)[0:4]

    def acopy(d, dev):
        return rcopy(st1.at[w], st1.at[dev], a_send, a_recv, (v, wpeer(d)))

    def bcopy(d, dev):
        return rcopy(st2.at[v], st2.at[dev], b_send, b_recv, (vpeer(d), w))

    def joined(parts):
        top = functools.reduce(jnp.maximum, [s[0:1, :] for s in parts])
        tot = jnp.zeros_like(top)
        wei = jnp.zeros_like(top)
        pic = jnp.zeros_like(top)
        for s in parts:
            share = jnp.exp(s[0:1, :] - top)
            tot = tot + s[1:2, :] * share
            wei = wei + s[2:3, :] * share
            pic = pic + s[3:4, :]
        return top, tot, wei, pic

    @each(1, WIDTH)
    def _(d):
        acopy(d, w).start()

    for k in range(AHEAD, LAST):
        last_piece(k).start()
    wait_block(V - END)
    block_total(V - END)

    def last_stats(k):
        last_piece(k).wait_recv()
        block_stats(plain + k, V - 1, 1 + k)

    for k in range(AHEAD):
        last_stats(k)

    landed(st1.at[0 : WIDTH - 1], a_recv)

    sub = lax.broadcasted_iota(jnp.int32, (4, pairs * LANES), 0)
    top, tot, wei, pic = joined([st1[q] for q in range(WIDTH)])
    st2[v] = jnp.where(sub == 0, top, jnp.where(sub == 1, tot, jnp.where(sub == 2, wei, pic)))

    @each(1, V)
    def _(d):
        bcopy(d, v).start()

    for k in range(AHEAD, LAST):
        last_stats(k)
    me = v * WIDTH + w
    span = pl.ds(pl.multiple_of(last_pair * pair, 16), pair)
    fin[me] = jnp.transpose(padded(columns_of(span, pair)))[0:4]

    def ccopy(k):
        return rcopy(
            fin.at[me], fin.at[me], c_send, c_recv, (flipped(k // WIDTH), lax.rem(w + k, WIDTH))
        )

    @each(1, V * WIDTH)
    def _(k):
        ccopy(V * WIDTH - k).start()

    xcopy().wait_send()
    drained(sq_all.at[0 : WIDTH - 1], q_send)
    scopy(own_half).wait_send()
    drained(ints_all.at[0 : WIDTH - 1], i_send)
    drained(msq_all.at[0 : V - 1], r_send)
    drained(raw.at[pl.ds(rows, late), own_half], h_send)
    drained(raw.at[pl.ds(rows, late), own_half], f_send)
    drained(wbuf.at[:, own_half, :], w_send)
    drained(sbuf.at[:, pl.ds(rows, late), :], y_send)
    drained(sbuf.at[1:n, 0:rows, :], ya_send)
    drained(zsend.at[pl.ds(1, 2 * n - 1)], z_send)
    drained(sown, own_send)
    drained(zown_send, zo_send)
    landed(st2.at[0 : V - 1], b_recv)
    early = joined([st2[q] for q in range(V)])
    landed(fin.at[0 : V * WIDTH - 1], c_recv)
    parts = [jnp.concatenate(early, axis=0)]
    for q in range(END * WIDTH):
        parts.append(
            jnp.concatenate(
                [fin[(pairs - 1 - k) * END * WIDTH + q] for k in range(pairs)], axis=1
            )
        )
    largest, tot, wei, pic = joined(parts)
    log_total = jnp.log(tot)
    wide = pairs * LANES
    place = lax.broadcasted_iota(jnp.int32, (8, wide), 0)
    used = lax.rem(lax.broadcasted_iota(jnp.int32, (1, wide), 1), LANES) < pair
    spread = jnp.zeros((8, wide), jnp.float32)
    for k, rest in enumerate(
        (pic - largest - log_total, largest + log_total - wei / tot)
    ):
        rest = jnp.where(used, rest, 0.0)
        for part in range(3):
            upper = rest.astype(jnp.bfloat16).astype(jnp.float32)
            spread = jnp.where(place == 2 * part + k, upper, spread)
            rest = rest - upper
    dealt = jnp.dot(
        spread.astype(jnp.bfloat16),
        pick[...],
        preferred_element_type=jnp.float32,
    )
    sums = dealt[0:2] + dealt[2:4] + dealt[4:6]
    out_ref[0:1, :] = sums[0:1]
    out_ref[4:6, :] = sums / fixed[0:1, :]
    out_ref[6:7, :] = fixed[1:2, :]
    highest = jnp.max(jnp.where(asked_rows[...] > 0.5, largest, LOW), axis=1, keepdims=True)
    there = lax.broadcasted_iota(jnp.int32, (reqs, LANES), 1)
    here = lax.broadcasted_iota(jnp.int32, (reqs, LANES), 0)
    out_ref[7:8, :] = jnp.sum(
        jnp.where(there == here + REQ_LANE, highest, 0.0), axis=0, keepdims=True
    )
    drained(st1.at[0 : WIDTH - 1], a_send)
    drained(st2.at[0 : V - 1], b_send)
    drained(fin.at[0 : V * WIDTH - 1], c_send)


def finish(rows, reqs, res_ref, tok_ref, stat_ref):
    tok_ref[...] = res_ref[0:1, 0:rows]
    stat_ref[...] = res_ref[4:8, REQ_LANE : REQ_LANE + reqs]


def body(hidden, norm_gain, head_weight, lengths, deal, targets):
    rows, feats = hidden.shape
    V = lax.axis_size("vocab")
    tokens = rows * V
    slab = head_weight.shape[1]
    quarter = slab // WIDTH
    cn = next(c for c in (512, 256, 128) if quarter % c == 0)
    n = quarter // cn
    mb = next(c for c in (384, 256, 192, 128, 64, 48, 16) if tokens % c == 0)
    reqs = lengths.shape[0]
    bw = tokens // WIDTH

    gain = norm_gain.reshape(-1, LANES)
    bwp = -(-bw // LANES) * LANES
    late = tokens - rows
    mb_late = next(c for c in (336, 192, 144, 96, 48, 16) if late % c == 0)

    cfg = (V, rows, tokens, feats, slab, quarter, cn, n, mb, mb_late, reqs)
    f32, bf16 = jnp.float32, jnp.bfloat16
    dma = pltpu.SemaphoreType.DMA
    vmem = pl.BlockSpec(memory_space=pltpu.VMEM)
    hbm = pl.BlockSpec(memory_space=pltpu.HBM)
    res = pl.pallas_call(
        functools.partial(kernel, cfg),
        out_shape=jax.ShapeDtypeStruct((8, LANES), f32),
        in_specs=[hbm] * 6,
        out_specs=vmem,
        scratch_shapes=[
            pltpu.SMEM((reqs,), jnp.int32),
            pltpu.VMEM((1, bw), jnp.int32),
            pltpu.VMEM((1, bw), jnp.int32),
            pltpu.VMEM((D // LANES, LANES), bf16),
            pltpu.VMEM((rows, feats), bf16),
            pltpu.VMEM((D // LANES, LANES), f32),
            pltpu.VMEM((WIDTH, 2, bwp), jnp.int32),
            pltpu.VMEM((tokens, LANES), jnp.int32),
            pltpu.VMEM((rows, feats), bf16),
            pltpu.VMEM((tokens, 2 * feats), bf16),
            pltpu.VMEM((2 * rows, 2 * feats), bf16),
            pltpu.VMEM((rows, LANES), f32),
            pltpu.VMEM((tokens, LANES), f32),
            pltpu.VMEM((WIDTH, 1, LANES), f32),
            pltpu.VMEM((V, 1, LANES), f32),
            pltpu.VMEM((tokens, 2 * feats), bf16),
            pltpu.VMEM((2 * n, 2 * feats, cn), bf16),
            pltpu.VMEM((n, tokens, cn), jnp.int16),
            pltpu.VMEM((n, tokens, cn), jnp.int16),
            pltpu.VMEM((LAST + 1, tokens, cn), f32),
            pltpu.VMEM((tokens, cn), f32),
            pltpu.VMEM((2 * n, 1, LANES), f32),
            pltpu.VMEM((2 * n, 1, LANES), f32),
            pltpu.VMEM((feats, cn), bf16),
            pltpu.VMEM((2, rows, cn), jnp.int16),
            pltpu.VMEM((2, rows, cn), jnp.int16),
            pltpu.VMEM((2, 1, LANES), f32),
            pltpu.VMEM((2, 1, LANES), f32),
            pltpu.VMEM((2, rows, LANES), f32),
            pltpu.VMEM((tokens, LANES), f32),
            pltpu.VMEM((tokens, LANES), f32),
            pltpu.VMEM((tokens, LANES), f32),
            pltpu.VMEM((tokens, LANES), f32),
            pltpu.VMEM((WIDTH, 4, V // END * LANES), f32),
            pltpu.VMEM((V, 4, V // END * LANES), f32),
            pltpu.VMEM((V * WIDTH, 4, LANES), f32),
            pltpu.VMEM((V // END * LANES, LANES), bf16),
            pltpu.VMEM((reqs, V // END * LANES), f32),
            pltpu.VMEM((8, LANES), f32),
            dma((16,)),
            dma,
            dma,
            dma,
            dma((2,)),
            dma((V,)),
            dma,
            dma,
            dma((4,)),
            dma((n,)),
            dma((n - LAST,)),
            dma((n,)),
            dma((2,)),
            dma,
            dma,
            dma,
            dma,
            dma,
            dma((LAST,)),
        ],
        compiler_params=pltpu.CompilerParams(
            collective_id=0, has_side_effects=True, vmem_limit_bytes=(50 if V <= 8 else 58) << 20
        ),
    )(*[
        pltpu.with_memory_space_constraint(x, pltpu.HBM)
        for x in (targets[None], deal[None], lengths, gain, hidden, head_weight)
    ])
    tok, stat = pl.pallas_call(
        functools.partial(finish, rows, reqs),
        out_shape=(
            jax.ShapeDtypeStruct((1, rows), f32),
            jax.ShapeDtypeStruct((4, reqs), f32),
        ),
        in_specs=[vmem],
        out_specs=(vmem, vmem),
        compiler_params=pltpu.CompilerParams(vmem_limit_bytes=4 << 20),
    )(res)
    return tok[0], stat


def solution(mesh):
    return jax.shard_map(
        body,
        mesh=mesh,
        in_specs=(P("vocab", "width"), P(), P("width", "vocab"), P(), P("width"), P("width")),
        out_specs=(P("vocab"), P()),
        check_vma=False,
    )
```

```python
import functools

import jax
import jax.numpy as jnp
from jax import lax
from jax.experimental import pallas as pl
from jax.experimental.pallas import tpu as pltpu
from jax.sharding import PartitionSpec as P

D = 2048
epsilon = 1e-06
LOW = -1e30
TINY = 1e-30
STEPS = 32767.0
DEPTH = 3
LAST = 4
AHEAD = 1
END = 2
LANES = 128
REQ_LANE = 64
WIDTH = 4


def kernel(
    cfg,
    aim_hbm,
    deal_hbm,
    lens_hbm,
    gain_hbm,
    hid_hbm,
    w_ref,
    out_ref,
    lens_ref,
    aim_ref,
    deal_ref,
    gain_ref,
    hid_ref,
    gains,
    ints_all,
    ints_cols,
    mate_hid,
    raw,
    split_rows,
    chip_scale,
    ratio,
    sq_all,
    msq_all,
    nrm,
    wbuf,
    sbuf,
    rbuf,
    xbuf,
    ybuf,
    zsend,
    zrecv,
    wmate,
    sown,
    rown,
    zown_send,
    zown,
    own_ratio,
    m_acc,
    t_acc,
    g_acc,
    p_acc,
    st1,
    st2,
    fin,
    pick,
    asked_rows,
    fixed,
    once_send,
    x_recv,
    s_recv,
    i_recv,
    q_recv,
    h_recv,
    f_recv,
    r_recv,
    wl_sem,
    w_recv,
    y_recv,
    z_recv,
    own_recv,
    ya_recv,
    za_recv,
    a_recv,
    b_recv,
    c_recv,
    last_recv,
):
    V, rows, tokens, feats, slab, quarter, cn, n, mb, mb_late, reqs = cfg
    v = lax.axis_index("vocab")
    w = lax.axis_index("width")
    lo = lax.rem(w, 2)
    hi = w // 2
    mate = w + 1 - 2 * lo
    far = w + 2 - 4 * hi
    bw = tokens // WIDTH
    x_send, i_send, q_send, h_send, f_send, r_send = [once_send.at[k] for k in range(6)]
    w_send, y_send, z_send, ya_send, a_send, b_send, s_send, own_send, zo_send, c_send = [
        once_send.at[k] for k in range(6, 16)
    ]
    plain = n - LAST
    depth = min(DEPTH, plain)
    pair = END * rows
    pairs = V // END
    last_pair = pairs - 1 - v // END

    def rcopy(src, dst, ss, rs, where):
        return pltpu.make_async_remote_copy(
            src_ref=src,
            dst_ref=dst,
            send_sem=ss,
            recv_sem=rs,
            device_id=where,
            device_id_type=pl.DeviceIdType.MESH,
        )

    def drained(ref, sem):
        rcopy(ref, ref, sem, x_recv, (v, mate)).wait_send()

    def landed(ref, sem):
        rcopy(ref, ref, x_send, sem, (v, mate)).wait_recv()

    bits = [1 << b for b in range(V.bit_length() - 1)]
    ones = [lax.rem(v // bit, 2) * bit for bit in bits]

    def flipped(d):
        other = 0
        for bit, one in zip(bits, ones):
            if isinstance(d, int):
                other = other + (bit - one if d & bit else one)
            else:
                other = other + lax.rem(one // bit + d // bit, 2) * bit
        return other

    def each(first, last):
        def run(step):
            if last - first > 2 * LANES // WIDTH:
                pl.loop(first, last)(step)
            else:
                for k in range(first, last):
                    step(k)

        return run

    def vpeer(d):
        return flipped(d)

    def vsource(d):
        return flipped(d)

    def wpeer(d):
        return lax.rem(w + d, WIDTH)

    def wsource(d):
        return lax.rem(w + WIDTH - d, WIDTH)

    def wcols(k, is_keep, dev):
        dev_far = dev + 2 - 4 * (dev // 2)
        q = dev if is_keep else dev_far
        base = k - n if is_keep else k
        return pl.ds(pl.multiple_of(q * quarter + base * cn, LANES), cn)

    own_half = pl.ds(pl.multiple_of(lo * feats, LANES), feats)
    mate_half = pl.ds(pl.multiple_of((1 - lo) * feats, LANES), feats)

    def wlocal(k, is_keep, sem):
        return pltpu.make_async_copy(
            w_ref.at[:, wcols(k, is_keep, w)], wbuf.at[k, own_half, :], wl_sem.at[sem]
        )

    def wloaded(part, sem):
        pltpu.make_async_copy(part, part, wl_sem.at[sem]).wait()

    def wremote(k, is_keep):
        return rcopy(
            w_ref.at[:, wcols(k, is_keep, mate)],
            wbuf.at[k, own_half, :],
            w_send,
            w_recv.at[lax.rem(k, n)],
            (v, mate),
        )

    def wwait(k, is_keep):
        rcopy(
            w_ref.at[:, wcols(k, is_keep, mate)],
            wbuf.at[k, mate_half, :],
            w_send,
            w_recv.at[lax.rem(k, n)],
            (v, mate),
        ).wait_recv()

    barrier = pltpu.get_barrier_semaphore()

    @each(1, WIDTH)
    def _(d):
        pl.semaphore_signal(
            barrier, inc=1, device_id=(v, wpeer(d)), device_id_type=pl.DeviceIdType.MESH
        )

    @each(1, V)
    def _(d):
        pl.semaphore_signal(
            barrier, inc=1, device_id=(vpeer(d), w), device_id_type=pl.DeviceIdType.MESH
        )

    loads = [
        pltpu.make_async_copy(source, there, once_send.at[k])
        for k, (source, there) in enumerate(
            (
                (hid_hbm, hid_ref),
                (gain_hbm, gain_ref),
                (aim_hbm, aim_ref),
                (deal_hbm, deal_ref),
                (lens_hbm, lens_ref),
            )
        )
    ]
    for load in loads:
        load.start()

    mate_first = pltpu.make_async_copy(w_ref.at[:, wcols(0, False, mate)], wmate, wl_sem.at[3])
    wlocal(0, False, 0).start()
    mate_first.start()

    late = tokens - rows
    groups = feats // LANES

    def slot(d):
        return pl.ds(pl.multiple_of(d * rows, 16), rows)

    def hcopy(d):
        return rcopy(hid_ref, raw.at[slot(d), own_half], h_send, h_recv.at[d], (vpeer(d), w))

    def squares(x):
        return jnp.sum(x * x, axis=1, keepdims=True)

    def to_row(column, wide):
        height = column.shape[0]
        there = lax.broadcasted_iota(jnp.int32, (height, wide), 1)
        here = lax.broadcasted_iota(jnp.int32, (height, wide), 0)
        return jnp.sum(jnp.where(there == here, column, 0.0), axis=0, keepdims=True)

    def to_column(row, height):
        wide = row.shape[1]
        there = lax.broadcasted_iota(jnp.int32, (height, wide), 1)
        here = lax.broadcasted_iota(jnp.int32, (height, wide), 0)
        return jnp.sum(jnp.where(there == here, row, 0.0), axis=1, keepdims=True)

    for load in loads:
        load.wait()
    gains[...] = gain_ref[...].astype(jnp.float32)
    x = hid_ref[...].astype(jnp.float32)
    sq = squares(x)
    sq_all[w] = to_row(sq, LANES)
    for g in range(groups):
        column = pl.ds(pl.multiple_of(lo * feats + g * LANES, LANES), LANES)
        scaled = x[:, g * LANES : (g + 1) * LANES] * gains[pl.ds(w * groups + g, 1), :]
        upper = scaled.astype(jnp.bfloat16)
        split_rows[0:rows, column] = upper
        split_rows[rows : 2 * rows, column] = (scaled - upper.astype(jnp.float32)).astype(
            jnp.bfloat16
        )
    ints_all[w] = jnp.zeros(ints_all.shape[1:], jnp.int32)
    ints_all[w, 0:1, 0:bw] = aim_ref[...]
    ints_all[w, 1:2, 0:bw] = deal_ref[...]
    def lanes_peak(z):
        peak = jnp.max(jnp.abs(z), axis=0, keepdims=True)
        parts = [peak[:, g * LANES : (g + 1) * LANES] for g in range(cn // LANES)]
        return functools.reduce(jnp.maximum, parts)

    def quantized(z, rate):
        for g in range(cn // LANES):
            part = slice(g * LANES, (g + 1) * LANES)
            yield part, jnp.round(z[:, part] * rate).astype(jnp.int32).astype(jnp.int16)

    def folded(both, scale):
        return (both[0:rows] + both[rows : 2 * rows]) * scale

    core_scale = lax.rsqrt(sq * (1.0 / feats) + epsilon)
    wlocal(0, False, 0).wait()
    mate_first.wait()

    @pl.loop(1, n)
    def _(k):
        wlocal(k, False, 1).start()

    for k, weights in enumerate((wbuf[0, own_half, :], wmate[...])):
        z = folded(
            jnp.dot(split_rows[:, own_half], weights, preferred_element_type=jnp.float32),
            core_scale,
        )
        peak = jnp.maximum(TINY, lanes_peak(z))
        zown_send[k] = peak * (1.0 / STEPS)
        for part, value in quantized(z, STEPS / peak):
            sown[k, :, part] = value
    pl.semaphore_wait(barrier, WIDTH - 1 + V - 1)

    def xcopy():
        return rcopy(hid_ref, mate_hid, x_send, x_recv, (v, mate))

    def icopy(d, dev):
        return rcopy(ints_all.at[w], ints_all.at[dev], i_send, i_recv, (v, wpeer(d)))

    across = far + 1 - 2 * lo

    def scopy(half):
        return rcopy(
            split_rows.at[:, half], split_rows.at[:, half], s_send, s_recv, (v, mate)
        )

    def qstart(there, sem):
        rcopy(sq_all.at[w], sq_all.at[w], q_send, q_recv.at[sem], (v, there)).start()

    def owncopy(k, there):
        return rcopy(sown.at[k], rown.at[lo], own_send, own_recv.at[0], (v, there))

    def zocopy(k, there):
        return rcopy(zown_send.at[k], zown.at[lo], zo_send, own_recv.at[1], (v, there))

    for k, there in enumerate((far, across)):
        owncopy(k, there).start()
        zocopy(k, there).start()
    scopy(own_half).start()
    qstart(mate, 0)
    wremote(1, False).start()
    qstart(far, 1)
    qstart(across, 1)

    @pl.loop(2, DEPTH)
    def _(k):
        wremote(k, False).start()

    xcopy().start()

    @each(1, V)
    def _(d):
        hcopy(V - d).start()

    @pl.loop(DEPTH, n)
    def _(k):
        wremote(k, False).start()

    wremote(0, False).start()

    @pl.loop(1, WIDTH)
    def _(d):
        icopy(d, w).start()

    ratio[pl.ds(rows, late), :] = jnp.ones((late, LANES), jnp.float32)
    m_acc[...] = jnp.full((tokens, LANES), LOW, jnp.float32)
    t_acc[...] = jnp.zeros((tokens, LANES), jnp.float32)
    g_acc[...] = jnp.zeros((tokens, LANES), jnp.float32)
    p_acc[...] = jnp.zeros((tokens, LANES), jnp.float32)

    landed(sq_all.at[mate], q_recv.at[0])
    chip_sq = sq + to_column(sq_all[mate], rows)
    chip_scale[...] = jnp.broadcast_to(
        lax.rsqrt(chip_sq * (1.0 / (2 * feats)) + epsilon), (rows, LANES)
    )
    scopy(mate_half).wait_recv()

    def vspan(dev):
        return pl.ds(pl.multiple_of(dev * rows, 16), rows)

    def normalize():
        landed(sq_all.at[0:2], q_recv.at[1])
        xcopy().wait_recv()
        total_sq = sq_all[0] + sq_all[1] + sq_all[2] + sq_all[3]
        mean_row = total_sq * (1.0 / D)
        msq_all[v] = mean_row
        mean_sq = to_column(mean_row, rows)
        scale = lax.rsqrt(mean_sq + epsilon)
        far_sq = to_column(sq_all[far] + sq_all[across], rows)
        far_scale = lax.rsqrt(far_sq * (1.0 / (2 * feats)) + epsilon)
        ratio[0:rows, :] = jnp.broadcast_to(scale / far_scale, (rows, LANES))
        for core, dev in ((lo, far), (1 - lo, across)):
            dev_sq = to_column(sq_all[dev], rows)
            dev_scale = lax.rsqrt(dev_sq * (1.0 / feats) + epsilon)
            own_ratio[core] = jnp.broadcast_to(scale / dev_scale, (rows, LANES))
        for half, dev, source in ((lo, w, hid_ref), (1 - lo, mate, mate_hid)):
            for g in range(groups):
                column = pl.ds(pl.multiple_of(half * feats + g * LANES, LANES), LANES)
                value = source[:, g * LANES : (g + 1) * LANES].astype(jnp.float32)
                nrm[0:rows, column] = (
                    value * scale * gains[pl.ds(dev * groups + g, 1), :]
                ).astype(jnp.bfloat16)

    def fcopy(d, half):
        part = raw.at[slot(d), half]
        return rcopy(part, part, f_send, f_recv, (v, mate))

    def rmscopy(d, dev):
        return rcopy(msq_all.at[v], msq_all.at[dev], r_send, r_recv, (vpeer(d), w))

    def ycopy(i):
        part = pl.ds(rows, late)
        return rcopy(
            sbuf.at[i, part, :], rbuf.at[i, part, :], y_send, y_recv.at[i], (v, far)
        )

    def yacopy(i):
        part = pl.ds(0, rows)
        return rcopy(
            sbuf.at[i, part, :], rbuf.at[i, part, :], ya_send, ya_recv, (v, far)
        )

    def zcopy(k):
        return rcopy(zsend.at[k], zrecv.at[k], z_send, z_recv.at[k - n], (v, far))

    def zacopy(k):
        return rcopy(zsend.at[k], zrecv.at[k], z_send, za_recv, (v, far))

    def yblock(c, d, sem):
        return rcopy(sbuf.at[c, slot(d), :], rbuf.at[c, slot(d), :], y_send, sem, (v, far))

    def start_block(d):
        @pl.loop(plain, n)
        def _(c):
            yblock(c, d, h_recv.at[d]).start()

    def wait_block(d):
        landed(rbuf.at[pl.ds(plain, LAST), slot(d), :], h_recv.at[d])

    def ystart(i):
        zcopy(n + i).start()
        ycopy(i).start()

    def yarrive(i):
        zcopy(n + i).wait_recv()

    def quantize(i, span, rate, z):
        for part, value in quantized(z, rate):
            sbuf[i, span, part] = value

    def first_dot(i):
        wwait(i, False)
        z = folded(
            jnp.dot(split_rows[...], wbuf[i], preferred_element_type=jnp.float32),
            chip_scale[:, 0:1],
        )
        peak = jnp.maximum(TINY, lanes_peak(z))
        zsend[i] = peak * (1.0 / STEPS)
        quantize(i, pl.ds(0, rows), STEPS / peak, z)
        zacopy(i).start()
        yacopy(i).start()

    def add_own():
        for core in range(2):
            scale = own_ratio[core] * zown[core]
            for g in range(cn // LANES):
                part = slice(g * LANES, (g + 1) * LANES)
                xbuf[0, 0:rows, part] += rown[core, :, part].astype(jnp.int32).astype(jnp.float32) * scale

    def send_dot(i):
        def multiply(r, peak):
            span = pl.ds(pl.multiple_of(rows + r * mb_late, 16), mb_late)
            z = jnp.dot(nrm[span, :], wbuf[i], preferred_element_type=jnp.float32)
            ybuf[span, :] = z
            return jnp.maximum(peak, lanes_peak(z))

        peak = lax.fori_loop(
            0, late // mb_late, multiply, jnp.full((1, LANES), TINY, jnp.float32)
        )
        zsend[n + i] = peak * (1.0 / STEPS)
        rate = STEPS / peak

        @pl.loop(1, V)
        def _(r):
            quantize(i, slot(r), rate, ybuf[slot(r), :])

    def keep_dot(i, place):
        wwait(n + i, True)

        @pl.loop(0, tokens // mb)
        def _(r):
            span = pl.ds(pl.multiple_of(r * mb, 16), mb)
            xbuf[place, span, :] = jnp.dot(
                nrm[span, :], wbuf[n + i], preferred_element_type=jnp.float32
            )

        @pl.when(i == 0)
        def _():
            add_own()

    rb = rows
    first_column = v * slab + w * quarter

    def stats(i):
        @pl.loop(0, V)
        def _(r):
            block_stats(i, r, 0)

    def block_stats(i, r, kept):
        held = slot(r)
        span = vspan(vsource(r))
        late_z = n * ((r + V - 1) // V) + i
        target = ints_cols[span, 0:1]
        factor = zrecv[late_z] * ratio[held, :]
        lane = lax.broadcasted_iota(jnp.int32, (rb, LANES), 1)
        aim = jnp.broadcast_to(target, (rb, LANES)) - lane - (first_column + i * cn)
        xs = [
            xbuf[kept, held, g * LANES : (g + 1) * LANES]
            + rbuf[i, held, g * LANES : (g + 1) * LANES].astype(jnp.int32).astype(jnp.float32)
            * factor
            for g in range(cn // LANES)
        ]
        m_old = m_acc[span, :]
        m_new = functools.reduce(jnp.maximum, xs, m_old)
        decay = jnp.exp(m_old - m_new)
        t = t_acc[span, :] * decay
        g_ = g_acc[span, :] * decay
        p = p_acc[span, :]
        for g, z in enumerate(xs):
            e = jnp.exp(z - m_new)
            t = t + e
            g_ = g_ + e * z
            p = p + jnp.where(aim == g * LANES, z, 0.0)
        m_acc[span, :] = m_new
        t_acc[span, :] = t
        g_acc[span, :] = g_
        p_acc[span, :] = p

    def relay(d):
        hcopy(d).wait_recv()
        fcopy(d, own_half).start()

    head = min(3, n)
    wloaded(wbuf.at[1:n, own_half, :], 1)

    @pl.loop(1, head)
    def _(i):
        first_dot(i)

    normalize()

    @each(1, V)
    def _(d):
        rmscopy(d, v).start()

    turns = min(n - head, V - 2)

    @pl.loop(0, turns)
    def _(i):
        first_dot(head + i)
        relay(V - 1 - i)

    @pl.loop(head + turns, n)
    def _(i):
        first_dot(i)

    wwait(0, False)

    @pl.loop(1 + turns, V)
    def _(d):
        relay(V - d)

    landed(msq_all.at[0 : V - 1], r_recv)
    landed(raw.at[pl.ds(rows, late), mate_half], f_recv)

    @pl.loop(1, V)
    def _(d):
        scale = lax.rsqrt(to_column(msq_all[vsource(d)], rows) + epsilon)
        for g in range(2 * groups):
            column = slice(g * LANES, (g + 1) * LANES)
            gain_row = gains[pl.ds((w - lo) * groups + g, 1), :]
            nrm[slot(d), column] = (
                raw[slot(d), column].astype(jnp.float32) * scale * gain_row
            ).astype(jnp.bfloat16)

    @pl.loop(0, depth)
    def _(i):
        send_dot(i)
        ystart(i)

    @pl.loop(0, n)
    def _(k):
        wremote(n + k, True).start()
        wlocal(n + k, True, 2).start()

    def padded(block):
        return jnp.concatenate([block, jnp.zeros((LANES - pair, LANES), jnp.float32)], axis=0)

    landed(ints_all.at[0 : WIDTH - 1], i_recv)

    for q in range(WIDTH):
        columns = [
            jnp.broadcast_to(to_column(ints_all[q, k : k + 1, :].astype(jnp.float32), bw), (bw, LANES))
            for k in range(2)
        ]
        pick_lane = lax.broadcasted_iota(jnp.int32, (bw, LANES), 1)
        ints_cols[q * bw : (q + 1) * bw, :] = jnp.where(
            pick_lane == 0, columns[0], columns[1]
        ).astype(jnp.int32)

    r_row = lax.broadcasted_iota(jnp.int32, (1, LANES), 1)
    ends = jnp.zeros((1, LANES), jnp.int32)
    counts = jnp.ones((1, LANES), jnp.int32)
    for r in range(reqs):
        ends = ends + jnp.where(r_row >= REQ_LANE + r, lens_ref[r], 0)
        counts = jnp.where(r_row == REQ_LANE + r, lens_ref[r], counts)
    asked = (r_row >= REQ_LANE) & (r_row < REQ_LANE + reqs)
    starts = jnp.where(asked, ends - counts, tokens).astype(jnp.float32)
    ends = ends.astype(jnp.float32)
    counts = counts.astype(jnp.float32)
    place = ints_cols[:, 1:2].astype(jnp.float32)
    spot = jnp.where(r_row < rows, v * rows + r_row, tokens).astype(jnp.float32)
    member = (place >= starts) & (place < ends)
    chosen = jnp.where(member | (place == spot), 1.0, 0.0)
    for k in range(pairs):
        part = padded(chosen[k * pair : (k + 1) * pair])
        span = slice(k * LANES, (k + 1) * LANES)
        pick[span, :] = part.astype(jnp.bfloat16)
        asked_rows[:, span] = jnp.transpose(part)[REQ_LANE : REQ_LANE + reqs]
    rms = jnp.concatenate(
        [to_column(jnp.sqrt(msq_all[q] + epsilon), rows) for q in range(V)], axis=0
    )
    fixed[0:1, :] = counts
    fixed[1:2, :] = jnp.sum(jnp.where(member, rms, 0.0), axis=0, keepdims=True) / counts

    wloaded(wbuf.at[n : 2 * n, own_half, :], 2)
    landed(rbuf.at[1:n, 0:rows, :], ya_recv)
    landed(zrecv.at[1:n], za_recv)
    landed(rown, own_recv.at[0])
    landed(zown, own_recv.at[1])
    rbuf[0, 0:rows, :] = jnp.zeros((rows, cn), jnp.int16)
    zrecv[0] = jnp.zeros((1, LANES), jnp.float32)

    def finished(i):
        yarrive(i)
        ycopy(i).wait_recv()

    @pl.loop(0, plain - depth)
    def _(i):
        keep_dot(i, 0)
        send_dot(i + depth)
        finished(i)
        ystart(i + depth)
        stats(i)

    @pl.loop(plain, n)
    def _(c):
        send_dot(c)
        zcopy(n + c).start()

    @pl.loop(1, 1 + DEPTH)
    def _(d):
        start_block(d)

    @pl.loop(plain - depth, plain)
    def _(i):
        keep_dot(i, 0)
        finished(i)
        stats(i)

    def block_total(d):
        @pl.loop(plain, n)
        def _(c):
            block_stats(c, d, 1 + c - plain)

    @pl.loop(plain, n)
    def _(c):
        keep_dot(c, 1 + c - plain)
        yarrive(c)

    block_total(0)

    @pl.loop(1, V - 1 - END)
    def _(d):
        wait_block(d)

        @pl.when(d + DEPTH < V - 1)
        def _():
            start_block(d + DEPTH)

        block_total(d)

    def last_piece(k):
        return yblock(plain + k, V - 1, last_recv.at[k])

    wait_block(V - 1 - END)
    for k in range(AHEAD):
        last_piece(k).start()
    block_total(V - 1 - END)

    def columns_of(span, height):
        m = m_acc[span, :]
        top = jnp.max(m, axis=1, keepdims=True)
        share = jnp.exp(m - top)
        tot = jnp.sum(t_acc[span, :] * share, axis=1, keepdims=True)
        wei = jnp.sum(g_acc[span, :] * share, axis=1, keepdims=True)
        pic = jnp.sum(p_acc[span, :], axis=1, keepdims=True)
        lane = lax.broadcasted_iota(jnp.int32, (height, LANES), 1)
        return jnp.where(
            lane == 0, top, jnp.where(lane == 1, tot, jnp.where(lane == 2, wei, pic))
        )

    lane = lax.broadcasted_iota(jnp.int32, (tokens, LANES), 1)
    line = lax.broadcasted_iota(jnp.int32, (tokens, LANES), 0)
    open_row = (line >= last_pair * pair) & (line < (last_pair + 1) * pair)
    table = jnp.where(
        open_row, jnp.where(lane == 0, LOW, 0.0), columns_of(slice(0, tokens), tokens)
    )
    for k in range(pairs):
        part = padded(table[k * pair : (k + 1) * pair])
        st1[w, :, k * LANES : (k + 1) * LANES] = jnp.transpose(part)[0:4]

    def acopy(d, dev):
        return rcopy(st1.at[w], st1.at[dev], a_send, a_recv, (v, wpeer(d)))

    def bcopy(d, dev):
        return rcopy(st2.at[v], st2.at[dev], b_send, b_recv, (vpeer(d), w))

    def joined(parts):
        top = functools.reduce(jnp.maximum, [s[0:1, :] for s in parts])
        tot = jnp.zeros_like(top)
        wei = jnp.zeros_like(top)
        pic = jnp.zeros_like(top)
        for s in parts:
            share = jnp.exp(s[0:1, :] - top)
            tot = tot + s[1:2, :] * share
            wei = wei + s[2:3, :] * share
            pic = pic + s[3:4, :]
        return top, tot, wei, pic

    @each(1, WIDTH)
    def _(d):
        acopy(d, w).start()

    for k in range(AHEAD, LAST):
        last_piece(k).start()
    wait_block(V - END)
    block_total(V - END)

    def last_stats(k):
        last_piece(k).wait_recv()
        block_stats(plain + k, V - 1, 1 + k)

    for k in range(AHEAD):
        last_stats(k)

    landed(st1.at[0 : WIDTH - 1], a_recv)

    sub = lax.broadcasted_iota(jnp.int32, (4, pairs * LANES), 0)
    top, tot, wei, pic = joined([st1[q] for q in range(WIDTH)])
    st2[v] = jnp.where(sub == 0, top, jnp.where(sub == 1, tot, jnp.where(sub == 2, wei, pic)))

    @each(1, V)
    def _(d):
        bcopy(d, v).start()

    for k in range(AHEAD, LAST):
        last_stats(k)
    me = v * WIDTH + w
    span = pl.ds(pl.multiple_of(last_pair * pair, 16), pair)
    fin[me] = jnp.transpose(padded(columns_of(span, pair)))[0:4]

    def ccopy(k):
        return rcopy(
            fin.at[me], fin.at[me], c_send, c_recv, (flipped(k // WIDTH), lax.rem(w + k, WIDTH))
        )

    @each(1, V * WIDTH)
    def _(k):
        ccopy(V * WIDTH - k).start()

    xcopy().wait_send()
    drained(sq_all.at[0 : WIDTH - 1], q_send)
    scopy(own_half).wait_send()
    drained(ints_all.at[0 : WIDTH - 1], i_send)
    drained(msq_all.at[0 : V - 1], r_send)
    drained(raw.at[pl.ds(rows, late), own_half], h_send)
    drained(raw.at[pl.ds(rows, late), own_half], f_send)
    drained(wbuf.at[:, own_half, :], w_send)
    drained(sbuf.at[:, pl.ds(rows, late), :], y_send)
    drained(sbuf.at[1:n, 0:rows, :], ya_send)
    drained(zsend.at[pl.ds(1, 2 * n - 1)], z_send)
    drained(sown, own_send)
    drained(zown_send, zo_send)
    landed(st2.at[0 : V - 1], b_recv)
    early = joined([st2[q] for q in range(V)])
    landed(fin.at[0 : V * WIDTH - 1], c_recv)
    parts = [jnp.concatenate(early, axis=0)]
    for q in range(END * WIDTH):
        parts.append(
            jnp.concatenate(
                [fin[(pairs - 1 - k) * END * WIDTH + q] for k in range(pairs)], axis=1
            )
        )
    largest, tot, wei, pic = joined(parts)
    log_total = jnp.log(tot)
    wide = pairs * LANES
    place = lax.broadcasted_iota(jnp.int32, (8, wide), 0)
    used = lax.rem(lax.broadcasted_iota(jnp.int32, (1, wide), 1), LANES) < pair
    spread = jnp.zeros((8, wide), jnp.float32)
    for k, rest in enumerate(
        (pic - largest - log_total, largest + log_total - wei / tot)
    ):
        rest = jnp.where(used, rest, 0.0)
        for part in range(3):
            upper = rest.astype(jnp.bfloat16).astype(jnp.float32)
            spread = jnp.where(place == 2 * part + k, upper, spread)
            rest = rest - upper
    dealt = jnp.dot(
        spread.astype(jnp.bfloat16),
        pick[...],
        preferred_element_type=jnp.float32,
    )
    sums = dealt[0:2] + dealt[2:4] + dealt[4:6]
    out_ref[0:1, :] = sums[0:1]
    out_ref[4:6, :] = sums / fixed[0:1, :]
    out_ref[6:7, :] = fixed[1:2, :]
    highest = jnp.max(jnp.where(asked_rows[...] > 0.5, largest, LOW), axis=1, keepdims=True)
    there = lax.broadcasted_iota(jnp.int32, (reqs, LANES), 1)
    here = lax.broadcasted_iota(jnp.int32, (reqs, LANES), 0)
    out_ref[7:8, :] = jnp.sum(
        jnp.where(there == here + REQ_LANE, highest, 0.0), axis=0, keepdims=True
    )
    drained(st1.at[0 : WIDTH - 1], a_send)
    drained(st2.at[0 : V - 1], b_send)
    drained(fin.at[0 : V * WIDTH - 1], c_send)


def finish(rows, reqs, res_ref, tok_ref, stat_ref):
    tok_ref[...] = res_ref[0:1, 0:rows]
    stat_ref[...] = res_ref[4:8, REQ_LANE : REQ_LANE + reqs]


def body(hidden, norm_gain, head_weight, lengths, deal, targets):
    rows, feats = hidden.shape
    V = lax.axis_size("vocab")
    tokens = rows * V
    slab = head_weight.shape[1]
    quarter = slab // WIDTH
    cn = next(c for c in (512, 256, 128) if quarter % c == 0)
    n = quarter // cn
    mb = next(c for c in (384, 256, 192, 128, 64, 48, 16) if tokens % c == 0)
    reqs = lengths.shape[0]
    bw = tokens // WIDTH

    gain = norm_gain.reshape(-1, LANES)
    bwp = -(-bw // LANES) * LANES
    late = tokens - rows
    mb_late = next(c for c in (336, 192, 144, 96, 48, 16) if late % c == 0)

    cfg = (V, rows, tokens, feats, slab, quarter, cn, n, mb, mb_late, reqs)
    f32, bf16 = jnp.float32, jnp.bfloat16
    dma = pltpu.SemaphoreType.DMA
    vmem = pl.BlockSpec(memory_space=pltpu.VMEM)
    hbm = pl.BlockSpec(memory_space=pltpu.HBM)
    res = pl.pallas_call(
        functools.partial(kernel, cfg),
        out_shape=jax.ShapeDtypeStruct((8, LANES), f32),
        in_specs=[hbm] * 6,
        out_specs=vmem,
        scratch_shapes=[
            pltpu.SMEM((reqs,), jnp.int32),
            pltpu.VMEM((1, bw), jnp.int32),
            pltpu.VMEM((1, bw), jnp.int32),
            pltpu.VMEM((D // LANES, LANES), bf16),
            pltpu.VMEM((rows, feats), bf16),
            pltpu.VMEM((D // LANES, LANES), f32),
            pltpu.VMEM((WIDTH, 2, bwp), jnp.int32),
            pltpu.VMEM((tokens, LANES), jnp.int32),
            pltpu.VMEM((rows, feats), bf16),
            pltpu.VMEM((tokens, 2 * feats), bf16),
            pltpu.VMEM((2 * rows, 2 * feats), bf16),
            pltpu.VMEM((rows, LANES), f32),
            pltpu.VMEM((tokens, LANES), f32),
            pltpu.VMEM((WIDTH, 1, LANES), f32),
            pltpu.VMEM((V, 1, LANES), f32),
            pltpu.VMEM((tokens, 2 * feats), bf16),
            pltpu.VMEM((2 * n, 2 * feats, cn), bf16),
            pltpu.VMEM((n, tokens, cn), jnp.int16),
            pltpu.VMEM((n, tokens, cn), jnp.int16),
            pltpu.VMEM((LAST + 1, tokens, cn), f32),
            pltpu.VMEM((tokens, cn), f32),
            pltpu.VMEM((2 * n, 1, LANES), f32),
            pltpu.VMEM((2 * n, 1, LANES), f32),
            pltpu.VMEM((feats, cn), bf16),
            pltpu.VMEM((2, rows, cn), jnp.int16),
            pltpu.VMEM((2, rows, cn), jnp.int16),
            pltpu.VMEM((2, 1, LANES), f32),
            pltpu.VMEM((2, 1, LANES), f32),
            pltpu.VMEM((2, rows, LANES), f32),
            pltpu.VMEM((tokens, LANES), f32),
            pltpu.VMEM((tokens, LANES), f32),
            pltpu.VMEM((tokens, LANES), f32),
            pltpu.VMEM((tokens, LANES), f32),
            pltpu.VMEM((WIDTH, 4, V // END * LANES), f32),
            pltpu.VMEM((V, 4, V // END * LANES), f32),
            pltpu.VMEM((V * WIDTH, 4, LANES), f32),
            pltpu.VMEM((V // END * LANES, LANES), bf16),
            pltpu.VMEM((reqs, V // END * LANES), f32),
            pltpu.VMEM((8, LANES), f32),
            dma((16,)),
            dma,
            dma,
            dma,
            dma((2,)),
            dma((V,)),
            dma,
            dma,
            dma((4,)),
            dma((n,)),
            dma((n - LAST,)),
            dma((n,)),
            dma((2,)),
            dma,
            dma,
            dma,
            dma,
            dma,
            dma((LAST,)),
        ],
        compiler_params=pltpu.CompilerParams(
            collective_id=0, has_side_effects=True, vmem_limit_bytes=(50 if V <= 8 else 58) << 20
        ),
    )(*[
        pltpu.with_memory_space_constraint(x, pltpu.HBM)
        for x in (targets[None], deal[None], lengths, gain, hidden, head_weight)
    ])
    tok, stat = pl.pallas_call(
        functools.partial(finish, rows, reqs),
        out_shape=(
            jax.ShapeDtypeStruct((1, rows), f32),
            jax.ShapeDtypeStruct((4, reqs), f32),
        ),
        in_specs=[vmem],
        out_specs=(vmem, vmem),
        compiler_params=pltpu.CompilerParams(vmem_limit_bytes=4 << 20),
    )(res)
    return tok[0], stat


def solution(mesh):
    return jax.shard_map(
        body,
        mesh=mesh,
        in_specs=(P("vocab", "width"), P(), P("width", "vocab"), P(), P("width"), P("width")),
        out_specs=(P("vocab"), P()),
        check_vma=False,
    )
```
